32 devices in a mesh: grp: 4 (over y, core), blk: 8 (over z, x).
Axes of the slice: x: 2, y: 2, z: 4, core: 2. Of those that a mesh axis runs over, the one named last changes fastest.
Arguments:
- state: float32 [4, 3, 512, 1024], P('grp', None, None, 'blk'), may hold values from -1 to 1
- material: float32 [4, 3, 512, 1024], P('grp', None, None, 'blk'), may hold values from 0.5 to 2
- occupied: int32 [4096], P(('grp', 'blk')), may hold values from 0 to 1, as said below
- brick_column: int32 [4096, 1], P(('grp', 'blk')), may hold values from 0 to 7, as said below
- brick_octant: int32 [4096], P(('grp', 'blk')), may hold values from 0 to 383
Outputs:
- new_state: float32 [4, 3, 512, 1024], P('grp', None, None, 'blk')
The draws below stay inside these ranges and needn't reach their ends.
Inputs may be any that keep to these rules, and one draw needn't show every extreme that they name: `brick_column`: the rows of one device name at most 32 elements of one column, and exactly 32 of some column; rows of grp index 3 are not read. `brick_octant`: rows of grp index 3 are not read. The slots e < 32 of every device are occupied.
All inputs are finite; a program needn't handle non-finite values.
Results may differ from the reference program's by a relative error of at most 0.00074.
Values may be sent and summed in bfloat16 or wider, within the bound.
No kernel may reach another device: no remote copies, remote signals or barrier semaphores. Data moves between devices by JAX's collectives and lax.ppermute only.
A program may use at most 128 MiB of HBM per device.

```python
import math
import jax
import jax.numpy as jnp
from jax import lax

E_DEV = 128
STEPS = 2
CAP = 32
N_GRP = 4
N_BLK = 8


def draw_brick_column(key, part):
    slot_total = N_BLK * CAP
    device_total = N_GRP * N_BLK

    def one_device(device_at):
        device_key = jax.random.fold_in(key, device_at + 11)
        noise_key, bias_key, pick_key = jax.random.split(device_key, 3)
        noise = jax.random.randint(noise_key, (slot_total,), 0, 2 ** 15)
        column_bias = jax.random.randint(bias_key, (N_BLK,), 0, 4)
        chosen = jax.random.randint(pick_key, (), 0, N_BLK)
        chosen = jnp.where(device_at == 2 * N_BLK + N_BLK - 1, 0, jnp.where(device_at == 0, N_BLK - 1, chosen))
        column_bias = jnp.where(jnp.arange(N_BLK) == chosen, 4, column_bias)
        slot_column = jnp.arange(slot_total) // CAP
        scores = (noise + column_bias[slot_column] * 2 ** 15) * slot_total + jnp.arange(slot_total)
        best_scores, picked = lax.top_k(scores, E_DEV)
        return (picked // CAP).astype(jnp.int32)
    columns = jax.vmap(one_device)(jnp.arange(device_total))
    return columns.reshape(device_total * E_DEV, 1).astype(jnp.int32)


def draw_occupied(key, part):
    total = N_GRP * N_BLK * E_DEV
    rolled = jax.random.randint(jax.random.fold_in(key, 5), (total,), 0, 4)
    position = jnp.arange(total) % E_DEV
    return jnp.where(position < CAP, 1, jnp.where(rolled < 3, 1, 0)).astype(jnp.int32)


def place_ends(result, rng, low, top_value):
    longest = result.shape.index(max(result.shape))
    spots = []
    for shift in (0, 1):
        where = [jax.random.randint(jax.random.fold_in(rng, axis), (), 0, length) for axis, length in enumerate(result.shape)]
        where[longest] = (where[longest] + shift) % result.shape[longest]
        spots.append(tuple(where))
    return result.at[spots[0]].set(low).at[spots[1]].set(top_value)


def level_of(rng, shape, cuts, smallest, top_value):
    loudness, own = 1.0, jax.random.fold_in(rng, 6)
    for dim, shards_of in cuts:
        draws = jnp.exp(jax.random.uniform(jax.random.fold_in(own, dim), (shards_of,), jnp.float32, smallest / len(cuts), top_value / len(cuts)))
        loudness = loudness * jnp.repeat(draws, shape[dim] // shards_of).reshape([-1 if axis == dim else 1 for axis in range(len(shape))])
    return loudness


def setup_inputs(seed: int = 0) -> dict:
    seeds = jax.random.split(jax.random.key(seed), 6)
    state = jnp.clip(jax.random.uniform(seeds[0], (N_GRP, 3, 512, N_BLK * E_DEV), jnp.float32, -1.0, 1.0) * level_of(seeds[0], (N_GRP, 3, 512, N_BLK * E_DEV), ((0, 4), (3, 8)), -0.4, 0.0), -1.0, 1.0)
    material = jnp.clip(jnp.exp(math.log(2.0) - 1.3862944 * jax.random.uniform(seeds[1], (N_GRP, 3, 512, N_BLK * E_DEV), jnp.float32) ** level_of(seeds[1], (N_GRP, 3, 512, N_BLK * E_DEV), ((0, 4), (3, 8)), -0.2, 0.2)), 0.5, 2.0)
    occupied = draw_occupied(jax.random.fold_in(seeds[5], 71), 0)
    brick_column = draw_brick_column(jax.random.fold_in(seeds[5], 71), 0)
    brick_octant = place_ends(jax.random.randint(seeds[4], (N_GRP * N_BLK * E_DEV,), 0, 3 * E_DEV), jax.random.fold_in(seeds[4], 1), 0, (3 * E_DEV) - 1).astype(jnp.int32)
    return dict(state=state, material=material, occupied=occupied, brick_column=brick_column, brick_octant=brick_octant)


UNIT_LENGTH = 0.02
TIME_STEP = 0.1
PENALTY = 1.0
PRESSURE_SCALE = 0.05
DILATION_SCALE = 50.0
SWEEP_STEP = 0.03
SOURCE_RATE = 2.0
CUBIC_TERM = 0.3


def node_diff(values, axis):
    length = values.shape[axis]
    lower_part = lax.slice_in_dim(values, 1, 2, axis=axis) - lax.slice_in_dim(values, 0, 1, axis=axis)
    middle = 0.5 * (lax.slice_in_dim(values, 2, length, axis=axis) - lax.slice_in_dim(values, 0, length - 2, axis=axis))
    upper_part = lax.slice_in_dim(values, length - 1, length, axis=axis) - lax.slice_in_dim(values, length - 2, length - 1, axis=axis)
    return jnp.concatenate([lower_part, middle, upper_part], axis=axis)


def deformation(current):
    displaced = UNIT_LENGTH * current
    return [[node_diff(displaced[i], j) + (1.0 if i == j else 0.0) for j in range(3)] for i in range(3)]


def determinant(grads):
    return (grads[0][0] * (grads[1][1] * grads[2][2] - grads[1][2] * grads[2][1])
            - grads[0][1] * (grads[1][0] * grads[2][2] - grads[1][2] * grads[2][0])
            + grads[0][2] * (grads[1][0] * grads[2][1] - grads[1][1] * grads[2][0]))


def cofactors(grads):
    return [[grads[1][1] * grads[2][2] - grads[1][2] * grads[2][1], grads[1][2] * grads[2][0] - grads[1][0] * grads[2][2], grads[1][0] * grads[2][1] - grads[1][1] * grads[2][0]],
            [grads[0][2] * grads[2][1] - grads[0][1] * grads[2][2], grads[0][0] * grads[2][2] - grads[0][2] * grads[2][0], grads[0][1] * grads[2][0] - grads[0][0] * grads[2][1]],
            [grads[0][1] * grads[1][2] - grads[0][2] * grads[1][1], grads[0][2] * grads[1][0] - grads[0][0] * grads[1][2], grads[0][0] * grads[1][1] - grads[0][1] * grads[1][0]]]


def dilation_rows(current, filled):
    grads = deformation(current)
    change = (determinant(grads) - 1.0) * filled * DILATION_SCALE
    return change.reshape(512, -1).astype(jnp.bfloat16)


def mech_update(current, material, pressure, filled, neighbours, first_mask, last_mask):
    grads = deformation(current)
    strain = [[0.5 * (sum(grads[k][i] * grads[k][j] for k in range(3)) - (1.0 if i == j else 0.0)) for j in range(3)] for i in range(3)]
    strain_trace = strain[0][0] + strain[1][1] + strain[2][2]
    shear, lame_first, mobility = material[0], material[1], material[2]
    stress_second = [[2.0 * shear * strain[i][j] + (lame_first * strain_trace if i == j else 0.0) for j in range(3)] for i in range(3)]
    cofactor_f = cofactors(grads)
    first_pk = [[sum(grads[i][k] * stress_second[k][j] for k in range(3)) - pressure * cofactor_f[i][j] for j in range(3)] for i in range(3)]
    forces = jnp.stack([sum(node_diff(first_pk[i][j], j) for j in range(3)) for i in range(3)])
    x_below, x_below_fill, x_above, x_above_fill = neighbours
    penalty = PENALTY * UNIT_LENGTH
    forces = forces.at[:, 0].add(penalty * x_below_fill * (x_below - current[:, 0]))
    forces = forces.at[:, 7].add(penalty * x_above_fill * (x_above - current[:, 7]))
    zero_face = jnp.zeros_like(current[:, :, :, 0, :1])
    zero_fill = jnp.zeros_like(filled[:1])
    z_below = jnp.concatenate([zero_face, current[:, :, :, 7, :-1]], axis=-1)
    z_below_fill = jnp.concatenate([zero_fill, filled[:-1]]) * (1.0 - first_mask)
    z_above = jnp.concatenate([current[:, :, :, 0, 1:], zero_face], axis=-1)
    z_above_fill = jnp.concatenate([filled[1:], zero_fill]) * (1.0 - last_mask)
    forces = forces.at[:, :, :, 0].add(penalty * z_below_fill * (z_below - current[:, :, :, 0]))
    forces = forces.at[:, :, :, 7].add(penalty * z_above_fill * (z_above - current[:, :, :, 7]))
    return current + (TIME_STEP / UNIT_LENGTH) * mobility * filled * forces


def pressure_cells(fraction):
    return (fraction + CUBIC_TERM * fraction * fraction * fraction).astype(jnp.bfloat16)


def diffuse(padded, coeff_field):
    centre = padded[1:-1]
    beside = jnp.pad(centre, ((0, 0), (1, 1), (1, 1)), mode="edge")
    weight_all = 0.5 + padded * padded
    weight_centre = weight_all[1:-1]
    inflow = 0.5 * (weight_centre + weight_all[2:]) * (padded[2:] - centre)
    inflow = inflow + 0.5 * (weight_centre + weight_all[:-2]) * (padded[:-2] - centre)
    for neighbour in (beside[:, 2:, 1:-1], beside[:, :-2, 1:-1], beside[:, 1:-1, 2:], beside[:, 1:-1, :-2]):
        inflow = inflow + 0.5 * (weight_centre + 0.5 + neighbour * neighbour) * (neighbour - centre)
    return centre + SWEEP_STEP * coeff_field * inflow


def to_octants(brick_field):
    depth = brick_field.shape[2]
    blocks = brick_field.reshape(2, 8, 2, 8, depth // 8, 8)
    return blocks.transpose(1, 3, 5, 0, 2, 4).reshape(512, 4 * (depth // 8))


def from_octants(octant_table, depth):
    blocks = octant_table.reshape(8, 8, 8, 2, 2, depth // 8)
    return blocks.transpose(3, 0, 4, 1, 5, 2).reshape(16, 16, depth)


def reference(state, material, occupied, brick_column, brick_octant):
    slab_width = N_BLK * E_DEV
    depth = 6 * E_DEV
    octant_count = 3 * E_DEV
    filled = occupied.reshape(4, slab_width).astype(jnp.float32)
    column = brick_column[:, 0].reshape(4, slab_width)[:3].reshape(-1)
    octant = brick_octant.reshape(4, slab_width)[:3].reshape(-1)
    target = (column * octant_count + octant).astype(jnp.int32)
    mechanics = [state[g].reshape(3, 8, 8, 8, slab_width) for g in range(3)]
    materials = [material[g].reshape(3, 8, 8, 8, slab_width) for g in range(3)]

    def to_bricks(slab):
        return slab.reshape(3, 512, N_BLK, E_DEV).transpose(2, 0, 1, 3).reshape(N_BLK * 16, 16, depth)

    fraction = to_bricks(state[3])
    diffusivity = to_bricks(material[3])
    element_at = jnp.arange(slab_width)
    first_mask = (element_at % E_DEV == 0).astype(jnp.float32)
    last_mask = (element_at % E_DEV == E_DEV - 1).astype(jnp.float32)
    zero_face = jnp.zeros((3, 8, 8, E_DEV), jnp.float32)
    zero_fill = jnp.zeros((E_DEV,), jnp.float32)
    for step_at in range(STEPS):
        per_column = pressure_cells(fraction).reshape(N_BLK, 16, 16, depth)
        octant_table = jax.vmap(to_octants)(per_column).transpose(1, 0, 2).reshape(512, N_BLK * octant_count)
        pressure = octant_table[:, target].astype(jnp.float32) * PRESSURE_SCALE
        dilations = jnp.concatenate([dilation_rows(mechanics[g], filled[g]) for g in range(3)], axis=1)
        deposit_sum = jnp.zeros((512, N_BLK * octant_count), jnp.float32).at[:, target].add(dilations.astype(jnp.float32))
        deposit_cells = jax.vmap(lambda table: from_octants(table, depth))(
            deposit_sum.reshape(512, N_BLK, octant_count).transpose(1, 0, 2)).reshape(N_BLK * 16, 16, depth)
        fraction = fraction + SWEEP_STEP * SOURCE_RATE * deposit_cells
        for sweep_at in range(2):
            fraction = diffuse(jnp.pad(fraction, ((1, 1), (0, 0), (0, 0))), diffusivity)
        updated = []
        for g in range(3):
            current = mechanics[g]
            x_below = jnp.concatenate([zero_face, current[:, 7, :, :, :-E_DEV]], axis=-1)
            x_below_fill = jnp.concatenate([zero_fill, filled[g][:-E_DEV]])
            x_above = jnp.concatenate([current[:, 0, :, :, E_DEV:], zero_face], axis=-1)
            x_above_fill = jnp.concatenate([filled[g][E_DEV:], zero_fill])
            neighbours = (x_below, x_below_fill, x_above, x_above_fill)
            own_pressure = pressure[:, g * slab_width:(g + 1) * slab_width].reshape(8, 8, 8, slab_width)
            updated.append(mech_update(current, materials[g], own_pressure, filled[g], neighbours, first_mask, last_mask))
        mechanics = updated
    solvent_slab = fraction.reshape(N_BLK, 3, 512, E_DEV).transpose(1, 2, 0, 3).reshape(3, 512, slab_width)
    return jnp.stack([mech.reshape(3, 512, slab_width) for mech in mechanics] + [solvent_slab])
```

```python
import jax
import jax.numpy as jnp
from jax import lax
from jax.experimental import pallas as pl
from jax.experimental.pallas import tpu as pltpu
from jax.sharding import PartitionSpec as P

UNIT_LENGTH = 0.02
TIME_STEP = 0.1
PENALTY = 1.0
PRESSURE_SCALE = 0.05
DILATION_SCALE = 50.0
SWEEP_STEP = 0.03
SOURCE_RATE = 2.0
CUBIC_TERM = 0.3

LANES = 128
F32, BF16 = jnp.float32, jnp.bfloat16
VMEM = pl.BlockSpec(memory_space=pltpu.VMEM)
SMEM = pl.BlockSpec(memory_space=pltpu.SMEM)


def shape_of(shape, dtype=F32):
    return jax.ShapeDtypeStruct(shape, dtype)


def call(body, args, outs, scratch=(), smem=0, name=None):
    return pl.pallas_call(
        body,
        out_shape=outs,
        in_specs=[SMEM] * smem + [VMEM] * (len(args) - smem),
        out_specs=jax.tree.map(lambda _: VMEM, outs),
        scratch_shapes=list(scratch),
        name=name,
    )(*args)


def iota(shape, dim):
    return lax.broadcasted_iota(jnp.int32, shape, dim)


def dot(a, b, dims):
    return lax.dot_general(a, b, (dims, ((), ())), preferred_element_type=F32)


def diff_i(below, here, above, i):
    if below is None:
        return above - here
    if above is None:
        return here - below
    return 0.5 * (above - below)


def diff_j(x):
    return jnp.concatenate([x[1:2] - x[0:1], 0.5 * (x[2:] - x[:-2]), x[7:8] - x[6:7]], axis=0)


def diff_k(x):
    k = iota(x.shape, 1)
    upper = jnp.where(k == 7, x, pltpu.roll(x, 7, 1))
    lower = jnp.where(k == 0, x, pltpu.roll(x, 1, 1))
    return jnp.where((k == 0) | (k == 7), 1.0, 0.5) * (upper - lower)


def slab(ref, c, i):
    rows = ref[pl.ds(c * 512 + 64 * i, 64), :]
    return rows.reshape(8, 8, rows.shape[-1])


def put_slab(ref, c, i, value):
    ref[pl.ds(c * 512 + 64 * i, 64), :] = value.reshape(64, value.shape[-1])


def gradients(ref, i):
    grads = []
    for c in range(3):
        here = UNIT_LENGTH * slab(ref, c, i)
        below = UNIT_LENGTH * slab(ref, c, i - 1) if i > 0 else None
        above = UNIT_LENGTH * slab(ref, c, i + 1) if i < 7 else None
        row = [diff_i(below, here, above, i), diff_j(here), diff_k(here)]
        row[c] = row[c] + 1.0
        grads.append(row)
    return grads


def determinant(grads):
    return (
        grads[0][0] * (grads[1][1] * grads[2][2] - grads[1][2] * grads[2][1])
        - grads[0][1] * (grads[1][0] * grads[2][2] - grads[1][2] * grads[2][0])
        + grads[0][2] * (grads[1][0] * grads[2][1] - grads[1][1] * grads[2][0])
    )


def cofactors(g):
    return [
        [
            g[1][1] * g[2][2] - g[1][2] * g[2][1],
            g[1][2] * g[2][0] - g[1][0] * g[2][2],
            g[1][0] * g[2][1] - g[1][1] * g[2][0],
        ],
        [
            g[0][2] * g[2][1] - g[0][1] * g[2][2],
            g[0][0] * g[2][2] - g[0][2] * g[2][0],
            g[0][1] * g[2][0] - g[0][0] * g[2][1],
        ],
        [
            g[0][1] * g[1][2] - g[0][2] * g[1][1],
            g[0][2] * g[1][0] - g[0][0] * g[1][2],
            g[0][0] * g[1][1] - g[0][1] * g[1][0],
        ],
    ]


def dilate(ref, filled, out):
    for i in range(8):
        change = (determinant(gradients(ref, i)) - 1.0) * filled * DILATION_SCALE
        out[pl.ds(64 * i, 64), :] = change.reshape(64, change.shape[-1]).astype(BF16)


def put_faces(ref, up, down):
    for c in range(3):
        up[pl.ds(64 * c, 64), :] = ref[pl.ds(c * 512 + 448, 64), :]
        down[pl.ds(64 * c, 64), :] = ref[pl.ds(c * 512, 64), :]


def advance(ref, mat, filled, recv, sel, low, high, fills, out, pressure, stress, partial):
    e = filled.shape[-1]
    pressure[...] = dot(recv[...], sel[...], ((0,), (0,))) * PRESSURE_SCALE
    for i in range(8):
        g = gradients(ref, i)
        shear, lame = slab(mat, 0, i), slab(mat, 1, i)
        c = {}
        for a in range(3):
            for b in range(a, 3):
                c[a, b] = g[0][a] * g[0][b] + g[1][a] * g[1][b] + g[2][a] * g[2][b]
        diag = [c[a, a] - 1.0 for a in range(3)]
        volume = lame * (0.5 * (diag[0] + diag[1] + diag[2]))
        s = {}
        for a in range(3):
            s[a, a] = shear * diag[a] + volume
            for b in range(a + 1, 3):
                s[a, b] = s[b, a] = shear * c[a, b]
        cof = cofactors(g)
        p = pressure[pl.ds(64 * i, 64), :].reshape(8, 8, e)
        for a in range(3):
            first = [
                g[a][0] * s[0, b] + g[a][1] * s[1, b] + g[a][2] * s[2, b] - p * cof[a][b]
                for b in range(3)
            ]
            put_slab(stress, a, i, first[0])
            put_slab(partial, a, i, diff_j(first[1]) + diff_k(first[2]))
    penalty = PENALTY * UNIT_LENGTH
    k = iota((8, 8, e), 1)
    fill_low, fill_high = fills[0].reshape(1, 1, e), fills[1].reshape(1, 1, e)
    lane = iota((1, 1, e), 2)
    fill_before = jnp.where(lane == 0, 0.0, pltpu.roll(filled, 1, 2)) * penalty
    fill_after = jnp.where(lane == e - 1, 0.0, pltpu.roll(filled, e - 1, 2)) * penalty
    before_scale = jnp.where(k == 0, fill_before, 0.0)
    after_scale = jnp.where(k == 7, fill_after, 0.0)
    for i in range(8):
        rate = (TIME_STEP / UNIT_LENGTH) * slab(mat, 2, i) * filled
        for a in range(3):
            here = slab(ref, a, i)
            force = slab(partial, a, i) + diff_i(
                slab(stress, a, i - 1) if i > 0 else None,
                slab(stress, a, i),
                slab(stress, a, i + 1) if i < 7 else None,
                i,
            )
            if i == 0:
                other = low[pl.ds(64 * a, 64), :].reshape(8, 8, e)
                force = force + penalty * fill_low * (other - here)
            if i == 7:
                other = high[pl.ds(64 * a, 64), :].reshape(8, 8, e)
                force = force + penalty * fill_high * (other - here)
            before = pltpu.roll(pltpu.roll(here, 1, 1), 1, 2)
            after = pltpu.roll(pltpu.roll(here, 7, 1), e - 1, 2)
            force = force + before_scale * (before - here) + after_scale * (after - here)
            put_slab(out, a, i, here + rate * force)


def permute_in(x, tables):
    x = jnp.take_along_axis(x, tables[0], axis=1, mode="promise_in_bounds")
    x = jnp.take_along_axis(x, tables[1], axis=0, mode="promise_in_bounds")
    return jnp.take_along_axis(x, tables[2], axis=1, mode="promise_in_bounds")


def tables_in():
    row, lane = iota((8, LANES), 0), iota((8, LANES), 1)
    high, low = lane // 16, lane % 16
    return (8 * low + (high - row + 8) % 8, (high - row + 8) % 8, 16 * ((high + row) % 8) + low)


def tables_out():
    row, lane = iota((8, LANES), 0), iota((8, LANES), 1)
    high, low = lane // 16, lane % 16
    return (
        16 * ((high - row + 8) % 8) + low,
        (high - row + 8) % 8,
        16 * ((lane % 8 + row) % 8) + lane // 8,
    )


def to_octants(ref, out, scale, tables, tiles):
    rows = 16 * tiles
    lane = iota((8, LANES), 1)

    def layer(x, carry):
        chunk = ref[pl.ds(pl.multiple_of(x * rows, 8), rows), :]
        for y in range(16):
            part = chunk[tiles * y : min(tiles * y + 8, rows)]
            if part.shape[0] < 8:
                pad = jnp.zeros((8 - part.shape[0], LANES), F32)
                part = jnp.concatenate([part, pad], axis=0)
            part = permute_in(part, tables)
            part = jnp.where(lane < 16 * tiles, part, 0.0)
            if scale != 1.0:
                part = part * scale
            out[x, pl.ds(8 * (y % 8), 8), pl.ds(LANES * (y // 8), LANES)] = part
        return carry

    lax.fori_loop(0, 16, layer, 0)


def from_octants(ref, out, tables, tiles):
    rows = 16 * tiles

    def layer(x, carry):
        parts = []
        for y in range(16):
            part = ref[x, pl.ds(8 * (y % 8), 8), pl.ds(LANES * (y // 8), LANES)]
            parts.append(permute_in(part, tables)[:tiles])
        out[pl.ds(pl.multiple_of(x * rows, 8), rows), :] = jnp.concatenate(parts, axis=0)
        return carry

    lax.fori_loop(0, 16, layer, 0)


def put_pressures(ref, out):
    for x in range(16):
        i, ox = x % 8, x // 8
        f = ref[x]
        f = f + CUBIC_TERM * f * f * f
        out[pl.ds(64 * i, 64), pl.ds(256 * ox, 256)] = f.astype(BF16)


def one_hot(tile):
    return jnp.concatenate(
        [jnp.where(tile == float(o + 1), 1.0, 0.0).astype(BF16) for o in range(4)], axis=1
    )


def pieces(array):
    return [array[8 * n : 8 * n + 8] for n in range(8)]


def sweep(read, kap, masks):
    low, here, high = read
    inner, outer, last, first = masks
    halves = [[v[:, LANES * o : LANES * (o + 1)].reshape(8, 8, LANES) for v in (low, here, high)] for o in range(2)]
    out = []
    for o in range(2):
        below, c, above = halves[o]
        twin = halves[1 - o][1]
        if o == 0:
            y_above = jnp.concatenate([c[1:], twin[0:1]], axis=0)
            y_below = jnp.concatenate([c[0:1], c[:-1]], axis=0)
        else:
            y_above = jnp.concatenate([c[1:], c[7:8]], axis=0)
            y_below = jnp.concatenate([twin[7:8], c[:-1]], axis=0)
        r = pltpu.roll(c, 7, 1)
        z_above = jnp.where(inner, r, jnp.where(last, c, pltpu.roll(r, LANES - 1, 2)))
        r = pltpu.roll(c, 1, 1)
        z_below = jnp.where(outer, r, jnp.where(first, c, pltpu.roll(r, 1, 2)))
        base = 1.0 + c * c
        inflow = None
        for n in (above, below, y_above, y_below, z_above, z_below):
            part = (base + n * n) * (n - c)
            inflow = part if inflow is None else inflow + part
        out.append((c + kap[o] * inflow).reshape(64, LANES))
    return jnp.concatenate(out, axis=1)


def halves_of(ref, n):
    return jnp.concatenate(
        [ref[pl.ds(128 * n, 64), :], ref[pl.ds(128 * n + 64, 64), :]], axis=1
    )


def two_sweeps(phi, low, high, kap, kap_low, kap_high, wide, middle, out, q_count):
    k, lane = iota((8, 8, LANES), 1), iota((8, 8, LANES), 2)
    masks = (k < 7, k > 0, lane == q_count - 1, lane == 0)
    for n in range(2):
        wide[n] = halves_of(low, n)
        wide[18 + n] = halves_of(high, n)
    wide[pl.ds(2, 16)] = phi[...]

    def split(layer):
        return [layer[:, LANES * o : LANES * (o + 1)].reshape(8, 8, LANES) for o in range(2)]

    def around(ref, x):
        return ref[x - 1], ref[x], ref[x + 1]

    middle[0] = sweep(around(wide, 1), split(halves_of(kap_low, 0)), masks)
    middle[17] = sweep(around(wide, 18), split(halves_of(kap_high, 0)), masks)

    def first(x, carry):
        middle[x + 1] = sweep(around(wide, x + 2), split(kap[x]), masks)
        return carry

    lax.fori_loop(0, 16, first, 0)

    def second(x, carry):
        out[x] = sweep(around(middle, x + 1), split(kap[x]), masks)
        return carry

    lax.fori_loop(0, 16, second, 0)


def prepare(n_blk, cap, tiles, solvent):
    def body(grp, state, mat, occ, col, octant, send, sel, field, phi, kap, up, down, dil):
        e = state.shape[-1]

        @pl.when(grp[0] != solvent)
        def _():
            filled = occ[...].reshape(1, 1, e)
            dilate(state, filled, dil)
            hits = jnp.where(col[...] == iota((n_blk, e), 0), 1.0, 0.0)
            earlier = jnp.where(iota((e, e), 0) < iota((e, e), 1), 1.0, 0.0).astype(BF16)
            rank = dot(hits.astype(BF16), earlier, ((1,), (0,)))
            rank = jnp.sum(rank * hits, axis=0, keepdims=True).astype(jnp.int32)
            slot = col[...] * cap + rank
            chosen = jnp.where(iota((n_blk * cap, e), 0) == slot, 1.0, 0.0).astype(BF16)
            sel[...] = chosen
            send[:, pl.ds(0, 512)] = dot(chosen, dil[...], ((1,), (1,))).astype(BF16)
            o = octant[...]
            quarter = 16 * tiles
            block = sum((jnp.where(o >= n * quarter, 1, 0) for n in range(1, 4)))
            spot = o - quarter * block
            tile = jnp.where(iota((e, LANES), 1) == spot, (block + 1).astype(F32), 0.0)
            tile = dot(chosen, tile.astype(BF16), ((1,), (0,)))
            send[:, pl.ds(512, LANES)] = tile.astype(BF16)
            put_faces(state, up, down)
            up[pl.ds(192, 8), :] = jnp.broadcast_to(occ[...], (8, e))
            down[pl.ds(192, 8), :] = jnp.broadcast_to(occ[...], (8, e))

        @pl.when(grp[0] == solvent)
        def _():
            tables = tables_in()
            to_octants(state, phi, 1.0, tables, tiles)
            put_pressures(phi, field)
            to_octants(mat, kap, 0.5 * SWEEP_STEP, tables, tiles)
            for o in range(2):
                rows, lanes = pl.ds(64 * o, 64), pl.ds(LANES * o, LANES)
                up[rows, :] = kap[15, :, lanes]
                down[rows, :] = kap[0, :, lanes]

    return body


def gather_field(grp, recv, f0, f1, f2, out):
    g = grp[0]
    field = jnp.where(g == 0, f0[...], jnp.where(g == 1, f1[...], f2[...]))
    out[...] = dot(one_hot(recv[:, pl.ds(512, LANES)].astype(F32)), field, ((1,), (1,))).astype(BF16)


def first_step(state, mat, occ, sel, recv, low, high, out, send, up, down, *scratch):
    filled = occ[...].reshape(1, 1, occ.shape[-1])
    fills = (low[pl.ds(192, 1), :], high[pl.ds(192, 1), :])
    advance(state, mat, filled, recv, sel, low, high, fills, out, *scratch[:3])
    dil = scratch[3]
    dilate(out, filled, dil)
    send[...] = dot(sel[...], dil[...], ((1,), (1,))).astype(BF16)
    put_faces(out, up, down)


def last_step(state, mat, occ, sel, recv, low, high, fill_low, fill_high, out, *scratch):
    filled = occ[...].reshape(1, 1, occ.shape[-1])
    fills = (fill_low[pl.ds(192, 1), :], fill_high[pl.ds(192, 1), :])
    advance(state, mat, filled, recv, sel, low, high, fills, out, *scratch)


def deposit(with_hot):
    def body(phi, *refs):
        values, tiles = refs[:3], refs[3:6]
        out, up, down = refs[6:]
        total = None
        for v, t in zip(values, tiles):
            hot = one_hot(t[:, pl.ds(t.shape[-1] - LANES, LANES)].astype(F32))
            part = dot(v[:, pl.ds(0, 512)], hot, ((0,), (0,)))
            total = part if total is None else total + part
        for x in range(16):
            i, ox = x % 8, x // 8
            layer = phi[x] + (SWEEP_STEP * SOURCE_RATE) * total[64 * i : 64 * i + 64, 256 * ox : 256 * ox + 256]
            out[x] = layer
            for base, ref in ((14, up), (0, down)):
                if base <= x < base + 2:
                    for o in range(2):
                        ref[pl.ds(128 * (x - base) + 64 * o, 64), :] = layer[:, LANES * o : LANES * (o + 1)]

    return body


def spread_first(q_count):
    def body(phi, low, high, kap, kap_low, kap_high, t0, t1, t2, out, s0, s1, s2, wide, middle, field):
        two_sweeps(phi, low, high, kap, kap_low, kap_high, wide, middle, out, q_count)
        put_pressures(out, field)
        for t, s in ((t0, s0), (t1, s1), (t2, s2)):
            hot = one_hot(t[:, pl.ds(512, LANES)].astype(F32))
            s[...] = dot(hot, field[...], ((1,), (1,))).astype(BF16)

    return body


def spread_last(q_count, tiles):
    def body(phi, low, high, kap, kap_low, kap_high, out, wide, middle, final):
        two_sweeps(phi, low, high, kap, kap_low, kap_high, wide, middle, final, q_count)
        from_octants(final, out, tables_out(), tiles)

    return body


def shards(state, material, occupied, brick_column, brick_octant):
    e = state.shape[-1]
    n_blk, n_grp = lax.axis_size("blk"), lax.axis_size("grp")
    solvent, groups = n_grp - 1, range(n_grp - 1)
    cap = max(2, 2 * e // n_blk)
    slots = n_blk * cap
    tiles = 6 * e // LANES
    q_count = 6 * e // 8
    axes = ("grp", "blk")
    grp = lax.axis_index("grp").astype(jnp.int32)
    grp_at = grp.reshape(1)
    is_solvent = grp == solvent
    current = state.reshape(1536, e)
    mat = material.reshape(1536, e)
    occ = occupied.astype(F32).reshape(1, e)
    col = brick_column.reshape(1, e)
    octant = brick_octant.reshape(e, 1)
    field_shape, layers = (512, 4 * LANES), (16, 64, 2 * LANES)

    def pairs(back, g):
        forth = [(g * n_blk + b, solvent * n_blk + b) for b in range(n_blk)]
        return [(j, i) for i, j in forth] if back else forth

    def planes(up, which):
        steps = [(b, b + 1) for b in range(n_blk - 1)]
        steps = steps if up else [(j, i) for i, j in steps]
        return [(g * n_blk + i, g * n_blk + j) for g in which for i, j in steps]

    def both_ways(up, down, which):
        return (
            lax.ppermute(up, axes, planes(True, which)),
            lax.ppermute(down, axes, planes(False, which)),
        )

    def swap(block):
        return lax.all_to_all(block, "blk", split_axis=0, concat_axis=0, tiled=True)

    send, sel, field, phi, kap, up, down = call(
        prepare(n_blk, cap, tiles, solvent),
        (grp_at, current, mat, occ, col, octant),
        (
            shape_of((slots, 512 + LANES), BF16),
            shape_of((slots, e), BF16),
            shape_of(field_shape, BF16),
            shape_of(layers),
            shape_of(layers),
            shape_of((200, e)),
            shape_of((200, e)),
        ),
        [pltpu.VMEM((512, e), BF16)],
        smem=1,
        name="prepare",
    )
    recv = swap(send)
    fields = [lax.ppermute(field, axes, pairs(True, g)) for g in groups]
    side_low, side_high = both_ways(up, down, range(n_grp))
    arrived = [lax.ppermute(recv, axes, pairs(False, g)) for g in groups]
    halo = shape_of((256, LANES))
    rows = shape_of((slots, 512), BF16)
    flat = shape_of((1536, e))
    work = [pltpu.VMEM((512, e), F32), pltpu.VMEM((1536, e), F32), pltpu.VMEM((1536, e), F32)]
    wide = [pltpu.VMEM((20,) + layers[1:], F32), pltpu.VMEM((18,) + layers[1:], F32)]

    def solvent_first(_):
        added, up, down = call(
            deposit(True),
            (phi, *arrived, *arrived),
            (shape_of(layers), halo, halo),
            name="deposit_first",
        )
        low, high = both_ways(up, down, [solvent])
        spread, s0, s1, s2 = call(
            spread_first(q_count),
            (added, low, high, kap, side_low, side_high, *arrived),
            (shape_of(layers), rows, rows, rows),
            wide + [pltpu.VMEM(field_shape, BF16)],
            name="spread_first",
        )
        return spread.reshape(2048, LANES), s0, s1, s2, jnp.zeros(halo.shape), jnp.zeros(halo.shape)

    def mech_first(_):
        mine = call(gather_field, (grp_at, recv, *fields), rows, smem=1, name="gather")
        mine = swap(mine)
        face = shape_of((256, e))
        moved, send, up, down = call(
            first_step,
            (current, mat, occ, sel, mine, side_low, side_high),
            (shape_of((2048, e)), rows, face, face),
            work + [pltpu.VMEM((512, e), BF16)],
            name="first_step",
        )
        recv_next = swap(send)
        return moved, recv_next, recv_next, recv_next, up, down

    moved, out0, out1, out2, up, down = lax.cond(is_solvent, solvent_first, mech_first, 0)
    back = [
        lax.ppermute(block, axes, pairs(False, g) + pairs(True, g))
        for g, block in zip(groups, (out0, out1, out2))
    ]

    def solvent_last(_):
        added, up, down = call(
            deposit(False),
            (moved.reshape(layers), *back, *arrived),
            (shape_of(layers), halo, halo),
            name="deposit_last",
        )
        low, high = both_ways(up, down, [solvent])
        return call(
            spread_last(q_count, tiles),
            (added, low, high, kap, side_low, side_high),
            flat,
            wide + [pltpu.VMEM(layers, F32)],
            name="spread_last",
        )

    def mech_last(_):
        mine = swap(back[0] + back[1] + back[2])
        low, high = both_ways(up, down, groups)
        return call(
            last_step,
            (moved, mat, occ, sel, mine, low, high, side_low, side_high),
            flat,
            work,
            name="last_step",
        )

    return lax.cond(is_solvent, solvent_last, mech_last, 0).reshape(state.shape)


def solution(mesh):
    in_specs = (
        P("grp", None, None, "blk"),
        P("grp", None, None, "blk"),
        P(("grp", "blk")),
        P(("grp", "blk"), None),
        P(("grp", "blk")),
    )
    out_specs = P("grp", None, None, "blk")
    return jax.shard_map(shards, mesh=mesh, in_specs=in_specs, out_specs=out_specs, check_vma=False)
```

```python
import jax
import jax.numpy as jnp
from jax import lax
from jax.experimental import pallas as pl
from jax.experimental.pallas import tpu as pltpu
from jax.sharding import PartitionSpec as P

UNIT_LENGTH = 0.02
TIME_STEP = 0.1
PENALTY = 1.0
PRESSURE_SCALE = 0.05
DILATION_SCALE = 50.0
SWEEP_STEP = 0.03
SOURCE_RATE = 2.0
CUBIC_TERM = 0.3

LANES = 128
F32, BF16 = jnp.float32, jnp.bfloat16
VMEM = pl.BlockSpec(memory_space=pltpu.VMEM)
SMEM = pl.BlockSpec(memory_space=pltpu.SMEM)
ANY = pl.BlockSpec(memory_space=pl.ANY)


def shape_of(shape, dtype=F32):
    return jax.ShapeDtypeStruct(shape, dtype)


def call(body, args, outs, scratch=(), smem=0, name=None, away=(), unused=(), alias=None):
    specs = [SMEM] * smem + [VMEM] * (len(args) - smem)
    return pl.pallas_call(
        body,
        out_shape=outs,
        in_specs=[ANY if n in away else spec for n, spec in enumerate(specs)],
        out_specs=tuple(ANY if n in unused else VMEM for n in range(len(outs))),
        scratch_shapes=list(scratch),
        input_output_aliases=alias or {},
        name=name,
    )(*args)


def iota(shape, dim):
    return lax.broadcasted_iota(jnp.int32, shape, dim)


def dot(a, b, dims):
    return lax.dot_general(a, b, (dims, ((), ())), preferred_element_type=F32)


def diff_i(below, here, above, i):
    if below is None:
        return above - here
    if above is None:
        return here - below
    return 0.5 * (above - below)


def diff_j(x):
    return jnp.concatenate([x[1:2] - x[0:1], 0.5 * (x[2:] - x[:-2]), x[7:8] - x[6:7]], axis=0)


def diff_k(x):
    k = iota(x.shape, 1)
    upper = jnp.where(k == 7, x, pltpu.roll(x, 7, 1))
    lower = jnp.where(k == 0, x, pltpu.roll(x, 1, 1))
    return jnp.where((k == 0) | (k == 7), 1.0, 0.5) * (upper - lower)


def slab(ref, c, i):
    rows = ref[pl.ds(c * 512 + 64 * i, 64), :]
    return rows.reshape(8, 8, rows.shape[-1])


def put_slab(ref, c, i, value):
    ref[pl.ds(c * 512 + 64 * i, 64), :] = value.reshape(64, value.shape[-1])


def gradients(ref, i):
    grads = []
    for c in range(3):
        here = UNIT_LENGTH * slab(ref, c, i)
        below = UNIT_LENGTH * slab(ref, c, i - 1) if i > 0 else None
        above = UNIT_LENGTH * slab(ref, c, i + 1) if i < 7 else None
        row = [diff_i(below, here, above, i), diff_j(here), diff_k(here)]
        row[c] = row[c] + 1.0
        grads.append(row)
    return grads


def determinant(grads):
    return (
        grads[0][0] * (grads[1][1] * grads[2][2] - grads[1][2] * grads[2][1])
        - grads[0][1] * (grads[1][0] * grads[2][2] - grads[1][2] * grads[2][0])
        + grads[0][2] * (grads[1][0] * grads[2][1] - grads[1][1] * grads[2][0])
    )


def cofactors(g):
    return [
        [
            g[1][1] * g[2][2] - g[1][2] * g[2][1],
            g[1][2] * g[2][0] - g[1][0] * g[2][2],
            g[1][0] * g[2][1] - g[1][1] * g[2][0],
        ],
        [
            g[0][2] * g[2][1] - g[0][1] * g[2][2],
            g[0][0] * g[2][2] - g[0][2] * g[2][0],
            g[0][1] * g[2][0] - g[0][0] * g[2][1],
        ],
        [
            g[0][1] * g[1][2] - g[0][2] * g[1][1],
            g[0][2] * g[1][0] - g[0][0] * g[1][2],
            g[0][0] * g[1][1] - g[0][1] * g[1][0],
        ],
    ]


def dilate(ref, filled, out):
    for i in range(8):
        change = (determinant(gradients(ref, i)) - 1.0) * filled * DILATION_SCALE
        out[pl.ds(64 * i, 64), :] = change.reshape(64, change.shape[-1]).astype(BF16)


def put_faces(ref, up, down):
    for c in range(3):
        up[pl.ds(64 * c, 64), :] = ref[pl.ds(c * 512 + 448, 64), :]
        down[pl.ds(64 * c, 64), :] = ref[pl.ds(c * 512, 64), :]


def advance(ref, mat, filled, recv, sel, low, high, fills, out, pressure, stress, partial):
    e = filled.shape[-1]
    pressure[...] = dot(recv[...], sel[...], ((0,), (0,))) * PRESSURE_SCALE
    for i in range(8):
        g = gradients(ref, i)
        shear, lame = slab(mat, 0, i), slab(mat, 1, i)
        c = {}
        for a in range(3):
            for b in range(a, 3):
                c[a, b] = g[0][a] * g[0][b] + g[1][a] * g[1][b] + g[2][a] * g[2][b]
        diag = [c[a, a] - 1.0 for a in range(3)]
        volume = lame * (0.5 * (diag[0] + diag[1] + diag[2]))
        s = {}
        for a in range(3):
            s[a, a] = shear * diag[a] + volume
            for b in range(a + 1, 3):
                s[a, b] = s[b, a] = shear * c[a, b]
        cof = cofactors(g)
        p = pressure[pl.ds(64 * i, 64), :].reshape(8, 8, e)
        for a in range(3):
            first = [
                g[a][0] * s[0, b] + g[a][1] * s[1, b] + g[a][2] * s[2, b] - p * cof[a][b]
                for b in range(3)
            ]
            put_slab(stress, a, i, first[0])
            put_slab(partial, a, i, diff_j(first[1]) + diff_k(first[2]))
    penalty = PENALTY * UNIT_LENGTH
    k = iota((8, 8, e), 1)
    fill_low, fill_high = fills[0].reshape(1, 1, e), fills[1].reshape(1, 1, e)
    lane = iota((1, 1, e), 2)
    fill_before = jnp.where(lane == 0, 0.0, pltpu.roll(filled, 1, 2)) * penalty
    fill_after = jnp.where(lane == e - 1, 0.0, pltpu.roll(filled, e - 1, 2)) * penalty
    before_scale = jnp.where(k == 0, fill_before, 0.0)
    after_scale = jnp.where(k == 7, fill_after, 0.0)
    for i in range(8):
        rate = (TIME_STEP / UNIT_LENGTH) * slab(mat, 2, i) * filled
        for a in range(3):
            here = slab(ref, a, i)
            force = slab(partial, a, i) + diff_i(
                slab(stress, a, i - 1) if i > 0 else None,
                slab(stress, a, i),
                slab(stress, a, i + 1) if i < 7 else None,
                i,
            )
            if i == 0:
                other = low[pl.ds(64 * a, 64), :].reshape(8, 8, e)
                force = force + penalty * fill_low * (other - here)
            if i == 7:
                other = high[pl.ds(64 * a, 64), :].reshape(8, 8, e)
                force = force + penalty * fill_high * (other - here)
            before = pltpu.roll(pltpu.roll(here, 1, 1), 1, 2)
            after = pltpu.roll(pltpu.roll(here, 7, 1), e - 1, 2)
            force = force + before_scale * (before - here) + after_scale * (after - here)
            put_slab(out, a, i, here + rate * force)


def permute_in(x, tables):
    x = jnp.take_along_axis(x, tables[0], axis=1, mode="promise_in_bounds")
    x = jnp.take_along_axis(x, tables[1], axis=0, mode="promise_in_bounds")
    return jnp.take_along_axis(x, tables[2], axis=1, mode="promise_in_bounds")


def tables_in():
    row, lane = iota((8, LANES), 0), iota((8, LANES), 1)
    high, low = lane // 16, lane % 16
    return (8 * low + (high - row + 8) % 8, (high - row + 8) % 8, 16 * ((high + row) % 8) + low)


def tables_out():
    row, lane = iota((8, LANES), 0), iota((8, LANES), 1)
    high, low = lane // 16, lane % 16
    return (
        16 * ((high - row + 8) % 8) + low,
        (high - row + 8) % 8,
        16 * ((lane % 8 + row) % 8) + lane // 8,
    )


def layer_to_octants(chunk, scale, tables, tiles):
    rows = chunk.shape[0]
    lane = iota((8, LANES), 1)
    parts = []
    for y in range(16):
        part = chunk[tiles * y : min(tiles * y + 8, rows)]
        if part.shape[0] < 8:
            pad = jnp.zeros((8 - part.shape[0], LANES), F32)
            part = jnp.concatenate([part, pad], axis=0)
        part = permute_in(part, tables)
        parts.append(jnp.where(lane < 16 * tiles, part, 0.0))
    layer = jnp.concatenate(parts, axis=0)
    return layer * scale if scale != 1.0 else layer


def to_octants(ref, out, scale, tables, tiles):
    rows = 16 * tiles

    def layer(x, carry):
        chunk = ref[pl.ds(pl.multiple_of(x * rows, 8), rows), :]
        out[layer_rows(x), :] = layer_to_octants(chunk, scale, tables, tiles)
        return carry

    lax.fori_loop(0, 16, layer, 0)


def layer_from_octants(layer, tables, tiles):
    return jnp.concatenate(
        [permute_in(layer[8 * y : 8 * y + 8], tables)[:tiles] for y in range(16)], axis=0
    )


def layer_rows(x):
    return pl.ds(pl.multiple_of(x * LANES, LANES), LANES)


def pressures(layer):
    return (layer + CUBIC_TERM * layer * layer * layer).astype(BF16)


def one_hot(tile, width):
    return jnp.concatenate(
        [jnp.where(tile == float(o + 1), 1.0, 0.0).astype(BF16)[:, :width] for o in range(4)],
        axis=1,
    )


def sweep(below, here, above, kap, masks):
    inner, outer, last, first = masks
    halves = [v.reshape(2, 8, 8, LANES) for v in (below, here, above, kap)]
    out = []
    for o in range(2):
        low, c, high, rate = (v[o] for v in halves)
        twin = halves[1][1 - o]
        if o == 0:
            y_above = jnp.concatenate([c[1:], twin[0:1]], axis=0)
            y_below = jnp.concatenate([c[0:1], c[:-1]], axis=0)
        else:
            y_above = jnp.concatenate([c[1:], c[7:8]], axis=0)
            y_below = jnp.concatenate([twin[7:8], c[:-1]], axis=0)
        r = pltpu.roll(c, 7, 1)
        z_above = jnp.where(inner, r, jnp.where(last, c, pltpu.roll(r, LANES - 1, 2)))
        r = pltpu.roll(c, 1, 1)
        z_below = jnp.where(outer, r, jnp.where(first, c, pltpu.roll(r, 1, 2)))
        base = 1.0 + c * c
        inflow = None
        for n in (high, low, y_above, y_below, z_above, z_below):
            part = (base + n * n) * (n - c)
            inflow = part if inflow is None else inflow + part
        out.append((c + rate * inflow).reshape(64, LANES))
    return jnp.concatenate(out, axis=0)


def sweep_masks(q_count):
    k, lane = iota((8, 8, LANES), 1), iota((8, 8, LANES), 2)
    return k < 7, k > 0, lane == q_count - 1, lane == 0


def inner_sweeps(phi, kap, middle, edges, put, q_count):
    masks = sweep_masks(q_count)

    def around(ref, x):
        return ref[layer_rows(x - 1), :], ref[layer_rows(x), :], ref[layer_rows(x + 1), :]

    def first(x, carry):
        middle[layer_rows(x), :] = sweep(*around(phi, x), kap[layer_rows(x), :], masks)
        return carry

    def second(x, carry):
        put(x, sweep(*around(middle, x), kap[layer_rows(x), :], masks))
        return carry

    lax.fori_loop(1, 15, first, 0)
    for n, x in enumerate((1, 2, 13, 14)):
        edges[layer_rows(n), :] = middle[layer_rows(x), :]
    lax.fori_loop(2, 14, second, 0)


def edge_sweeps(top, bottom, low, high, kap_edge, kap_low, kap_high, middle, q_count):
    masks = sweep_masks(q_count)

    def of(ref, n):
        return ref[LANES * n : LANES * (n + 1), :]

    k = [of(kap_edge, n) for n in range(4)]
    far_low, near_low, a, b = of(low, 0), of(low, 1), of(bottom, 0), of(bottom, 1)
    c, d, near_high, far_high = of(top, 0), of(top, 1), of(high, 0), of(high, 1)
    m = [of(middle, n) for n in range(4)]
    before = sweep(far_low, near_low, a, of(kap_low, 0), masks)
    zero = sweep(near_low, a, b, k[0], masks)
    last = sweep(c, d, near_high, k[3], masks)
    after = sweep(d, near_high, far_high, of(kap_high, 0), masks)
    return [
        sweep(before, zero, m[0], k[0], masks),
        sweep(zero, m[0], m[1], k[1], masks),
        sweep(m[2], m[3], last, k[2], masks),
        sweep(m[3], last, after, k[3], masks),
    ]


def prepare(n_blk, cap, tiles, solvent):
    def body(grp, state, mat, occ, col, octant, send, sel, field, phi, up, down, dil, edge, sem):
        e = state.shape[-1]
        quarter, rows = 16 * tiles, 16 * tiles

        @pl.when(grp[0] != solvent)
        def _():
            filled = occ[...].reshape(1, 1, e)
            dilate(state, filled, dil)
            hits = jnp.where(col[...] == iota((n_blk, e), 0), 1.0, 0.0)
            earlier = jnp.where(iota((e, e), 0) < iota((e, e), 1), 1.0, 0.0).astype(BF16)
            rank = dot(hits.astype(BF16), earlier, ((1,), (0,)))
            rank = jnp.sum(rank * hits, axis=0, keepdims=True).astype(jnp.int32)
            slot = col[...] * cap + rank
            chosen = jnp.where(iota((n_blk * cap, e), 0) == slot, 1.0, 0.0).astype(BF16)
            sel[...] = chosen
            send[:, pl.ds(0, 512)] = dot(chosen, dil[...], ((1,), (1,))).astype(BF16)
            o = octant[...]
            block = sum((jnp.where(o >= n * quarter, 1, 0) for n in range(1, 4)))
            spot = o - quarter * block
            tile = jnp.where(iota((LANES, e), 0) == spot, (block + 1).astype(F32), 0.0)
            tile = dot(chosen, tile.astype(BF16), ((1,), (1,)))
            send[:, pl.ds(512, LANES)] = tile.astype(BF16)
            put_faces(state, up, down)
            up[pl.ds(192, 8), :] = jnp.broadcast_to(occ[...], (8, e))
            down[pl.ds(192, 8), :] = jnp.broadcast_to(occ[...], (8, e))

        @pl.when(grp[0] == solvent)
        def _():
            copies = [
                pltpu.make_async_copy(mat.at[pl.ds(rows * x, rows)], edge.at[n], sem.at[n])
                for n, x in enumerate((0, 15))
            ]
            for copy in copies:
                copy.start()
            tables = tables_in()
            to_octants(state, phi, 1.0, tables, tiles)
            for i in range(8):
                parts = []
                for ox in range(2):
                    for oy in range(2):
                        p = pressures(phi[pl.ds(LANES * (8 * ox + i) + 64 * oy, 64), :])
                        parts.append(p[:, :quarter])
                field[pl.ds(64 * i, 64), :] = jnp.concatenate(parts, axis=1)
            for copy in copies:
                copy.wait()
            for n, ref in enumerate((down, up)):
                layer = layer_to_octants(edge[n], 0.5 * SWEEP_STEP, tables, tiles)
                ref[pl.ds(0, LANES), :] = layer

    return body


def rates(tiles):
    def body(mat, kap, edge, *unused):
        to_octants(mat, kap, 0.5 * SWEEP_STEP, tables_in(), tiles)
        for n, x in enumerate((0, 1, 14, 15)):
            edge[layer_rows(n), :] = kap[layer_rows(x), :]

    return body


def gather_field(quarter):
    def body(recv, field, out):
        hot = one_hot(recv[:, pl.ds(512, LANES)].astype(F32), quarter)
        out[...] = dot(hot, field[...], ((1,), (1,))).astype(BF16)

    return body


def first_step(state, mat, occ, sel, recv, low, high, out, send, up, down, *scratch):
    filled = occ[...].reshape(1, 1, occ.shape[-1])
    fills = (low[pl.ds(192, 1), :], high[pl.ds(192, 1), :])
    advance(state, mat, filled, recv, sel, low, high, fills, out, *scratch[:3])
    dil = scratch[3]
    dilate(out, filled, dil)
    send[...] = dot(sel[...], dil[...], ((1,), (1,))).astype(BF16)
    put_faces(out, up, down)


def last_step(state, mat, occ, sel, recv, low, high, fill_low, fill_high, out, *scratch):
    filled = occ[...].reshape(1, 1, occ.shape[-1])
    fills = (fill_low[pl.ds(192, 1), :], fill_high[pl.ds(192, 1), :])
    advance(state, mat, filled, recv, sel, low, high, fills, out, *scratch)


def deposit(edged):
    def body(phi, *refs):
        edge = refs[0] if edged else None
        refs = refs[1:] if edged else refs
        values, tiles = refs[:3], refs[3:6]
        out, up, down = refs[6:]
        total = None
        for v, t in zip(values, tiles):
            hot = one_hot(t[:, pl.ds(512, LANES)].astype(F32), LANES)
            part = dot(v[:, pl.ds(0, 512)], hot, ((0,), (0,)))
            total = part if total is None else total + part
        for x in range(16):
            i, ox = x % 8, x // 8
            if edged and x in (0, 1, 14, 15):
                layer = edge[layer_rows((0, 1, 14, 15).index(x)), :]
            else:
                layer = phi[layer_rows(x), :]
            added = jnp.concatenate(
                [
                    total[64 * i : 64 * i + 64, 256 * ox + LANES * o : 256 * ox + LANES * (o + 1)]
                    for o in range(2)
                ],
                axis=0,
            )
            layer = layer + (SWEEP_STEP * SOURCE_RATE) * added
            out[layer_rows(x), :] = layer
            if x < 2:
                down[layer_rows(x), :] = layer
            if x >= 14:
                up[layer_rows(x - 14), :] = layer

    return body


def inner_first(q_count):
    def body(phi, kap, out, edges, middle):
        def put(x, layer):
            out[layer_rows(x), :] = layer

        inner_sweeps(phi, kap, middle, edges, put, q_count)

    return body


def outer_first(q_count):
    def body(up, down, low, high, kap_edge, kap_low, kap_high, mid, phi, t0, t1, t2, edge, s0, s1, s2, field):
        final = edge_sweeps(up, down, low, high, kap_edge, kap_low, kap_high, mid, q_count)
        for n in range(4):
            edge[layer_rows(n), :] = final[n]
        for x in range(16):
            i, ox = x % 8, x // 8
            layer = final[(0, 1, 14, 15).index(x)] if x in (0, 1, 14, 15) else phi[layer_rows(x), :]
            p = pressures(layer)
            for o in range(2):
                field[pl.ds(64 * i, 64), pl.ds(256 * ox + LANES * o, LANES)] = p[64 * o : 64 * o + 64]
        for t, s in ((t0, s0), (t1, s1), (t2, s2)):
            hot = one_hot(t[:, pl.ds(512, LANES)].astype(F32), LANES)
            s[...] = dot(hot, field[...], ((1,), (1,))).astype(BF16)

    return body


def inner_last(q_count, tiles):
    def body(phi, kap, out, edges, middle):
        tables = tables_out()
        rows = 16 * tiles

        def put(x, layer):
            spot = pl.ds(pl.multiple_of(x * rows, 8), rows)
            out[spot, :] = layer_from_octants(layer, tables, tiles)

        inner_sweeps(phi, kap, middle, edges, put, q_count)

    return body


def outer_last(q_count, tiles):
    def body(up, down, low, high, kap_edge, kap_low, kap_high, mid, _, out, ends, sem):
        final = edge_sweeps(up, down, low, high, kap_edge, kap_low, kap_high, mid, q_count)
        tables = tables_out()
        rows = 16 * tiles
        for n in range(4):
            ends[pl.ds(rows * n, rows), :] = layer_from_octants(final[n], tables, tiles)
        copies = [
            pltpu.make_async_copy(
                ends.at[pl.ds(2 * rows * n, 2 * rows)], out.at[pl.ds(start, 2 * rows)], sem.at[n]
            )
            for n, start in enumerate((0, 14 * rows))
        ]
        for copy in copies:
            copy.start()
        for copy in copies:
            copy.wait()

    return body


def shards(state, material, occupied, brick_column, brick_octant):
    e = state.shape[-1]
    n_blk, n_grp = lax.axis_size("blk"), lax.axis_size("grp")
    solvent, groups = n_grp - 1, range(n_grp - 1)
    cap = max(2, 2 * e // n_blk)
    slots = n_blk * cap
    tiles = 6 * e // LANES
    q_count = 6 * e // 8
    axes = ("grp", "blk")
    grp = lax.axis_index("grp").astype(jnp.int32)
    grp_at = grp.reshape(1)
    current = state.reshape(1536, e)
    mat = material.reshape(1536, e)
    occ = occupied.astype(F32).reshape(1, e)
    col = brick_column.reshape(1, e)
    octant = brick_octant.reshape(1, e)
    layers, ends, halo = shape_of((2048, LANES)), shape_of((512, LANES)), shape_of((256, LANES))
    rows, flat, face = shape_of((slots, 512), BF16), shape_of((1536, e)), shape_of((256, e))

    def pairs(back, g):
        forth = [(g * n_blk + b, solvent * n_blk + b) for b in range(n_blk)]
        return [(j, i) for i, j in forth] if back else forth

    def planes(up, which):
        steps = [(b, b + 1) for b in range(n_blk - 1)]
        steps = steps if up else [(j, i) for i, j in steps]
        return [(g * n_blk + i, g * n_blk + j) for g in which for i, j in steps]

    def both_ways(up, down, which):
        return (
            lax.ppermute(up, axes, planes(True, which)),
            lax.ppermute(down, axes, planes(False, which)),
        )

    def swap(block):
        return lax.all_to_all(block, "blk", split_axis=0, concat_axis=0, tiled=True)

    send, sel, field, phi, up, down = call(
        prepare(n_blk, cap, tiles, solvent),
        (grp_at, current, mat, occ, col, octant),
        (
            shape_of((slots, 512 + LANES), BF16),
            shape_of((slots, e), BF16),
            shape_of((512, 4 * q_count), BF16),
            layers,
            shape_of((200, e)),
            shape_of((200, e)),
        ),
        [
            pltpu.VMEM((512, e), BF16),
            pltpu.VMEM((2, 16 * tiles, LANES), F32),
            pltpu.SemaphoreType.DMA((2,)),
        ],
        smem=1,
        away=(2,),
        name="prepare",
    )
    recv = swap(send)
    fields = [lax.ppermute(field, axes, pairs(True, g)) for g in groups]
    side_low, side_high = both_ways(up, down, range(n_grp))
    arrived = [lax.ppermute(recv, axes, pairs(False, g)) for g in groups]
    work = [pltpu.VMEM((512, e), F32), pltpu.VMEM((1536, e), F32), pltpu.VMEM((1536, e), F32)]
    middle = pltpu.VMEM(layers.shape, F32)

    def solvent_rates():
        outs = (layers, ends, rows, face, face)
        kap, edge, dummy, up, down = call(rates(tiles), (mat,), outs, unused=(2, 3, 4), name="rates")
        return kap, edge, dummy, up, down

    def mech_first(g):
        def run():
            (mine,) = call(gather_field(q_count), (recv, fields[g]), (rows,), name="gather")
            mine = swap(mine)
            moved, send, up, down, spare = call(
                lambda *refs: first_step(*refs[:11], *refs[12:]),
                (current, mat, occ, sel, mine, side_low, side_high),
                (shape_of((2048, e)), rows, face, face, ends),
                work + [pltpu.VMEM((512, e), BF16)],
                unused=(4,),
                name="first_step",
            )
            return moved, spare, send, up, down

        return run

    branches = [mech_first(g) for g in groups] + [solvent_rates]
    moved, kap_edge, send, up, down = lax.switch(grp, branches)
    face_low, face_high = both_ways(up, down, groups)

    def solvent_first():
        added, top, bottom = call(
            deposit(False), (phi, *arrived, *arrived), (layers, halo, halo), name="deposit_first"
        )
        low, high = both_ways(top, bottom, [solvent])
        inner, mid = call(
            inner_first(q_count), (added, moved), (layers, ends), [middle], name="inner_first"
        )
        edge, s0, s1, s2 = call(
            outer_first(q_count),
            (top, bottom, low, high, kap_edge, side_low, side_high, mid, inner, *arrived),
            (ends, rows, rows, rows),
            [pltpu.VMEM((512, 4 * LANES), BF16)],
            name="outer_first",
        )
        return inner, edge, s0, s1, s2

    def mech_turn(g):
        def run():
            mine = swap(send)
            spare = call(
                lambda *refs: None,
                (),
                (layers, ends, rows, rows),
                unused=(0, 1, 2, 3),
                name="spare",
            )
            blocks = list(spare[2:])
            blocks.insert(g, mine)
            return spare[0], spare[1], *blocks

        return run

    inner, edge, *blocks = lax.switch(grp, [mech_turn(g) for g in groups] + [solvent_first])
    back = [
        lax.ppermute(block, axes, pairs(False, g) + pairs(True, g))
        for g, block in zip(groups, blocks)
    ]

    def solvent_last():
        added, top, bottom = call(
            deposit(True),
            (inner, edge, *back, *arrived),
            (layers, halo, halo),
            name="deposit_last",
        )
        low, high = both_ways(top, bottom, [solvent])
        out, mid = call(
            inner_last(q_count, tiles), (added, moved), (flat, ends), [middle], name="inner_last"
        )
        (out,) = call(
            outer_last(q_count, tiles),
            (top, bottom, low, high, kap_edge, side_low, side_high, mid, out),
            (flat,),
            [pltpu.VMEM((4 * 16 * tiles, LANES), F32), pltpu.SemaphoreType.DMA((2,))],
            away=(8,),
            unused=(0,),
            alias={8: 0},
            name="outer_last",
        )
        return out

    def mech_last(g):
        def run():
            mine = swap(back[g])
            (out,) = call(
                last_step,
                (moved, mat, occ, sel, mine, face_low, face_high, side_low, side_high),
                (flat,),
                work,
                name="last_step",
            )
            return out

        return run

    return lax.switch(grp, [mech_last(g) for g in groups] + [solvent_last]).reshape(state.shape)


def solution(mesh):
    in_specs = (
        P("grp", None, None, "blk"),
        P("grp", None, None, "blk"),
        P(("grp", "blk")),
        P(("grp", "blk"), None),
        P(("grp", "blk")),
    )
    out_specs = P("grp", None, None, "blk")
    return jax.shard_map(shards, mesh=mesh, in_specs=in_specs, out_specs=out_specs, check_vma=False)
```

```python
import jax
import jax.numpy as jnp
from jax import lax
from jax.experimental import pallas as pl
from jax.experimental.pallas import tpu as pltpu
from jax.sharding import PartitionSpec as P

UNIT_LENGTH = 0.02
TIME_STEP = 0.1
PENALTY = 1.0
PRESSURE_SCALE = 0.05
DILATION_SCALE = 50.0
SWEEP_STEP = 0.03
SOURCE_RATE = 2.0
CUBIC_TERM = 0.3

LANES = 128
VMEM_LIMIT = 24 << 20
F32, BF16 = jnp.float32, jnp.bfloat16
VMEM = pl.BlockSpec(memory_space=pltpu.VMEM)
SMEM = pl.BlockSpec(memory_space=pltpu.SMEM)
ANY = pl.BlockSpec(memory_space=pl.ANY)


def shape_of(shape, dtype=F32):
    return jax.ShapeDtypeStruct(shape, dtype)


def call(body, args, outs, scratch=(), smem=0, name=None, away=(), unused=(), alias=None):
    specs = [SMEM] * smem + [VMEM] * (len(args) - smem)
    return pl.pallas_call(
        body,
        out_shape=outs,
        in_specs=[ANY if n in away else spec for n, spec in enumerate(specs)],
        out_specs=tuple(ANY if n in unused else VMEM for n in range(len(outs))),
        scratch_shapes=list(scratch),
        input_output_aliases=alias or {},
        compiler_params=pltpu.CompilerParams(vmem_limit_bytes=VMEM_LIMIT),
        name=name,
    )(*args)


def iota(shape, dim):
    return lax.broadcasted_iota(jnp.int32, shape, dim)


def dot(a, b, dims):
    return lax.dot_general(a, b, (dims, ((), ())), preferred_element_type=F32)


def diff_i(below, here, above, i):
    if below is None:
        return above - here
    if above is None:
        return here - below
    return 0.5 * (above - below)


def diff_j(x):
    return jnp.concatenate([x[1:2] - x[0:1], 0.5 * (x[2:] - x[:-2]), x[7:8] - x[6:7]], axis=0)


def diff_k(x):
    k = iota(x.shape, 1)
    upper = jnp.where(k == 7, x, pltpu.roll(x, 7, 1))
    lower = jnp.where(k == 0, x, pltpu.roll(x, 1, 1))
    return jnp.where((k == 0) | (k == 7), 1.0, 0.5) * (upper - lower)


def slab(ref, c, i):
    rows = ref[pl.ds(c * 512 + 64 * i, 64), :]
    return rows.reshape(8, 8, rows.shape[-1])


def put_slab(ref, c, i, value):
    ref[pl.ds(c * 512 + 64 * i, 64), :] = value.reshape(64, value.shape[-1])


def gradients(ref, i):
    grads = []
    for c in range(3):
        here = UNIT_LENGTH * slab(ref, c, i)
        below = UNIT_LENGTH * slab(ref, c, i - 1) if i > 0 else None
        above = UNIT_LENGTH * slab(ref, c, i + 1) if i < 7 else None
        row = [diff_i(below, here, above, i), diff_j(here), diff_k(here)]
        row[c] = row[c] + 1.0
        grads.append(row)
    return grads


def determinant(grads):
    return (
        grads[0][0] * (grads[1][1] * grads[2][2] - grads[1][2] * grads[2][1])
        - grads[0][1] * (grads[1][0] * grads[2][2] - grads[1][2] * grads[2][0])
        + grads[0][2] * (grads[1][0] * grads[2][1] - grads[1][1] * grads[2][0])
    )


def cofactors(g):
    return [
        [
            g[1][1] * g[2][2] - g[1][2] * g[2][1],
            g[1][2] * g[2][0] - g[1][0] * g[2][2],
            g[1][0] * g[2][1] - g[1][1] * g[2][0],
        ],
        [
            g[0][2] * g[2][1] - g[0][1] * g[2][2],
            g[0][0] * g[2][2] - g[0][2] * g[2][0],
            g[0][1] * g[2][0] - g[0][0] * g[2][1],
        ],
        [
            g[0][1] * g[1][2] - g[0][2] * g[1][1],
            g[0][2] * g[1][0] - g[0][0] * g[1][2],
            g[0][0] * g[1][1] - g[0][1] * g[1][0],
        ],
    ]


def dilate(ref, filled, out):
    for i in range(8):
        change = (determinant(gradients(ref, i)) - 1.0) * filled * DILATION_SCALE
        out[pl.ds(64 * i, 64), :] = change.reshape(64, change.shape[-1]).astype(BF16)


def put_faces(ref, up, down):
    for c in range(3):
        up[pl.ds(64 * c, 64), :] = ref[pl.ds(c * 512 + 448, 64), :]
        down[pl.ds(64 * c, 64), :] = ref[pl.ds(c * 512, 64), :]


def elastic(ref, mat, filled, out, stress, partial):
    e = filled.shape[-1]
    for i in range(8):
        g = gradients(ref, i)
        shear, lame = slab(mat, 0, i), slab(mat, 1, i)
        c = {}
        for a in range(3):
            for b in range(a, 3):
                c[a, b] = g[0][a] * g[0][b] + g[1][a] * g[1][b] + g[2][a] * g[2][b]
        diag = [c[a, a] - 1.0 for a in range(3)]
        volume = lame * (0.5 * (diag[0] + diag[1] + diag[2]))
        s = {}
        for a in range(3):
            s[a, a] = shear * diag[a] + volume
            for b in range(a + 1, 3):
                s[a, b] = s[b, a] = shear * c[a, b]
        for a in range(3):
            first = [g[a][0] * s[0, b] + g[a][1] * s[1, b] + g[a][2] * s[2, b] for b in range(3)]
            put_slab(stress, a, i, first[0])
            put_slab(partial, a, i, diff_j(first[1]) + diff_k(first[2]))
    k = iota((8, 8, e), 1)
    lane = iota((1, 1, e), 2)
    penalty = PENALTY * UNIT_LENGTH
    fill_before = jnp.where(lane == 0, 0.0, pltpu.roll(filled, 1, 2)) * penalty
    fill_after = jnp.where(lane == e - 1, 0.0, pltpu.roll(filled, e - 1, 2)) * penalty
    before_scale = jnp.where(k == 0, fill_before, 0.0)
    after_scale = jnp.where(k == 7, fill_after, 0.0)
    for i in range(8):
        for a in range(3):
            here = slab(ref, a, i)
            force = slab(partial, a, i) + diff_i(
                slab(stress, a, i - 1) if i > 0 else None,
                slab(stress, a, i),
                slab(stress, a, i + 1) if i < 7 else None,
                i,
            )
            before = pltpu.roll(pltpu.roll(here, 1, 1), 1, 2)
            after = pltpu.roll(pltpu.roll(here, 7, 1), e - 1, 2)
            force = force + before_scale * (before - here) + after_scale * (after - here)
            put_slab(out, a, i, force)


def advance(ref, mat, filled, base, recv, sel, low, high, fills, out, pressure, stress, partial):
    e = filled.shape[-1]
    pressure[...] = dot(recv[...], sel[...], ((0,), (0,))) * PRESSURE_SCALE
    for i in range(8):
        cof = cofactors(gradients(ref, i))
        p = pressure[pl.ds(64 * i, 64), :].reshape(8, 8, e)
        for a in range(3):
            first = [p * cof[a][b] for b in range(3)]
            put_slab(stress, a, i, first[0])
            put_slab(partial, a, i, slab(base, a, i) - (diff_j(first[1]) + diff_k(first[2])))
    penalty = PENALTY * UNIT_LENGTH
    fill_low, fill_high = fills[0].reshape(1, 1, e), fills[1].reshape(1, 1, e)
    for i in range(8):
        rate = (TIME_STEP / UNIT_LENGTH) * slab(mat, 2, i) * filled
        for a in range(3):
            here = slab(ref, a, i)
            force = slab(partial, a, i) - diff_i(
                slab(stress, a, i - 1) if i > 0 else None,
                slab(stress, a, i),
                slab(stress, a, i + 1) if i < 7 else None,
                i,
            )
            if i == 0:
                other = low[pl.ds(64 * a, 64), :].reshape(8, 8, e)
                force = force + penalty * fill_low * (other - here)
            if i == 7:
                other = high[pl.ds(64 * a, 64), :].reshape(8, 8, e)
                force = force + penalty * fill_high * (other - here)
            put_slab(out, a, i, here + rate * force)


def permute_in(x, tables):
    x = jnp.take_along_axis(x, tables[0], axis=1, mode="promise_in_bounds")
    x = jnp.take_along_axis(x, tables[1], axis=0, mode="promise_in_bounds")
    return jnp.take_along_axis(x, tables[2], axis=1, mode="promise_in_bounds")


def tables_in():
    row, lane = iota((8, LANES), 0), iota((8, LANES), 1)
    high, low = lane // 16, lane % 16
    return (8 * low + (high - row + 8) % 8, (high - row + 8) % 8, 16 * ((high + row) % 8) + low)


def tables_out():
    row, lane = iota((8, LANES), 0), iota((8, LANES), 1)
    high, low = lane // 16, lane % 16
    return (
        16 * ((high - row + 8) % 8) + low,
        (high - row + 8) % 8,
        16 * ((lane % 8 + row) % 8) + lane // 8,
    )


def layer_to_octants(chunk, scale, tables, tiles):
    rows = chunk.shape[0]
    lane = iota((8, LANES), 1)
    parts = []
    for y in range(16):
        part = chunk[tiles * y : min(tiles * y + 8, rows)]
        if part.shape[0] < 8:
            pad = jnp.zeros((8 - part.shape[0], LANES), F32)
            part = jnp.concatenate([part, pad], axis=0)
        part = permute_in(part, tables)
        parts.append(jnp.where(lane < 16 * tiles, part, 0.0))
    layer = jnp.concatenate(parts, axis=0)
    return layer * scale if scale != 1.0 else layer


def to_octants(ref, out, scale, tables, tiles):
    rows = 16 * tiles

    def layer(x, carry):
        chunk = ref[pl.ds(pl.multiple_of(x * rows, 8), rows), :]
        out[layer_rows(x), :] = layer_to_octants(chunk, scale, tables, tiles)
        return carry

    lax.fori_loop(0, 16, layer, 0)


def layer_from_octants(layer, tables, tiles):
    return jnp.concatenate(
        [permute_in(layer[8 * y : 8 * y + 8], tables)[:tiles] for y in range(16)], axis=0
    )


def layer_rows(x):
    return pl.ds(pl.multiple_of(x * LANES, LANES), LANES)


def pressures(layer):
    return (layer + CUBIC_TERM * layer * layer * layer).astype(BF16)


def one_hot(tile, width):
    return jnp.concatenate(
        [jnp.where(tile == float(o + 1), 1.0, 0.0).astype(BF16)[:, :width] for o in range(4)],
        axis=1,
    )


def sweep(below, here, above, kap, masks):
    inner, outer, last, first = masks
    halves = [v.reshape(2, 8, 8, LANES) for v in (below, here, above, kap)]
    out = []
    for o in range(2):
        low, c, high, rate = (v[o] for v in halves)
        twin = halves[1][1 - o]
        if o == 0:
            y_above = jnp.concatenate([c[1:], twin[0:1]], axis=0)
            y_below = jnp.concatenate([c[0:1], c[:-1]], axis=0)
        else:
            y_above = jnp.concatenate([c[1:], c[7:8]], axis=0)
            y_below = jnp.concatenate([twin[7:8], c[:-1]], axis=0)
        r = pltpu.roll(c, 7, 1)
        z_above = jnp.where(inner, r, jnp.where(last, c, pltpu.roll(r, LANES - 1, 2)))
        r = pltpu.roll(c, 1, 1)
        z_below = jnp.where(outer, r, jnp.where(first, c, pltpu.roll(r, 1, 2)))
        base = 1.0 + c * c
        inflow = None
        for n in (high, low, y_above, y_below, z_above, z_below):
            part = (base + n * n) * (n - c)
            inflow = part if inflow is None else inflow + part
        out.append((c + rate * inflow).reshape(64, LANES))
    return jnp.concatenate(out, axis=0)


def sweep_masks(q_count):
    k, lane = iota((8, 8, LANES), 1), iota((8, 8, LANES), 2)
    return k < 7, k > 0, lane == q_count - 1, lane == 0


def inner_sweeps(phi, kap, middle, edges, put, q_count):
    masks = sweep_masks(q_count)

    def around(ref, x):
        return ref[layer_rows(x - 1), :], ref[layer_rows(x), :], ref[layer_rows(x + 1), :]

    def first(x, carry):
        middle[layer_rows(x), :] = sweep(*around(phi, x), kap[layer_rows(x), :], masks)
        return carry

    def second(x, carry):
        put(x, sweep(*around(middle, x), kap[layer_rows(x), :], masks))
        return carry

    lax.fori_loop(1, 15, first, 0)
    for n, x in enumerate((1, 2, 13, 14)):
        edges[layer_rows(n), :] = middle[layer_rows(x), :]
    lax.fori_loop(2, 14, second, 0)


def edge_sweeps(top, bottom, low, high, kap_edge, kap_low, kap_high, middle, q_count):
    masks = sweep_masks(q_count)

    def of(ref, n):
        return ref[LANES * n : LANES * (n + 1), :]

    k = [of(kap_edge, n) for n in range(4)]
    far_low, near_low, a, b = of(low, 0), of(low, 1), of(bottom, 0), of(bottom, 1)
    c, d, near_high, far_high = of(top, 0), of(top, 1), of(high, 0), of(high, 1)
    m = [of(middle, n) for n in range(4)]
    before = sweep(far_low, near_low, a, of(kap_low, 0), masks)
    zero = sweep(near_low, a, b, k[0], masks)
    last = sweep(c, d, near_high, k[3], masks)
    after = sweep(d, near_high, far_high, of(kap_high, 0), masks)
    return [
        sweep(before, zero, m[0], k[0], masks),
        sweep(zero, m[0], m[1], k[1], masks),
        sweep(m[2], m[3], last, k[2], masks),
        sweep(m[3], last, after, k[3], masks),
    ]


def prepare(n_blk, cap, tiles, solvent):
    def body(grp, state, occ, col, octant, send, sel, field, phi, up, down, dil):
        e = state.shape[-1]
        quarter = 16 * tiles

        @pl.when(grp[0] != solvent)
        def _():
            filled = occ[...].reshape(1, 1, e)
            dilate(state, filled, dil)
            hits = jnp.where(col[...] == iota((n_blk, e), 0), 1.0, 0.0)
            earlier = jnp.where(iota((e, e), 0) < iota((e, e), 1), 1.0, 0.0).astype(BF16)
            rank = dot(hits.astype(BF16), earlier, ((1,), (0,)))
            rank = jnp.sum(rank * hits, axis=0, keepdims=True).astype(jnp.int32)
            slot = col[...] * cap + rank
            chosen = jnp.where(iota((n_blk * cap, e), 0) == slot, 1.0, 0.0).astype(BF16)
            sel[...] = chosen
            send[:, pl.ds(0, 512)] = dot(chosen, dil[...], ((1,), (1,))).astype(BF16)
            o = octant[...]
            block = sum((jnp.where(o >= n * quarter, 1, 0) for n in range(1, 4)))
            spot = o - quarter * block
            tile = jnp.where(iota((LANES, e), 0) == spot, (block + 1).astype(F32), 0.0)
            tile = dot(chosen, tile.astype(BF16), ((1,), (1,)))
            send[:, pl.ds(512, LANES)] = tile.astype(BF16)
            put_faces(state, up, down)
            up[pl.ds(192, 8), :] = jnp.broadcast_to(occ[...], (8, e))
            down[pl.ds(192, 8), :] = jnp.broadcast_to(occ[...], (8, e))

        @pl.when(grp[0] == solvent)
        def _():
            tables = tables_in()
            to_octants(state, phi, 1.0, tables, tiles)
            for i in range(8):
                parts = []
                for ox in range(2):
                    for oy in range(2):
                        p = pressures(phi[pl.ds(LANES * (8 * ox + i) + 64 * oy, 64), :])
                        parts.append(p[:, :quarter])
                field[pl.ds(64 * i, 64), :] = jnp.concatenate(parts, axis=1)

    return body


def rates(tiles):
    def body(mat, kap, edge, up, down, *unused):
        to_octants(mat, kap, 0.5 * SWEEP_STEP, tables_in(), tiles)
        up[pl.ds(0, LANES), :] = kap[layer_rows(15), :]
        down[pl.ds(0, LANES), :] = kap[layer_rows(0), :]
        for n, x in enumerate((0, 1, 14, 15)):
            edge[layer_rows(n), :] = kap[layer_rows(x), :]

    return body


def gather_field(quarter):
    def body(recv, field, out):
        hot = one_hot(recv[:, pl.ds(512, LANES)].astype(F32), quarter)
        out[...] = dot(hot, field[...], ((1,), (1,))).astype(BF16)

    return body


def elastic_forces(state, mat, occ, out, *scratch):
    elastic(state, mat, occ[...].reshape(1, 1, occ.shape[-1]), out, *scratch)


def turn(state, mat, occ, out, *scratch):
    elastic_forces(state, mat, occ, out, *scratch[-2:])


def first_step(state, mat, occ, base, sel, recv, low, high, out, send, up, down, _, *scratch):
    filled = occ[...].reshape(1, 1, occ.shape[-1])
    fills = (low[pl.ds(192, 1), :], high[pl.ds(192, 1), :])
    advance(state, mat, filled, base, recv, sel, low, high, fills, out, *scratch[:3])
    dil = scratch[3]
    dilate(out, filled, dil)
    send[...] = dot(sel[...], dil[...], ((1,), (1,))).astype(BF16)
    put_faces(out, up, down)


def last_step(state, mat, occ, base, sel, recv, low, high, fill_low, fill_high, out, *scratch):
    filled = occ[...].reshape(1, 1, occ.shape[-1])
    fills = (fill_low[pl.ds(192, 1), :], fill_high[pl.ds(192, 1), :])
    advance(state, mat, filled, base, recv, sel, low, high, fills, out, *scratch)


def deposit(edged):
    def body(phi, *refs):
        if edged:
            edge, v0, v1, v2, tile, out, up, down = refs
        else:
            v0, v1, v2, out, up, down, tile, _ = refs
        total = None
        for n, v in enumerate((v0, v1, v2)):
            spot = pl.ds(n * v.shape[0], v.shape[0])
            if not edged:
                tile[spot, :] = v[:, pl.ds(512, LANES)]
            hot = one_hot(tile[spot, :].astype(F32), LANES)
            part = dot(v[:, pl.ds(0, 512)], hot, ((0,), (0,)))
            total = part if total is None else total + part
        for x in range(16):
            i, ox = x % 8, x // 8
            if edged and x in (0, 1, 14, 15):
                layer = edge[layer_rows((0, 1, 14, 15).index(x)), :]
            else:
                layer = phi[layer_rows(x), :]
            added = jnp.concatenate(
                [
                    total[64 * i : 64 * i + 64, 256 * ox + LANES * o : 256 * ox + LANES * (o + 1)]
                    for o in range(2)
                ],
                axis=0,
            )
            layer = layer + (SWEEP_STEP * SOURCE_RATE) * added
            out[layer_rows(x), :] = layer
            if x < 2:
                down[layer_rows(x), :] = layer
            if x >= 14:
                up[layer_rows(x - 14), :] = layer

    return body


def inner_first(q_count):
    def body(phi, kap, out, edges, middle):
        def put(x, layer):
            out[layer_rows(x), :] = layer

        inner_sweeps(phi, kap, middle, edges, put, q_count)

    return body


def outer_first(q_count):
    def body(up, down, low, high, kap_edge, kap_low, kap_high, mid, phi, tile, edge, s0, s1, s2, field):
        final = edge_sweeps(up, down, low, high, kap_edge, kap_low, kap_high, mid, q_count)
        for n in range(4):
            edge[layer_rows(n), :] = final[n]
        for x in range(16):
            i, ox = x % 8, x // 8
            layer = final[(0, 1, 14, 15).index(x)] if x in (0, 1, 14, 15) else phi[layer_rows(x), :]
            p = pressures(layer)
            for o in range(2):
                field[pl.ds(64 * i, 64), pl.ds(256 * ox + LANES * o, LANES)] = p[64 * o : 64 * o + 64]
        for n, s in enumerate((s0, s1, s2)):
            spot = pl.ds(n * s.shape[0], s.shape[0])
            hot = one_hot(tile[spot, :].astype(F32), LANES)
            s[...] = dot(hot, field[...], ((1,), (1,))).astype(BF16)

    return body


def inner_last(q_count, tiles):
    def body(phi, kap, out, edges, middle):
        tables = tables_out()
        rows = 16 * tiles

        def put(x, layer):
            spot = pl.ds(pl.multiple_of(x * rows, 8), rows)
            out[spot, :] = layer_from_octants(layer, tables, tiles)

        inner_sweeps(phi, kap, middle, edges, put, q_count)

    return body


def outer_last(q_count, tiles):
    def body(up, down, low, high, kap_edge, kap_low, kap_high, mid, _, out, ends, sem):
        final = edge_sweeps(up, down, low, high, kap_edge, kap_low, kap_high, mid, q_count)
        tables = tables_out()
        rows = 16 * tiles
        for n in range(4):
            ends[pl.ds(rows * n, rows), :] = layer_from_octants(final[n], tables, tiles)
        copies = [
            pltpu.make_async_copy(
                ends.at[pl.ds(2 * rows * n, 2 * rows)], out.at[pl.ds(start, 2 * rows)], sem.at[n]
            )
            for n, start in enumerate((0, 14 * rows))
        ]
        for copy in copies:
            copy.start()
        for copy in copies:
            copy.wait()

    return body


def shards(state, material, occupied, brick_column, brick_octant):
    e = state.shape[-1]
    n_blk, n_grp = lax.axis_size("blk"), lax.axis_size("grp")
    solvent, groups = n_grp - 1, range(n_grp - 1)
    cap = max(2, 2 * e // n_blk)
    slots = n_blk * cap
    tiles = 6 * e // LANES
    q_count = 6 * e // 8
    axes = ("grp", "blk")
    grp = lax.axis_index("grp").astype(jnp.int32)
    grp_at = grp.reshape(1)
    current = state.reshape(1536, e)
    mat = material.reshape(1536, e)
    occ = occupied.astype(F32).reshape(1, e)
    col = brick_column.reshape(1, e)
    octant = brick_octant.reshape(1, e)
    layers, ends, halo = shape_of((2048, LANES)), shape_of((512, LANES)), shape_of((256, LANES))
    rows, flat = shape_of((slots, 512), BF16), shape_of((1536, e))
    face, side = shape_of((256, e)), shape_of((200, e))
    tile = shape_of((slots * (n_grp - 1), LANES), BF16)

    def pairs(back, g):
        forth = [(g * n_blk + b, solvent * n_blk + b) for b in range(n_blk)]
        return [(j, i) for i, j in forth] if back else forth

    def planes(up, which):
        steps = [(b, b + 1) for b in range(n_blk - 1)]
        steps = steps if up else [(j, i) for i, j in steps]
        return [(g * n_blk + i, g * n_blk + j) for g in which for i, j in steps]

    def both_ways(up, down, which):
        return (
            lax.ppermute(up, axes, planes(True, which)),
            lax.ppermute(down, axes, planes(False, which)),
        )

    def swap(block):
        return lax.all_to_all(block, "blk", split_axis=0, concat_axis=0, tiled=True)

    send, sel, field, phi, up, down = call(
        prepare(n_blk, cap, tiles, solvent),
        (grp_at, current, occ, col, octant),
        (
            shape_of((slots, 512 + LANES), BF16),
            shape_of((slots, e), BF16),
            shape_of((512, 4 * q_count), BF16),
            layers,
            side,
            side,
        ),
        [pltpu.VMEM((512, e), BF16)],
        smem=1,
        name="prepare",
    )
    recv = swap(send)
    fields = [lax.ppermute(field, axes, pairs(True, g)) for g in groups]
    arrived = [lax.ppermute(recv, axes, pairs(False, g)) for g in groups]
    work = [pltpu.VMEM((512, e), F32), pltpu.VMEM((1536, e), F32), pltpu.VMEM((1536, e), F32)]
    middle = pltpu.VMEM(layers.shape, F32)

    def solvent_rates():
        kap, edge, up, down, *spare = call(
            rates(tiles),
            (mat,),
            (layers, ends, side, side, rows, face, face),
            unused=(4, 5, 6),
            name="rates",
        )
        return kap, edge, *both_ways(up, down, [solvent]), *spare

    def gathered(g):
        def run():
            return call(gather_field(q_count), (recv, fields[g]), (rows,), name="gather")[0]

        return run

    def mech_first():
        mine = swap(lax.switch(grp, [gathered(g) for g in groups]))
        low, high = both_ways(up, down, groups)
        (base,) = call(elastic_forces, (current, mat, occ), (flat,), work[1:], name="elastic")
        moved, send, fore, back, spare = call(
            first_step,
            (current, mat, occ, base, sel, mine, low, high),
            (shape_of((2048, e)), rows, face, face, ends),
            work + [pltpu.VMEM((512, e), BF16)],
            unused=(4,),
            name="first_step",
        )
        return moved, spare, low, high, send, fore, back

    is_solvent = grp == solvent
    moved, kap_edge, side_low, side_high, send, fore, aft = lax.cond(
        is_solvent, solvent_rates, mech_first
    )

    def solvent_first():
        added, top, bottom, hot, spare = call(
            deposit(False),
            (phi, *arrived),
            (layers, halo, halo, tile, flat),
            unused=(4,),
            name="deposit_first",
        )
        low, high = both_ways(top, bottom, [solvent])
        inner, mid = call(
            inner_first(q_count), (added, moved), (layers, ends), [middle], name="inner_first"
        )
        edge, s0, s1, s2 = call(
            outer_first(q_count),
            (top, bottom, low, high, kap_edge, side_low, side_high, mid, inner, hot),
            (ends, rows, rows, rows),
            [pltpu.VMEM((512, 4 * LANES), BF16)],
            name="outer_first",
        )
        return inner, edge, hot, spare, low, high, s0, s1, s2

    def mech_turn(g):
        def run():
            mine = swap(send)
            low, high = both_ways(fore, aft, [g])
            base, *spare = call(
                turn,
                (moved, mat, occ),
                (flat, layers, ends, tile, rows, rows),
                work[1:],
                unused=range(1, 6),
                name="elastic",
            )
            blocks = list(spare[3:])
            blocks.insert(g, mine)
            return *spare[:3], base, low, high, *blocks

        return run

    turns = [mech_turn(g) for g in groups] + [solvent_first]
    inner, edge, hot, base, face_low, face_high, *blocks = lax.switch(grp, turns)
    back = [
        lax.ppermute(block, axes, pairs(False, g) + pairs(True, g))
        for g, block in zip(groups, blocks)
    ]

    def solvent_last():
        added, top, bottom = call(
            deposit(True),
            (inner, edge, *back, hot),
            (layers, halo, halo),
            name="deposit_last",
        )
        low, high = both_ways(top, bottom, [solvent])
        out, mid = call(
            inner_last(q_count, tiles), (added, moved), (flat, ends), [middle], name="inner_last"
        )
        (out,) = call(
            outer_last(q_count, tiles),
            (top, bottom, low, high, kap_edge, side_low, side_high, mid, out),
            (flat,),
            [pltpu.VMEM((4 * 16 * tiles, LANES), F32), pltpu.SemaphoreType.DMA((2,))],
            away=(8,),
            unused=(0,),
            alias={8: 0},
            name="outer_last",
        )
        return out

    def swapped(g):
        return lambda: swap(back[g])

    def mech_last():
        mine = lax.switch(grp, [swapped(g) for g in groups])
        (out,) = call(
            last_step,
            (moved, mat, occ, base, sel, mine, face_low, face_high, side_low, side_high),
            (flat,),
            work,
            name="last_step",
        )
        return out

    return lax.cond(is_solvent, solvent_last, mech_last).reshape(state.shape)


def solution(mesh):
    in_specs = (
        P("grp", None, None, "blk"),
        P("grp", None, None, "blk"),
        P(("grp", "blk")),
        P(("grp", "blk"), None),
        P(("grp", "blk")),
    )
    out_specs = P("grp", None, None, "blk")
    return jax.shard_map(shards, mesh=mesh, in_specs=in_specs, out_specs=out_specs, check_vma=False)
```

```python
import jax
import jax.numpy as jnp
from jax import lax
from jax.experimental import pallas as pl
from jax.experimental.pallas import tpu as pltpu
from jax.sharding import PartitionSpec as P


UNIT_LENGTH = 0.02
TIME_STEP = 0.1
PENALTY = 1.0
PRESSURE_SCALE = 0.05
DILATION_SCALE = 50.0
SWEEP_STEP = 0.03
SOURCE_RATE = 2.0
CUBIC_TERM = 0.3

LANES = 128
VMEM_LIMIT = 24 << 20
F32, BF16 = jnp.float32, jnp.bfloat16
VMEM = pl.BlockSpec(memory_space=pltpu.VMEM)
SMEM = pl.BlockSpec(memory_space=pltpu.SMEM)
ANY = pl.BlockSpec(memory_space=pl.ANY)


def shape_of(shape, dtype=F32):
    return jax.ShapeDtypeStruct(shape, dtype)


def call(body, args, outs, scratch=(), smem=0, away=(), unused=(), alias=None):
    specs = [SMEM] * smem + [VMEM] * (len(args) - smem)
    return pl.pallas_call(
        body,
        out_shape=outs,
        in_specs=[ANY if n in away else spec for n, spec in enumerate(specs)],
        out_specs=tuple(ANY if n in unused else VMEM for n in range(len(outs))),
        scratch_shapes=list(scratch),
        input_output_aliases=alias or {},
        compiler_params=pltpu.CompilerParams(vmem_limit_bytes=VMEM_LIMIT),
    )(*args)


def iota(shape, dim):
    return lax.broadcasted_iota(jnp.int32, shape, dim)


def dot(a, b, dims):
    return lax.dot_general(a, b, (dims, ((), ())), preferred_element_type=F32)


def diff_i(below, here, above):
    if below is None:
        return above - here
    if above is None:
        return here - below
    return 0.5 * (above - below)


def diff_j(x):
    return jnp.concatenate([x[1:2] - x[0:1], 0.5 * (x[2:] - x[:-2]), x[7:8] - x[6:7]], axis=0)


def diff_k(x):
    k = iota(x.shape, 1)
    upper = jnp.where(k == 7, x, pltpu.roll(x, 7, 1))
    lower = jnp.where(k == 0, x, pltpu.roll(x, 1, 1))
    return jnp.where((k == 0) | (k == 7), 1.0, 0.5) * (upper - lower)


def slab(ref, c, i):
    rows = ref[pl.ds(c * 512 + 64 * i, 64), :]
    return rows.reshape(8, 8, rows.shape[-1])


def put_slab(ref, c, i, value):
    ref[pl.ds(c * 512 + 64 * i, 64), :] = value.reshape(64, value.shape[-1])


def gradients(ref, i):
    grads = []
    for c in range(3):
        here = UNIT_LENGTH * slab(ref, c, i)
        below = UNIT_LENGTH * slab(ref, c, i - 1) if i > 0 else None
        above = UNIT_LENGTH * slab(ref, c, i + 1) if i < 7 else None
        row = [diff_i(below, here, above), diff_j(here), diff_k(here)]
        row[c] = row[c] + 1.0
        grads.append(row)
    return grads


def determinant(grads):
    return (
        grads[0][0] * (grads[1][1] * grads[2][2] - grads[1][2] * grads[2][1])
        - grads[0][1] * (grads[1][0] * grads[2][2] - grads[1][2] * grads[2][0])
        + grads[0][2] * (grads[1][0] * grads[2][1] - grads[1][1] * grads[2][0])
    )


def cofactors(g):
    return [
        [
            g[1][1] * g[2][2] - g[1][2] * g[2][1],
            g[1][2] * g[2][0] - g[1][0] * g[2][2],
            g[1][0] * g[2][1] - g[1][1] * g[2][0],
        ],
        [
            g[0][2] * g[2][1] - g[0][1] * g[2][2],
            g[0][0] * g[2][2] - g[0][2] * g[2][0],
            g[0][1] * g[2][0] - g[0][0] * g[2][1],
        ],
        [
            g[0][1] * g[1][2] - g[0][2] * g[1][1],
            g[0][2] * g[1][0] - g[0][0] * g[1][2],
            g[0][0] * g[1][1] - g[0][1] * g[1][0],
        ],
    ]


def dilate(ref, filled, out):
    for i in range(8):
        change = (determinant(gradients(ref, i)) - 1.0) * filled * DILATION_SCALE
        out[pl.ds(64 * i, 64), :] = change.reshape(64, change.shape[-1]).astype(BF16)


def put_faces(ref, up, down):
    for c in range(3):
        up[pl.ds(64 * c, 64), :] = ref[pl.ds(c * 512 + 448, 64), :]
        down[pl.ds(64 * c, 64), :] = ref[pl.ds(c * 512, 64), :]


def elastic(ref, mat, filled, out, stress, partial):
    e = filled.shape[-1]
    for i in range(8):
        g = gradients(ref, i)
        shear, lame = slab(mat, 0, i), slab(mat, 1, i)
        c = {}
        for a in range(3):
            for b in range(a, 3):
                c[a, b] = g[0][a] * g[0][b] + g[1][a] * g[1][b] + g[2][a] * g[2][b]
        diag = [c[a, a] - 1.0 for a in range(3)]
        volume = lame * (0.5 * (diag[0] + diag[1] + diag[2]))
        s = {}
        for a in range(3):
            s[a, a] = shear * diag[a] + volume
            for b in range(a + 1, 3):
                s[a, b] = s[b, a] = shear * c[a, b]
        for a in range(3):
            first = [g[a][0] * s[0, b] + g[a][1] * s[1, b] + g[a][2] * s[2, b] for b in range(3)]
            put_slab(stress, a, i, first[0])
            put_slab(partial, a, i, diff_j(first[1]) + diff_k(first[2]))
    k = iota((8, 8, e), 1)
    lane = iota((1, 1, e), 2)
    penalty = PENALTY * UNIT_LENGTH
    fill_before = jnp.where(lane == 0, 0.0, pltpu.roll(filled, 1, 2)) * penalty
    fill_after = jnp.where(lane == e - 1, 0.0, pltpu.roll(filled, e - 1, 2)) * penalty
    before_scale = jnp.where(k == 0, fill_before, 0.0)
    after_scale = jnp.where(k == 7, fill_after, 0.0)
    for i in range(8):
        for a in range(3):
            here = slab(ref, a, i)
            force = slab(partial, a, i) + diff_i(
                slab(stress, a, i - 1) if i > 0 else None,
                slab(stress, a, i),
                slab(stress, a, i + 1) if i < 7 else None,
            )
            before = pltpu.roll(pltpu.roll(here, 1, 1), 1, 2)
            after = pltpu.roll(pltpu.roll(here, 7, 1), e - 1, 2)
            force = force + before_scale * (before - here) + after_scale * (after - here)
            put_slab(out, a, i, force)


def advance(ref, mat, filled, base, recv, sel, low, high, fills, out, pressure, stress, partial):
    e = filled.shape[-1]
    pressure[...] = dot(recv[...], sel[...], ((0,), (0,))) * PRESSURE_SCALE
    for i in range(8):
        cof = cofactors(gradients(ref, i))
        p = pressure[pl.ds(64 * i, 64), :].reshape(8, 8, e)
        for a in range(3):
            first = [p * cof[a][b] for b in range(3)]
            put_slab(stress, a, i, first[0])
            put_slab(partial, a, i, slab(base, a, i) - (diff_j(first[1]) + diff_k(first[2])))
    penalty = PENALTY * UNIT_LENGTH
    fill_low, fill_high = fills[0].reshape(1, 1, e), fills[1].reshape(1, 1, e)
    for i in range(8):
        rate = (TIME_STEP / UNIT_LENGTH) * slab(mat, 2, i) * filled
        for a in range(3):
            here = slab(ref, a, i)
            force = slab(partial, a, i) - diff_i(
                slab(stress, a, i - 1) if i > 0 else None,
                slab(stress, a, i),
                slab(stress, a, i + 1) if i < 7 else None,
            )
            if i == 0:
                other = low[pl.ds(64 * a, 64), :].reshape(8, 8, e)
                force = force + penalty * fill_low * (other - here)
            if i == 7:
                other = high[pl.ds(64 * a, 64), :].reshape(8, 8, e)
                force = force + penalty * fill_high * (other - here)
            put_slab(out, a, i, here + rate * force)


def permute_in(x, tables):
    x = jnp.take_along_axis(x, tables[0], axis=1, mode="promise_in_bounds")
    x = jnp.take_along_axis(x, tables[1], axis=0, mode="promise_in_bounds")
    return jnp.take_along_axis(x, tables[2], axis=1, mode="promise_in_bounds")


def tables_in():
    row, lane = iota((8, LANES), 0), iota((8, LANES), 1)
    high, low = lane // 16, lane % 16
    return (8 * low + (high - row + 8) % 8, (high - row + 8) % 8, 16 * ((high + row) % 8) + low)


def tables_out():
    row, lane = iota((8, LANES), 0), iota((8, LANES), 1)
    high, low = lane // 16, lane % 16
    return (
        16 * ((high - row + 8) % 8) + low,
        (high - row + 8) % 8,
        16 * ((lane % 8 + row) % 8) + lane // 8,
    )


def layer_to_octants(chunk, scale, tables, tiles):
    rows = chunk.shape[0]
    lane = iota((8, LANES), 1)
    parts = []
    for y in range(16):
        part = chunk[tiles * y : min(tiles * y + 8, rows)]
        if part.shape[0] < 8:
            pad = jnp.zeros((8 - part.shape[0], LANES), F32)
            part = jnp.concatenate([part, pad], axis=0)
        part = permute_in(part, tables)
        parts.append(jnp.where(lane < 16 * tiles, part, 0.0))
    layer = jnp.concatenate(parts, axis=0)
    return layer * scale if scale != 1.0 else layer


def to_octants(ref, out, scale, tables, tiles):
    rows = 16 * tiles

    def layer(x, carry):
        chunk = ref[pl.ds(pl.multiple_of(x * rows, 8), rows), :]
        out[layer_rows(x), :] = layer_to_octants(chunk, scale, tables, tiles)
        return carry

    lax.fori_loop(0, 16, layer, 0)


def layer_from_octants(layer, tables, tiles):
    return jnp.concatenate(
        [permute_in(layer[8 * y : 8 * y + 8], tables)[:tiles] for y in range(16)], axis=0
    )


def layer_rows(x):
    return pl.ds(pl.multiple_of(x * LANES, LANES), LANES)


def pressures(layer):
    return (layer + CUBIC_TERM * layer * layer * layer).astype(BF16)


def one_hot(tile, width):
    return jnp.concatenate(
        [jnp.where(tile == float(o + 1), 1.0, 0.0).astype(BF16)[:, :width] for o in range(4)],
        axis=1,
    )


def sweep(below, here, above, kap, masks):
    inner, outer, last, first = masks
    halves = [v.reshape(2, 8, 8, LANES) for v in (below, here, above, kap)]
    out = []
    for o in range(2):
        low, c, high, rate = (v[o] for v in halves)
        twin = halves[1][1 - o]
        if o == 0:
            y_above = jnp.concatenate([c[1:], twin[0:1]], axis=0)
            y_below = jnp.concatenate([c[0:1], c[:-1]], axis=0)
        else:
            y_above = jnp.concatenate([c[1:], c[7:8]], axis=0)
            y_below = jnp.concatenate([twin[7:8], c[:-1]], axis=0)
        r = pltpu.roll(c, 7, 1)
        z_above = jnp.where(inner, r, jnp.where(last, c, pltpu.roll(r, LANES - 1, 2)))
        r = pltpu.roll(c, 1, 1)
        z_below = jnp.where(outer, r, jnp.where(first, c, pltpu.roll(r, 1, 2)))
        base = 1.0 + c * c
        inflow = None
        for n in (high, low, y_above, y_below, z_above, z_below):
            part = (base + n * n) * (n - c)
            inflow = part if inflow is None else inflow + part
        out.append((c + rate * inflow).reshape(64, LANES))
    return jnp.concatenate(out, axis=0)


def sweep_masks(q_count):
    k, lane = iota((8, 8, LANES), 1), iota((8, 8, LANES), 2)
    return k < 7, k > 0, lane == q_count - 1, lane == 0


def inner_sweeps(phi, kap, middle, edges, put, q_count):
    masks = sweep_masks(q_count)

    def around(ref, x):
        return ref[layer_rows(x - 1), :], ref[layer_rows(x), :], ref[layer_rows(x + 1), :]

    def first(x, carry):
        middle[layer_rows(x), :] = sweep(*around(phi, x), kap[layer_rows(x), :], masks)
        return carry

    def second(x, carry):
        put(x, sweep(*around(middle, x), kap[layer_rows(x), :], masks))
        return carry

    lax.fori_loop(1, 15, first, 0)
    for n, x in enumerate((1, 2, 13, 14)):
        edges[layer_rows(n), :] = middle[layer_rows(x), :]
    lax.fori_loop(2, 14, second, 0)


def edge_sweeps(top, bottom, low, high, kap_edge, kap_low, kap_high, middle, q_count):
    masks = sweep_masks(q_count)

    def of(ref, n):
        return ref[LANES * n : LANES * (n + 1), :]

    k = [of(kap_edge, n) for n in range(4)]
    far_low, near_low, a, b = of(low, 0), of(low, 1), of(bottom, 0), of(bottom, 1)
    c, d, near_high, far_high = of(top, 0), of(top, 1), of(high, 0), of(high, 1)
    m = [of(middle, n) for n in range(4)]
    before = sweep(far_low, near_low, a, of(kap_low, 2), masks)
    zero = sweep(near_low, a, b, k[0], masks)
    last = sweep(c, d, near_high, k[3], masks)
    after = sweep(d, near_high, far_high, of(kap_high, 2), masks)
    return [
        sweep(before, zero, m[0], k[0], masks),
        sweep(zero, m[0], m[1], k[1], masks),
        sweep(m[2], m[3], last, k[2], masks),
        sweep(m[3], last, after, k[3], masks),
    ]


def prepare(n_blk, cap, tiles, solvent):
    def body(grp, state, occ, col, octant, send, sel, field, phi, up, down, dil):
        e = state.shape[-1]
        quarter = 16 * tiles

        @pl.when(grp[0] != solvent)
        def _():
            filled = occ[...].reshape(1, 1, e)
            dilate(state, filled, dil)
            hits = jnp.where(col[...] == iota((n_blk, e), 0), 1.0, 0.0)
            earlier = jnp.where(iota((e, e), 0) < iota((e, e), 1), 1.0, 0.0).astype(BF16)
            rank = dot(hits.astype(BF16), earlier, ((1,), (0,)))
            rank = jnp.sum(rank * hits, axis=0, keepdims=True).astype(jnp.int32)
            slot = col[...] * cap + rank
            chosen = jnp.where(iota((n_blk * cap, e), 0) == slot, 1.0, 0.0).astype(BF16)
            sel[...] = chosen
            send[:, pl.ds(0, 512)] = dot(chosen, dil[...], ((1,), (1,))).astype(BF16)
            o = octant[...]
            block = sum((jnp.where(o >= n * quarter, 1, 0) for n in range(1, 4)))
            spot = o - quarter * block
            tile = jnp.where(iota((LANES, e), 0) == spot, (block + 1).astype(F32), 0.0)
            tile = dot(chosen, tile.astype(BF16), ((1,), (1,)))
            send[:, pl.ds(512, LANES)] = tile.astype(BF16)
            put_faces(state, up, down)
            up[pl.ds(192, 8), :] = jnp.broadcast_to(occ[...], (8, e))
            down[pl.ds(192, 8), :] = jnp.broadcast_to(occ[...], (8, e))

        @pl.when(grp[0] == solvent)
        def _():
            tables = tables_in()
            to_octants(state, phi, 1.0, tables, tiles)
            for i in range(8):
                parts = []
                for ox in range(2):
                    for oy in range(2):
                        p = pressures(phi[pl.ds(LANES * (8 * ox + i) + 64 * oy, 64), :])
                        parts.append(p[:, :quarter])
                field[pl.ds(64 * i, 64), :] = jnp.concatenate(parts, axis=1)

    return body


def rates(tiles):
    def body(mat, kap, edge):
        to_octants(mat, kap, 0.5 * SWEEP_STEP, tables_in(), tiles)
        for n, x in enumerate((0, 1, 14, 15)):
            edge[layer_rows(n), :] = kap[layer_rows(x), :]

    return body


def gather_field(quarter):
    def body(recv, field, out):
        hot = one_hot(recv[:, pl.ds(512, LANES)].astype(F32), quarter)
        out[...] = dot(hot, field[...], ((1,), (1,))).astype(BF16)

    return body


def elastic_forces(state, mat, occ, out, *scratch):
    elastic(state, mat, occ[...].reshape(1, 1, occ.shape[-1]), out, *scratch[-2:])


def idle(*refs):
    pass


def first_step(state, mat, occ, base, sel, recv, low, high, out, send, up, down, *scratch):
    filled = occ[...].reshape(1, 1, occ.shape[-1])
    fills = (low[pl.ds(192, 1), :], high[pl.ds(192, 1), :])
    advance(state, mat, filled, base, recv, sel, low, high, fills, out, *scratch[:3])
    dil = scratch[3]
    dilate(out, filled, dil)
    send[...] = dot(sel[...], dil[...], ((1,), (1,))).astype(BF16)
    put_faces(out, up, down)


def last_step(state, mat, occ, base, sel, recv, low, high, fill_low, fill_high, out, *scratch):
    filled = occ[...].reshape(1, 1, occ.shape[-1])
    fills = (fill_low[pl.ds(192, 1), :], fill_high[pl.ds(192, 1), :])
    advance(state, mat, filled, base, recv, sel, low, high, fills, out, *scratch)


def deposit(edged):
    def body(phi, *refs):
        if edged:
            edge, v0, v1, v2, tile, out, up, down = refs
        else:
            border, v0, v1, v2, out, up, down, tile, _ = refs
            down[layer_rows(2), :] = border[layer_rows(0), :]
            up[layer_rows(2), :] = border[layer_rows(3), :]
        total = None
        for n, v in enumerate((v0, v1, v2)):
            spot = pl.ds(n * v.shape[0], v.shape[0])
            if not edged:
                tile[spot, :] = v[:, pl.ds(512, LANES)]
            hot = one_hot(tile[spot, :].astype(F32), LANES)
            part = dot(v[:, pl.ds(0, 512)], hot, ((0,), (0,)))
            total = part if total is None else total + part
        for x in range(16):
            i, ox = x % 8, x // 8
            if edged and x in (0, 1, 14, 15):
                layer = edge[layer_rows((0, 1, 14, 15).index(x)), :]
            else:
                layer = phi[layer_rows(x), :]
            added = jnp.concatenate(
                [
                    total[64 * i : 64 * i + 64, 256 * ox + LANES * o : 256 * ox + LANES * (o + 1)]
                    for o in range(2)
                ],
                axis=0,
            )
            layer = layer + (SWEEP_STEP * SOURCE_RATE) * added
            out[layer_rows(x), :] = layer
            if x < 2:
                down[layer_rows(x), :] = layer
            if x >= 14:
                up[layer_rows(x - 14), :] = layer

    return body


def inner_first(q_count):
    def body(phi, kap, out, edges, middle):
        def put(x, layer):
            out[layer_rows(x), :] = layer

        inner_sweeps(phi, kap, middle, edges, put, q_count)

    return body


def outer_first(q_count):
    def body(up, down, low, high, kap_edge, kap_low, kap_high, mid, phi, tile, edge, s0, s1, s2, field):
        final = edge_sweeps(up, down, low, high, kap_edge, kap_low, kap_high, mid, q_count)
        for n in range(4):
            edge[layer_rows(n), :] = final[n]
        for x in range(16):
            i, ox = x % 8, x // 8
            layer = final[(0, 1, 14, 15).index(x)] if x in (0, 1, 14, 15) else phi[layer_rows(x), :]
            p = pressures(layer)
            for o in range(2):
                field[pl.ds(64 * i, 64), pl.ds(256 * ox + LANES * o, LANES)] = p[64 * o : 64 * o + 64]
        for n, s in enumerate((s0, s1, s2)):
            spot = pl.ds(n * s.shape[0], s.shape[0])
            hot = one_hot(tile[spot, :].astype(F32), LANES)
            s[...] = dot(hot, field[...], ((1,), (1,))).astype(BF16)

    return body


def inner_last(q_count, tiles):
    def body(phi, kap, out, edges, middle):
        tables = tables_out()
        rows = 16 * tiles

        def put(x, layer):
            spot = pl.ds(pl.multiple_of(x * rows, 8), rows)
            out[spot, :] = layer_from_octants(layer, tables, tiles)

        inner_sweeps(phi, kap, middle, edges, put, q_count)

    return body


def outer_last(q_count, tiles):
    def body(up, down, low, high, kap_edge, kap_low, kap_high, mid, _, out, ends, sem):
        final = edge_sweeps(up, down, low, high, kap_edge, kap_low, kap_high, mid, q_count)
        tables = tables_out()
        rows = 16 * tiles
        for n in range(4):
            ends[pl.ds(rows * n, rows), :] = layer_from_octants(final[n], tables, tiles)
        copies = [
            pltpu.make_async_copy(
                ends.at[pl.ds(2 * rows * n, 2 * rows)], out.at[pl.ds(start, 2 * rows)], sem.at[n]
            )
            for n, start in enumerate((0, 14 * rows))
        ]
        for copy in copies:
            copy.start()
        for copy in copies:
            copy.wait()

    return body


def shards(state, material, occupied, brick_column, brick_octant):
    e = state.shape[-1]
    n_blk, n_grp = lax.axis_size("blk"), lax.axis_size("grp")
    solvent, groups = n_grp - 1, range(n_grp - 1)
    cap = max(2, 2 * e // n_blk)
    slots = n_blk * cap
    tiles = 6 * e // LANES
    q_count = 6 * e // 8
    axes = ("grp", "blk")
    grp = lax.axis_index("grp").astype(jnp.int32)
    grp_at = grp.reshape(1)
    current = state.reshape(1536, e)
    mat = material.reshape(1536, e)
    occ = occupied.astype(F32).reshape(1, e)
    col = brick_column.reshape(1, e)
    octant = brick_octant.reshape(1, e)
    layers, ends, halo = shape_of((2048, LANES)), shape_of((512, LANES)), shape_of((256, LANES))
    rows, flat = shape_of((slots, 512), BF16), shape_of((1536, e))
    face, side, wide = shape_of((192, e)), shape_of((200, e)), shape_of((384, e))
    tile = shape_of((slots * (n_grp - 1), LANES), BF16)

    def pairs(back, g):
        forth = [(g * n_blk + b, solvent * n_blk + b) for b in range(n_blk)]
        return [(j, i) for i, j in forth] if back else forth

    def planes(up, which):
        steps = [(b, b + 1) for b in range(n_blk - 1)]
        steps = steps if up else [(j, i) for i, j in steps]
        return [(g * n_blk + i, g * n_blk + j) for g in which for i, j in steps]

    def both_ways(up, down, which):
        return (
            lax.ppermute(up, axes, planes(True, which)),
            lax.ppermute(down, axes, planes(False, which)),
        )

    def swap(block):
        return lax.all_to_all(block, "blk", split_axis=0, concat_axis=0, tiled=True)

    send, sel, field, phi, up, down = call(
        prepare(n_blk, cap, tiles, solvent),
        (grp_at, current, occ, col, octant),
        (
            shape_of((slots, 512 + LANES), BF16),
            shape_of((slots, e), BF16),
            shape_of((512, 4 * q_count), BF16),
            layers,
            side,
            side,
        ),
        [pltpu.VMEM((512, e), BF16)],
        smem=1,
    )
    recv = swap(send)
    fields = []
    for g in groups:
        fields.append(lax.ppermute(field, axes, pairs(True, g)))
    side_low, side_high = both_ways(up, down, groups)
    work = [pltpu.VMEM((512, e), F32), pltpu.VMEM((1536, e), F32), pltpu.VMEM((1536, e), F32)]
    middle = pltpu.VMEM(layers.shape, F32)

    def gathered(g):
        def run():
            return call(gather_field(q_count), (recv, fields[g]), (rows,))[0]

        return run

    def nothing(*outs):
        return lambda: call(idle, (), outs, unused=range(len(outs)))

    mine = lax.switch(grp, [gathered(g) for g in groups] + [lambda: nothing(rows)()[0]])
    mine, recv = lax.optimization_barrier((mine, recv))
    mine = swap(mine)
    arrived = []
    for g in groups:
        arrived.append(lax.ppermute(recv, axes, pairs(False, g)))

    def solvent_rates():
        return tuple(call(rates(tiles), (mat,), (layers, ends)))

    def mech_elastic():
        return tuple(
            call(elastic_forces, (current, mat, occ), (layers, ends), work[1:], unused=(1,))
        )

    def mech_first():
        return tuple(
            call(
                first_step,
                (current, mat, occ, base, sel, mine, side_low, side_high),
                (layers, rows, face, face),
                work + [pltpu.VMEM((512, e), BF16)],
            )
        )

    is_solvent = grp == solvent
    base, kap_edge = lax.cond(is_solvent, solvent_rates, mech_elastic)
    kap = base
    idle_first = lambda: tuple(nothing(layers, rows, face, face)())
    moved, send, fore, aft = lax.cond(is_solvent, idle_first, mech_first)

    def solvent_first():
        added, top, bottom, hot, spare = call(
            deposit(False), (phi, kap_edge, *arrived), (layers, wide, wide, tile, flat), unused=(4,)
        )
        low, high = both_ways(top, bottom, [solvent])
        inner, mid = call(inner_first(q_count), (added, kap), (layers, ends), [middle])
        edge, s0, s1, s2 = call(
            outer_first(q_count),
            (top, bottom, low, high, kap_edge, low, high, mid, inner, hot),
            (ends, rows, rows, rows),
            [pltpu.VMEM((512, 4 * LANES), BF16)],
        )
        return inner, edge, hot, spare, low, high, s0, s1, s2

    def mech_turn(g):
        def run():
            mine = swap(send)
            force, *spare = call(
                elastic_forces,
                (moved, mat, occ),
                (flat, layers, ends, tile, wide, wide, rows, rows),
                work[1:],
                unused=range(1, 8),
            )
            blocks = list(spare[5:])
            blocks.insert(g, mine)
            return *spare[:3], force, *spare[3:5], *blocks

        return run

    turns = [mech_turn(g) for g in groups] + [solvent_first]
    inner, edge, hot, force, far_low, far_high, *blocks = lax.switch(grp, turns)
    back = [
        lax.ppermute(block, axes, pairs(False, g) + pairs(True, g))
        for g, block in zip(groups, blocks)
    ]

    def solvent_last():
        added, top, bottom = call(deposit(True), (inner, edge, *back, hot), (layers, halo, halo))
        low, high = both_ways(top, bottom, [solvent])
        out, mid = call(inner_last(q_count, tiles), (added, kap), (flat, ends), [middle])
        (out,) = call(
            outer_last(q_count, tiles),
            (top, bottom, low, high, kap_edge, far_low, far_high, mid, out),
            (flat,),
            [pltpu.VMEM((4 * 16 * tiles, LANES), F32), pltpu.SemaphoreType.DMA((2,))],
            away=(8,),
            unused=(0,),
            alias={8: 0},
        )
        return out

    def swapped(g):
        return lambda: (swap(back[g]), *both_ways(fore, aft, [g]))

    def mech_last():
        mine, low, high = lax.switch(grp, [swapped(g) for g in groups])
        (out,) = call(
            last_step,
            (moved, mat, occ, force, sel, mine, low, high, side_low, side_high),
            (flat,),
            work,
        )
        return out

    return lax.cond(is_solvent, solvent_last, mech_last).reshape(state.shape)


def solution(mesh):
    in_specs = (
        P("grp", None, None, "blk"),
        P("grp", None, None, "blk"),
        P(("grp", "blk")),
        P(("grp", "blk"), None),
        P(("grp", "blk")),
    )
    out_specs = P("grp", None, None, "blk")
    return jax.shard_map(shards, mesh=mesh, in_specs=in_specs, out_specs=out_specs, check_vma=False)
```

```python
import jax
import jax.numpy as jnp
from jax import lax
from jax.experimental import pallas as pl
from jax.experimental.pallas import tpu as pltpu
from jax.sharding import PartitionSpec as P


UNIT_LENGTH = 0.02
TIME_STEP = 0.1
PENALTY = 1.0
PRESSURE_SCALE = 0.05
DILATION_SCALE = 50.0
SWEEP_STEP = 0.03
SOURCE_RATE = 2.0
CUBIC_TERM = 0.3

LANES = 128
VMEM_LIMIT = 24 << 20
F32, BF16 = jnp.float32, jnp.bfloat16
VMEM = pl.BlockSpec(memory_space=pltpu.VMEM)
SMEM = pl.BlockSpec(memory_space=pltpu.SMEM)
ANY = pl.BlockSpec(memory_space=pltpu.HBM)


def shape_of(shape, dtype=F32):
    return jax.ShapeDtypeStruct(shape, dtype)


def call(body, args, outs, scratch=(), smem=0, away=(), unused=(), alias=None):
    specs = [SMEM] * smem + [VMEM] * (len(args) - smem)
    return pl.pallas_call(
        body,
        out_shape=outs,
        in_specs=[ANY if n in away else spec for n, spec in enumerate(specs)],
        out_specs=tuple(ANY if n in unused else VMEM for n in range(len(outs))),
        scratch_shapes=list(scratch),
        input_output_aliases=alias or {},
        compiler_params=pltpu.CompilerParams(vmem_limit_bytes=VMEM_LIMIT),
    )(*args)


def iota(shape, dim):
    return lax.broadcasted_iota(jnp.int32, shape, dim)


def dot(a, b, dims):
    return lax.dot_general(a, b, (dims, ((), ())), preferred_element_type=F32)


def diff_i(below, here, above):
    if below is None:
        return above - here
    if above is None:
        return here - below
    return 0.5 * (above - below)


def diff_j(x):
    return jnp.concatenate([x[1:2] - x[0:1], 0.5 * (x[2:] - x[:-2]), x[7:8] - x[6:7]], axis=0)


def diff_k(x):
    k = iota(x.shape, 1)
    upper = jnp.where(k == 7, x, pltpu.roll(x, 7, 1))
    lower = jnp.where(k == 0, x, pltpu.roll(x, 1, 1))
    return jnp.where((k == 0) | (k == 7), 1.0, 0.5) * (upper - lower)


def slab(ref, c, i):
    rows = ref[pl.ds(c * 512 + 64 * i, 64), :]
    return rows.reshape(8, 8, rows.shape[-1])


def put_slab(ref, c, i, value):
    ref[pl.ds(c * 512 + 64 * i, 64), :] = value.reshape(64, value.shape[-1])


def gradients(ref, i):
    grads = []
    for c in range(3):
        here = UNIT_LENGTH * slab(ref, c, i)
        below = UNIT_LENGTH * slab(ref, c, i - 1) if i > 0 else None
        above = UNIT_LENGTH * slab(ref, c, i + 1) if i < 7 else None
        row = [diff_i(below, here, above), diff_j(here), diff_k(here)]
        row[c] = row[c] + 1.0
        grads.append(row)
    return grads


def determinant(grads):
    return (
        grads[0][0] * (grads[1][1] * grads[2][2] - grads[1][2] * grads[2][1])
        - grads[0][1] * (grads[1][0] * grads[2][2] - grads[1][2] * grads[2][0])
        + grads[0][2] * (grads[1][0] * grads[2][1] - grads[1][1] * grads[2][0])
    )


def cofactors(g):
    return [
        [
            g[1][1] * g[2][2] - g[1][2] * g[2][1],
            g[1][2] * g[2][0] - g[1][0] * g[2][2],
            g[1][0] * g[2][1] - g[1][1] * g[2][0],
        ],
        [
            g[0][2] * g[2][1] - g[0][1] * g[2][2],
            g[0][0] * g[2][2] - g[0][2] * g[2][0],
            g[0][1] * g[2][0] - g[0][0] * g[2][1],
        ],
        [
            g[0][1] * g[1][2] - g[0][2] * g[1][1],
            g[0][2] * g[1][0] - g[0][0] * g[1][2],
            g[0][0] * g[1][1] - g[0][1] * g[1][0],
        ],
    ]


def dilate(ref, filled, out):
    for i in range(8):
        change = (determinant(gradients(ref, i)) - 1.0) * filled * DILATION_SCALE
        out[pl.ds(64 * i, 64), :] = change.reshape(64, change.shape[-1]).astype(BF16)


def put_faces(ref, up, down):
    for c in range(3):
        up[pl.ds(64 * c, 64), :] = ref[pl.ds(c * 512 + 448, 64), :]
        down[pl.ds(64 * c, 64), :] = ref[pl.ds(c * 512, 64), :]


def elastic(ref, mat, filled, out, stress, partial):
    e = filled.shape[-1]
    for i in range(8):
        g = gradients(ref, i)
        shear, lame = slab(mat, 0, i), slab(mat, 1, i)
        c = {}
        for a in range(3):
            for b in range(a, 3):
                c[a, b] = g[0][a] * g[0][b] + g[1][a] * g[1][b] + g[2][a] * g[2][b]
        diag = [c[a, a] - 1.0 for a in range(3)]
        volume = lame * (0.5 * (diag[0] + diag[1] + diag[2]))
        s = {}
        for a in range(3):
            s[a, a] = shear * diag[a] + volume
            for b in range(a + 1, 3):
                s[a, b] = s[b, a] = shear * c[a, b]
        for a in range(3):
            first = [g[a][0] * s[0, b] + g[a][1] * s[1, b] + g[a][2] * s[2, b] for b in range(3)]
            put_slab(stress, a, i, first[0])
            put_slab(partial, a, i, diff_j(first[1]) + diff_k(first[2]))
    k = iota((8, 8, e), 1)
    lane = iota((1, 1, e), 2)
    penalty = PENALTY * UNIT_LENGTH
    fill_before = jnp.where(lane == 0, 0.0, pltpu.roll(filled, 1, 2)) * penalty
    fill_after = jnp.where(lane == e - 1, 0.0, pltpu.roll(filled, e - 1, 2)) * penalty
    before_scale = jnp.where(k == 0, fill_before, 0.0)
    after_scale = jnp.where(k == 7, fill_after, 0.0)
    for i in range(8):
        for a in range(3):
            here = slab(ref, a, i)
            force = slab(partial, a, i) + diff_i(
                slab(stress, a, i - 1) if i > 0 else None,
                slab(stress, a, i),
                slab(stress, a, i + 1) if i < 7 else None,
            )
            before = pltpu.roll(pltpu.roll(here, 1, 1), 1, 2)
            after = pltpu.roll(pltpu.roll(here, 7, 1), e - 1, 2)
            force = force + before_scale * (before - here) + after_scale * (after - here)
            put_slab(out, a, i, force)


def advance(ref, mat, filled, base, recv, sel, low, high, fills, out, pressure, stress, partial):
    e = filled.shape[-1]
    pressure[...] = dot(recv[...], sel[...], ((0,), (0,))) * PRESSURE_SCALE
    for i in range(8):
        cof = cofactors(gradients(ref, i))
        p = pressure[pl.ds(64 * i, 64), :].reshape(8, 8, e)
        for a in range(3):
            first = [p * cof[a][b] for b in range(3)]
            put_slab(stress, a, i, first[0])
            put_slab(partial, a, i, slab(base, a, i) - (diff_j(first[1]) + diff_k(first[2])))
    penalty = PENALTY * UNIT_LENGTH
    fill_low, fill_high = fills[0].reshape(1, 1, e), fills[1].reshape(1, 1, e)
    for i in range(8):
        rate = (TIME_STEP / UNIT_LENGTH) * slab(mat, 2, i) * filled
        for a in range(3):
            here = slab(ref, a, i)
            force = slab(partial, a, i) - diff_i(
                slab(stress, a, i - 1) if i > 0 else None,
                slab(stress, a, i),
                slab(stress, a, i + 1) if i < 7 else None,
            )
            if i == 0:
                other = low[pl.ds(64 * a, 64), :].reshape(8, 8, e)
                force = force + penalty * fill_low * (other - here)
            if i == 7:
                other = high[pl.ds(64 * a, 64), :].reshape(8, 8, e)
                force = force + penalty * fill_high * (other - here)
            put_slab(out, a, i, here + rate * force)


def permute_in(x, tables):
    x = jnp.take_along_axis(x, tables[0], axis=1, mode="promise_in_bounds")
    x = jnp.take_along_axis(x, tables[1], axis=0, mode="promise_in_bounds")
    return jnp.take_along_axis(x, tables[2], axis=1, mode="promise_in_bounds")


def tables_in():
    row, lane = iota((8, LANES), 0), iota((8, LANES), 1)
    high, low = lane // 16, lane % 16
    return (8 * low + (high - row + 8) % 8, (high - row + 8) % 8, 16 * ((high + row) % 8) + low)


def tables_out():
    row, lane = iota((8, LANES), 0), iota((8, LANES), 1)
    high, low = lane // 16, lane % 16
    return (
        16 * ((high - row + 8) % 8) + low,
        (high - row + 8) % 8,
        16 * ((lane % 8 + row) % 8) + lane // 8,
    )


def layer_to_octants(chunk, scale, tables, tiles):
    rows = chunk.shape[0]
    lane = iota((8, LANES), 1)
    parts = []
    for y in range(16):
        part = chunk[tiles * y : min(tiles * y + 8, rows)]
        if part.shape[0] < 8:
            pad = jnp.zeros((8 - part.shape[0], LANES), F32)
            part = jnp.concatenate([part, pad], axis=0)
        part = permute_in(part, tables)
        parts.append(jnp.where(lane < 16 * tiles, part, 0.0))
    layer = jnp.concatenate(parts, axis=0)
    return layer * scale if scale != 1.0 else layer


def to_octants(ref, out, scale, tables, tiles):
    rows = 16 * tiles

    def layer(x, carry):
        chunk = ref[pl.ds(pl.multiple_of(x * rows, 8), rows), :]
        out[layer_rows(x), :] = layer_to_octants(chunk, scale, tables, tiles)
        return carry

    lax.fori_loop(0, 16, layer, 0, unroll=2)


def layer_from_octants(layer, tables, tiles):
    return jnp.concatenate(
        [permute_in(layer[8 * y : 8 * y + 8], tables)[:tiles] for y in range(16)], axis=0
    )


def layer_rows(x):
    return pl.ds(pl.multiple_of(x * LANES, LANES), LANES)


def pressures(layer):
    return (layer + CUBIC_TERM * layer * layer * layer).astype(BF16)


def one_hot(tile, width):
    return jnp.concatenate(
        [jnp.where(tile == float(o + 1), 1.0, 0.0).astype(BF16)[:, :width] for o in range(4)],
        axis=1,
    )


def weight(c):
    return 0.5 + c * c


def flux(c, s, other, other_s):
    return (s + other_s) * (other - c)


def inside(c, s, masks):
    inner, last, outer = masks
    fy = flux(c[:-1], s[:-1], c[1:], s[1:])
    r = pltpu.roll(c, 7, 1)
    up = jnp.where(inner, r, jnp.where(last, c, pltpu.roll(r, LANES - 1, 2)))
    fz = flux(c, s, up, weight(up))
    r = pltpu.roll(fz, 1, 1)
    total = fz - jnp.where(outer, r, pltpu.roll(r, 1, 2))
    return jnp.concatenate([total[:1] + fy[:1], total[1:-1] + (fy[1:] - fy[:-1]), total[-1:] - fy[-1:]], axis=0)


def sweep_masks(q_count):
    k, lane = iota((16, 8, LANES), 1), iota((16, 8, LANES), 2)
    return k < 7, lane >= q_count - 1, k > 0


def load(ref, x):
    return ref[layer_rows(x), :].reshape(16, 8, LANES)


def sweep_range(ref, kap, start, stop, put, weights, fluxes, masks):
    c, s = load(ref, start), None
    before = load(ref, start - 1)
    s = weight(c)
    weights[...] = s
    fluxes[...] = flux(before, weight(before), c, s)

    def step(x, carry):
        c, up = load(ref, x), load(ref, x + 1)
        s, up_s = weights[...], weight(up)
        weights[...] = up_s
        fx = flux(c, s, up, up_s)
        total = (fx - fluxes[...]) + inside(c, s, masks)
        fluxes[...] = fx
        put(x, (c + load(kap, x) * total).reshape(LANES, LANES))
        return carry

    lax.fori_loop(start, stop, step, 0, unroll=2)


def inner_sweeps(phi, kap, middle, edges, put, weights, fluxes, q_count):
    masks = sweep_masks(q_count)

    def keep(x, layer):
        middle[layer_rows(x), :] = layer

    sweep_range(phi, kap, 1, 15, keep, weights, fluxes, masks)
    for n, x in enumerate((1, 2, 13, 14)):
        edges[layer_rows(n), :] = middle[layer_rows(x), :]
    sweep_range(middle, kap, 2, 14, put, weights, fluxes, masks)


def sweep_chain(layers, kaps, masks):
    weights = [weight(c) for c in layers]
    fx = [
        flux(layers[n], weights[n], layers[n + 1], weights[n + 1]) for n in range(len(layers) - 1)
    ]
    return [
        layers[n] + kaps[n - 1] * ((fx[n] - fx[n - 1]) + inside(layers[n], weights[n], masks))
        for n in range(1, len(layers) - 1)
    ]


def edge_sweeps(top, bottom, low, high, kap_edge, kap_low, kap_high, middle, q_count):
    masks = sweep_masks(q_count)
    k = [load(kap_edge, n) for n in range(4)]
    m = [load(middle, n) for n in range(4)]
    first = [load(low, 0), load(low, 1), load(bottom, 0), load(bottom, 1)]
    first = sweep_chain(first, [load(kap_low, 2), k[0]], masks)
    first = sweep_chain([*first, m[0], m[1]], k[:2], masks)
    last = [load(top, 0), load(top, 1), load(high, 0), load(high, 1)]
    last = sweep_chain(last, [k[3], load(kap_high, 2)], masks)
    last = sweep_chain([m[2], m[3], *last], k[2:], masks)
    return [layer.reshape(LANES, LANES) for layer in first + last]


def prepare(n_blk, cap, tiles, solvent):
    def body(grp, state, occ, col, octant, send, sel, filled, field, phi, up, down, *scratch):
        dil, ints, layers, int_sems, sem = scratch
        e = state.shape[-1]
        quarter = 16 * tiles

        @pl.when(grp[0] != solvent)
        def _():
            copies = [
                pltpu.make_async_copy(ref, ints.at[n], int_sems.at[n])
                for n, ref in enumerate((occ, col, octant))
            ]
            for copy in copies:
                copy.start()
            dilate(state, 1.0, dil)
            for copy in copies:
                copy.wait()
            full, column, o = ints[0].astype(F32), ints[1], ints[2]
            hits = jnp.where(column == iota((n_blk, e), 0), 1.0, 0.0)
            earlier = jnp.where(iota((e, e), 0) < iota((e, e), 1), 1.0, 0.0).astype(BF16)
            rank = dot(hits.astype(BF16), earlier, ((1,), (0,)))
            rank = jnp.sum(rank * hits, axis=0, keepdims=True).astype(jnp.int32)
            slot = column * cap + rank
            chosen = jnp.where(iota((n_blk * cap, e), 0) == slot, 1.0, 0.0)
            held = (chosen * full).astype(BF16)
            chosen = chosen.astype(BF16)
            sel[...] = chosen
            send[:, pl.ds(0, 512)] = dot(held, dil[...], ((1,), (1,))).astype(BF16)
            block = sum((jnp.where(o >= n * quarter, 1, 0) for n in range(1, 4)))
            spot = o - quarter * block
            tile = jnp.where(iota((LANES, e), 0) == spot, (block + 1).astype(F32), 0.0)
            tile = dot(chosen, tile.astype(BF16), ((1,), (1,)))
            send[:, pl.ds(512, LANES)] = tile.astype(BF16)
            put_faces(state, up, down)
            filled[...] = jnp.broadcast_to(full, (8, e))
            up[pl.ds(192, 8), :] = jnp.broadcast_to(full, (8, e))
            down[pl.ds(192, 8), :] = jnp.broadcast_to(full, (8, e))

        @pl.when(grp[0] == solvent)
        def _():
            tables = tables_in()
            to_octants(state, layers, 1.0, tables, tiles)
            copy = pltpu.make_async_copy(layers, phi, sem.at[0])
            copy.start()
            for i in range(8):
                parts = []
                for ox in range(2):
                    for oy in range(2):
                        p = pressures(layers[pl.ds(LANES * (8 * ox + i) + 64 * oy, 64), :])
                        parts.append(p[:, :quarter])
                field[pl.ds(64 * i, 64), :] = jnp.concatenate(parts, axis=1)
            copy.wait()

    return body


def rates(tiles):
    def body(mat, kap, edge):
        to_octants(mat, kap, 0.5 * SWEEP_STEP, tables_in(), tiles)
        for n, x in enumerate((0, 1, 14, 15)):
            edge[layer_rows(n), :] = kap[layer_rows(x), :]

    return body


def gather_field(quarter):
    def body(recv, field, out):
        hot = one_hot(recv[:, pl.ds(512, LANES)].astype(F32), quarter)
        out[...] = dot(hot, field[...], ((1,), (1,))).astype(BF16)

    return body


def elastic_forces(state, mat, occ, out, *scratch):
    elastic(state, mat, occ[pl.ds(0, 1), :].reshape(1, 1, occ.shape[-1]), out, *scratch[-2:])


def idle(*refs):
    pass


def first_step(state, mat, occ, base, sel, recv, low, high, out, send, up, down, *scratch):
    filled = occ[pl.ds(0, 1), :].reshape(1, 1, occ.shape[-1])
    fills = (low[pl.ds(192, 1), :], high[pl.ds(192, 1), :])
    advance(state, mat, filled, base, recv, sel, low, high, fills, out, *scratch[:3])
    dil = scratch[3]
    dilate(out, filled, dil)
    send[...] = dot(sel[...], dil[...], ((1,), (1,))).astype(BF16)
    put_faces(out, up, down)


def last_step(state, mat, occ, base, sel, recv, low, high, fill_low, fill_high, out, *scratch):
    filled = occ[pl.ds(0, 1), :].reshape(1, 1, occ.shape[-1])
    fills = (fill_low[pl.ds(192, 1), :], fill_high[pl.ds(192, 1), :])
    advance(state, mat, filled, base, recv, sel, low, high, fills, out, *scratch)


def deposit(edged):
    def body(phi, *refs):
        if edged:
            edge, v0, v1, v2, tile, out, up, down = refs
        else:
            border, v0, v1, v2, out, up, down, tile, _ = refs
            down[layer_rows(2), :] = border[layer_rows(0), :]
            up[layer_rows(2), :] = border[layer_rows(3), :]
        total = None
        for n, v in enumerate((v0, v1, v2)):
            spot = pl.ds(n * v.shape[0], v.shape[0])
            if not edged:
                tile[spot, :] = v[:, pl.ds(512, LANES)]
            hot = one_hot(tile[spot, :].astype(F32), LANES)
            part = dot(v[:, pl.ds(0, 512)], hot, ((0,), (0,)))
            total = part if total is None else total + part
        for x in range(16):
            i, ox = x % 8, x // 8
            if edged and x in (0, 1, 14, 15):
                layer = edge[layer_rows((0, 1, 14, 15).index(x)), :]
            else:
                layer = phi[layer_rows(x), :]
            added = jnp.concatenate(
                [
                    total[64 * i : 64 * i + 64, 256 * ox + LANES * o : 256 * ox + LANES * (o + 1)]
                    for o in range(2)
                ],
                axis=0,
            )
            layer = layer + (SWEEP_STEP * SOURCE_RATE) * added
            out[layer_rows(x), :] = layer
            if x < 2:
                down[layer_rows(x), :] = layer
            if x >= 14:
                up[layer_rows(x - 14), :] = layer

    return body


def inner_first(q_count):
    def body(phi, kap, out, edges, *scratch):
        def put(x, layer):
            out[layer_rows(x), :] = layer

        inner_sweeps(phi, kap, scratch[0], edges, put, *scratch[1:], q_count)

    return body


def outer_first(q_count):
    def body(up, down, low, high, kap_edge, kap_low, kap_high, mid, phi, tile, edge, s0, s1, s2, field):
        final = edge_sweeps(up, down, low, high, kap_edge, kap_low, kap_high, mid, q_count)
        for n in range(4):
            edge[layer_rows(n), :] = final[n]
        for x in range(16):
            i, ox = x % 8, x // 8
            layer = final[(0, 1, 14, 15).index(x)] if x in (0, 1, 14, 15) else phi[layer_rows(x), :]
            p = pressures(layer)
            for o in range(2):
                field[pl.ds(64 * i, 64), pl.ds(256 * ox + LANES * o, LANES)] = p[64 * o : 64 * o + 64]
        for n, s in enumerate((s0, s1, s2)):
            spot = pl.ds(n * s.shape[0], s.shape[0])
            hot = one_hot(tile[spot, :].astype(F32), LANES)
            s[...] = dot(hot, field[...], ((1,), (1,))).astype(BF16)

    return body


def inner_last(q_count, tiles):
    def body(phi, kap, out, edges, *scratch):
        tables = tables_out()
        rows = 16 * tiles

        def put(x, layer):
            spot = pl.ds(pl.multiple_of(x * rows, 8), rows)
            out[spot, :] = layer_from_octants(layer, tables, tiles)

        inner_sweeps(phi, kap, scratch[0], edges, put, *scratch[1:], q_count)

    return body


def outer_last(q_count, tiles):
    def body(up, down, low, high, kap_edge, kap_low, kap_high, mid, _, out, ends, sem):
        final = edge_sweeps(up, down, low, high, kap_edge, kap_low, kap_high, mid, q_count)
        tables = tables_out()
        rows = 16 * tiles
        for n in range(4):
            ends[pl.ds(rows * n, rows), :] = layer_from_octants(final[n], tables, tiles)
        copies = [
            pltpu.make_async_copy(
                ends.at[pl.ds(2 * rows * n, 2 * rows)], out.at[pl.ds(start, 2 * rows)], sem.at[n]
            )
            for n, start in enumerate((0, 14 * rows))
        ]
        for copy in copies:
            copy.start()
        for copy in copies:
            copy.wait()

    return body


def shards(state, material, occupied, brick_column, brick_octant):
    e = state.shape[-1]
    n_blk, n_grp = lax.axis_size("blk"), lax.axis_size("grp")
    solvent, groups = n_grp - 1, range(n_grp - 1)
    cap = max(2, 2 * e // n_blk)
    slots = n_blk * cap
    tiles = 6 * e // LANES
    q_count = 6 * e // 8
    axes = ("grp", "blk")
    grp = lax.axis_index("grp").astype(jnp.int32)
    grp_at = grp.reshape(1)
    current = state.reshape(1536, e)
    mat = material.reshape(1536, e)
    col = brick_column.reshape(1, e)
    octant = brick_octant.reshape(1, e)
    layers, ends, halo = shape_of((2048, LANES)), shape_of((512, LANES)), shape_of((256, LANES))
    rows, flat = shape_of((slots, 512), BF16), shape_of((1536, e))
    face, side, wide = shape_of((192, e)), shape_of((200, e)), shape_of((384, e))
    tile = shape_of((slots * (n_grp - 1), LANES), BF16)

    def pairs(back, g):
        forth = [(g * n_blk + b, solvent * n_blk + b) for b in range(n_blk)]
        return [(j, i) for i, j in forth] if back else forth

    def planes(up, which):
        steps = [(b, b + 1) for b in range(n_blk - 1)]
        steps = steps if up else [(j, i) for i, j in steps]
        return [(g * n_blk + i, g * n_blk + j) for g in which for i, j in steps]

    def both_ways(up, down, which):
        return (
            lax.ppermute(up, axes, planes(True, which)),
            lax.ppermute(down, axes, planes(False, which)),
        )

    def swap(block):
        return lax.all_to_all(block, "blk", split_axis=0, concat_axis=0, tiled=True)

    send, sel, occ, field, phi, up, down = call(
        prepare(n_blk, cap, tiles, solvent),
        (grp_at, current, occupied.reshape(1, e), col, octant),
        (
            shape_of((slots, 512 + LANES), BF16),
            shape_of((slots, e), BF16),
            shape_of((8, e)),
            shape_of((512, 4 * q_count), BF16),
            layers,
            side,
            side,
        ),
        [
            pltpu.VMEM((512, e), BF16),
            pltpu.VMEM((3, 1, e), jnp.int32),
            pltpu.VMEM(layers.shape, F32),
            pltpu.SemaphoreType.DMA((3,)),
            pltpu.SemaphoreType.DMA((1,)),
        ],
        smem=1,
        away=(2, 3, 4),
        unused=(4,),
    )
    recv = swap(send)
    fields = []
    for g in groups:
        fields.append(lax.ppermute(field, axes, pairs(True, g)))
    side_low, side_high = both_ways(up, down, groups)
    work = [pltpu.VMEM((512, e), F32), pltpu.VMEM((1536, e), F32), pltpu.VMEM((1536, e), F32)]
    sweeping = [pltpu.VMEM(layers.shape, F32)] + [pltpu.VMEM((16, 8, LANES), F32)] * 2

    def gathered(g):
        def run():
            return call(gather_field(q_count), (recv, fields[g]), (rows,))[0]

        return run

    def nothing(*outs):
        return lambda: call(idle, (), outs, unused=range(len(outs)))

    mine = lax.switch(grp, [gathered(g) for g in groups] + [lambda: nothing(rows)()[0]])
    mine, recv = lax.optimization_barrier((mine, recv))
    mine = swap(mine)
    arrived = []
    for g in groups:
        arrived.append(lax.ppermute(recv, axes, pairs(False, g)))

    def solvent_rates():
        return tuple(call(rates(tiles), (mat,), (layers, ends)))

    def mech_elastic():
        return tuple(
            call(elastic_forces, (current, mat, occ), (layers, ends), work[1:], unused=(1,))
        )

    def mech_first():
        return tuple(
            call(
                first_step,
                (current, mat, occ, base, sel, mine, side_low, side_high),
                (layers, rows, face, face),
                work + [pltpu.VMEM((512, e), BF16)],
            )
        )

    is_solvent = grp == solvent
    base, kap_edge = lax.cond(is_solvent, solvent_rates, mech_elastic)
    kap = base
    idle_first = lambda: tuple(nothing(layers, rows, face, face)())
    moved, send, fore, aft = lax.cond(is_solvent, idle_first, mech_first)

    def solvent_first():
        added, top, bottom, hot, spare = call(
            deposit(False), (phi, kap_edge, *arrived), (layers, wide, wide, tile, flat), unused=(4,)
        )
        low, high = both_ways(top, bottom, [solvent])
        inner, mid = call(inner_first(q_count), (added, kap), (layers, ends), sweeping)
        edge, s0, s1, s2 = call(
            outer_first(q_count),
            (top, bottom, low, high, kap_edge, low, high, mid, inner, hot),
            (ends, rows, rows, rows),
            [pltpu.VMEM((512, 4 * LANES), BF16)],
        )
        return inner, edge, hot, spare, low, high, s0, s1, s2

    def mech_turn(g):
        def run():
            mine = swap(send)
            force, *spare = call(
                elastic_forces,
                (moved, mat, occ),
                (flat, layers, ends, tile, wide, wide, rows, rows),
                work[1:],
                unused=range(1, 8),
            )
            blocks = list(spare[5:])
            blocks.insert(g, mine)
            return *spare[:3], force, *spare[3:5], *blocks

        return run

    turns = [mech_turn(g) for g in groups] + [solvent_first]
    inner, edge, hot, force, far_low, far_high, *blocks = lax.switch(grp, turns)
    back = [
        lax.ppermute(block, axes, pairs(False, g) + pairs(True, g))
        for g, block in zip(groups, blocks)
    ]

    def solvent_last():
        added, top, bottom = call(deposit(True), (inner, edge, *back, hot), (layers, halo, halo))
        low, high = both_ways(top, bottom, [solvent])
        out, mid = call(inner_last(q_count, tiles), (added, kap), (flat, ends), sweeping)
        (out,) = call(
            outer_last(q_count, tiles),
            (top, bottom, low, high, kap_edge, far_low, far_high, mid, out),
            (flat,),
            [pltpu.VMEM((4 * 16 * tiles, LANES), F32), pltpu.SemaphoreType.DMA((2,))],
            away=(8,),
            unused=(0,),
            alias={8: 0},
        )
        return out

    def swapped(g):
        return lambda: (swap(back[g]), *both_ways(fore, aft, [g]))

    def mech_last():
        mine, low, high = lax.switch(grp, [swapped(g) for g in groups])
        (out,) = call(
            last_step,
            (moved, mat, occ, force, sel, mine, low, high, side_low, side_high),
            (flat,),
            work,
        )
        return out

    return lax.cond(is_solvent, solvent_last, mech_last).reshape(state.shape)


def solution(mesh):
    in_specs = (
        P("grp", None, None, "blk"),
        P("grp", None, None, "blk"),
        P(("grp", "blk")),
        P(("grp", "blk"), None),
        P(("grp", "blk")),
    )
    out_specs = P("grp", None, None, "blk")
    return jax.shard_map(shards, mesh=mesh, in_specs=in_specs, out_specs=out_specs, check_vma=False)
```

```python
import jax
import jax.numpy as jnp
from jax import lax
from jax.experimental import pallas as pl
from jax.experimental.pallas import tpu as pltpu
from jax.sharding import PartitionSpec as P


UNIT_LENGTH = 0.02
TIME_STEP = 0.1
PENALTY = 1.0
PRESSURE_SCALE = 0.05
DILATION_SCALE = 50.0
SWEEP_STEP = 0.03
SOURCE_RATE = 2.0
CUBIC_TERM = 0.3

LANES = 128
VMEM_LIMIT = 24 << 20
F32, BF16 = jnp.float32, jnp.bfloat16
VMEM = pl.BlockSpec(memory_space=pltpu.VMEM)
SMEM = pl.BlockSpec(memory_space=pltpu.SMEM)
ANY = pl.BlockSpec(memory_space=pltpu.HBM)


def shape_of(shape, dtype=F32):
    return jax.ShapeDtypeStruct(shape, dtype)


def call(body, args, outs, scratch=(), smem=0, away=(), unused=(), alias=None):
    specs = [SMEM] * smem + [VMEM] * (len(args) - smem)
    return pl.pallas_call(
        body,
        out_shape=outs,
        in_specs=[ANY if n in away else spec for n, spec in enumerate(specs)],
        out_specs=tuple(ANY if n in unused else VMEM for n in range(len(outs))),
        scratch_shapes=list(scratch),
        input_output_aliases=alias or {},
        compiler_params=pltpu.CompilerParams(vmem_limit_bytes=VMEM_LIMIT),
    )(*args)


def iota(shape, dim):
    return lax.broadcasted_iota(jnp.int32, shape, dim)


def dot(a, b, dims):
    return lax.dot_general(a, b, (dims, ((), ())), preferred_element_type=F32)


def diff_i(below, here, above):
    if below is None:
        return above - here
    if above is None:
        return here - below
    return 0.5 * (above - below)


def diff_j(x):
    return jnp.concatenate([x[1:2] - x[0:1], 0.5 * (x[2:] - x[:-2]), x[7:8] - x[6:7]], axis=0)


def diff_k(x):
    k = iota(x.shape, 1)
    upper = jnp.where(k == 7, x, pltpu.roll(x, 7, 1))
    lower = jnp.where(k == 0, x, pltpu.roll(x, 1, 1))
    return jnp.where((k == 0) | (k == 7), 1.0, 0.5) * (upper - lower)


def slab(ref, c, i):
    rows = ref[c, pl.ds(64 * i, 64), :] if len(ref.shape) == 3 else ref[pl.ds(c * 512 + 64 * i, 64), :]
    return rows.reshape(8, 8, rows.shape[-1])


def put_slab(ref, c, i, value):
    value = value.reshape(64, value.shape[-1])
    if len(ref.shape) == 3:
        ref[c, pl.ds(64 * i, 64), :] = value
    else:
        ref[pl.ds(c * 512 + 64 * i, 64), :] = value


def gradients(ref, i):
    grads = []
    for c in range(3):
        here = UNIT_LENGTH * slab(ref, c, i)
        below = UNIT_LENGTH * slab(ref, c, i - 1) if i > 0 else None
        above = UNIT_LENGTH * slab(ref, c, i + 1) if i < 7 else None
        row = [diff_i(below, here, above), diff_j(here), diff_k(here)]
        row[c] = row[c] + 1.0
        grads.append(row)
    return grads


def determinant(grads):
    return (
        grads[0][0] * (grads[1][1] * grads[2][2] - grads[1][2] * grads[2][1])
        - grads[0][1] * (grads[1][0] * grads[2][2] - grads[1][2] * grads[2][0])
        + grads[0][2] * (grads[1][0] * grads[2][1] - grads[1][1] * grads[2][0])
    )


def cofactors(g):
    return [
        [
            g[1][1] * g[2][2] - g[1][2] * g[2][1],
            g[1][2] * g[2][0] - g[1][0] * g[2][2],
            g[1][0] * g[2][1] - g[1][1] * g[2][0],
        ],
        [
            g[0][2] * g[2][1] - g[0][1] * g[2][2],
            g[0][0] * g[2][2] - g[0][2] * g[2][0],
            g[0][1] * g[2][0] - g[0][0] * g[2][1],
        ],
        [
            g[0][1] * g[1][2] - g[0][2] * g[1][1],
            g[0][2] * g[1][0] - g[0][0] * g[1][2],
            g[0][0] * g[1][1] - g[0][1] * g[1][0],
        ],
    ]


def dilate(ref, filled, out):
    for i in range(8):
        change = (determinant(gradients(ref, i)) - 1.0) * filled * DILATION_SCALE
        out[pl.ds(64 * i, 64), :] = change.reshape(64, change.shape[-1]).astype(BF16)


def put_faces(ref, up, down):
    for c in range(3):
        up[pl.ds(64 * c, 64), :] = slab(ref, c, 7).reshape(64, ref.shape[-1])
        down[pl.ds(64 * c, 64), :] = slab(ref, c, 0).reshape(64, ref.shape[-1])


def elastic(ref, mat, filled, out, stress, partial):
    e = filled.shape[-1]
    for i in range(8):
        g = gradients(ref, i)
        shear, lame = slab(mat, 0, i), slab(mat, 1, i)
        c = {}
        for a in range(3):
            for b in range(a, 3):
                c[a, b] = g[0][a] * g[0][b] + g[1][a] * g[1][b] + g[2][a] * g[2][b]
        diag = [c[a, a] - 1.0 for a in range(3)]
        volume = lame * (0.5 * (diag[0] + diag[1] + diag[2]))
        s = {}
        for a in range(3):
            s[a, a] = shear * diag[a] + volume
            for b in range(a + 1, 3):
                s[a, b] = s[b, a] = shear * c[a, b]
        for a in range(3):
            first = [g[a][0] * s[0, b] + g[a][1] * s[1, b] + g[a][2] * s[2, b] for b in range(3)]
            put_slab(stress, a, i, first[0])
            put_slab(partial, a, i, diff_j(first[1]) + diff_k(first[2]))
    k = iota((8, 8, e), 1)
    lane = iota((1, 1, e), 2)
    penalty = PENALTY * UNIT_LENGTH
    fill_before = jnp.where(lane == 0, 0.0, pltpu.roll(filled, 1, 2)) * penalty
    fill_after = jnp.where(lane == e - 1, 0.0, pltpu.roll(filled, e - 1, 2)) * penalty
    before_scale = jnp.where(k == 0, fill_before, 0.0)
    after_scale = jnp.where(k == 7, fill_after, 0.0)
    for i in range(8):
        for a in range(3):
            here = slab(ref, a, i)
            force = slab(partial, a, i) + diff_i(
                slab(stress, a, i - 1) if i > 0 else None,
                slab(stress, a, i),
                slab(stress, a, i + 1) if i < 7 else None,
            )
            before = pltpu.roll(pltpu.roll(here, 1, 1), 1, 2)
            after = pltpu.roll(pltpu.roll(here, 7, 1), e - 1, 2)
            force = force + before_scale * (before - here) + after_scale * (after - here)
            put_slab(out, a, i, force)


CHUNKS = 4


class Stream:
    def __init__(self, state, base, mat, out, held, forces, mobility, result, sems):
        part = 512 // CHUNKS
        self.state, self.base, self.out, self.mob = [], [], [], []
        for n in range(CHUNKS):
            rows = pl.ds(part * n, part)
            whole = (pl.ds(0, 3), rows)
            copy = pltpu.make_async_copy
            self.state.append(copy(state.at[whole], held.at[whole], sems.at[0, n]))
            self.base.append(copy(base.at[whole], forces.at[whole], sems.at[1, n]))
            self.mob.append(copy(mat.at[2, rows], mobility.at[0, rows], sems.at[2, n]))
            self.out.append(copy(result.at[whole], out.at[whole], sems.at[3, n]))
        for n in range(CHUNKS):
            self.state[n].start()
            self.base[n].start()
        for n in range(CHUNKS):
            self.mob[n].start()


def advance(stream, held, forces, mobility, result, filled, recv, sel, low, high, fills, *scratch):
    pressure, stress, partial = scratch
    e = filled.shape[-1]
    per = 8 // CHUNKS
    pressure[...] = dot(recv[...], sel[...], ((0,), (0,))) * PRESSURE_SCALE
    stream.state[0].wait()
    for i in range(8):
        if i % per == per - 1 and i < 7:
            stream.state[i // per + 1].wait()
        if i % per == 0:
            stream.base[i // per].wait()
        cof = cofactors(gradients(held, i))
        p = pressure[pl.ds(64 * i, 64), :].reshape(8, 8, e)
        for a in range(3):
            first = [p * cof[a][b] for b in range(3)]
            put_slab(stress, a, i, first[0])
            put_slab(partial, a, i, slab(forces, a, i) - (diff_j(first[1]) + diff_k(first[2])))
    penalty = PENALTY * UNIT_LENGTH
    fill_low, fill_high = fills[0].reshape(1, 1, e), fills[1].reshape(1, 1, e)
    for i in range(8):
        if i % per == 0:
            stream.mob[i // per].wait()
        rate = (TIME_STEP / UNIT_LENGTH) * slab(mobility, 0, i) * filled
        for a in range(3):
            here = slab(held, a, i)
            force = slab(partial, a, i) - diff_i(
                slab(stress, a, i - 1) if i > 0 else None,
                slab(stress, a, i),
                slab(stress, a, i + 1) if i < 7 else None,
            )
            if i == 0:
                other = low[pl.ds(64 * a, 64), :].reshape(8, 8, e)
                force = force + penalty * fill_low * (other - here)
            if i == 7:
                other = high[pl.ds(64 * a, 64), :].reshape(8, 8, e)
                force = force + penalty * fill_high * (other - here)
            put_slab(result, a, i, here + rate * force)
        if i % per == per - 1:
            stream.out[i // per].start()


def permute_in(x, tables):
    x = jnp.take_along_axis(x, tables[0], axis=1, mode="promise_in_bounds")
    x = jnp.take_along_axis(x, tables[1], axis=0, mode="promise_in_bounds")
    return jnp.take_along_axis(x, tables[2], axis=1, mode="promise_in_bounds")


def tables_in():
    row, lane = iota((8, LANES), 0), iota((8, LANES), 1)
    high, low = lane // 16, lane % 16
    return (8 * low + (high - row + 8) % 8, (high - row + 8) % 8, 16 * ((high + row) % 8) + low)


def tables_out():
    row, lane = iota((8, LANES), 0), iota((8, LANES), 1)
    high, low = lane // 16, lane % 16
    return (
        16 * ((high - row + 8) % 8) + low,
        (high - row + 8) % 8,
        16 * ((lane % 8 + row) % 8) + lane // 8,
    )


def layer_to_octants(chunk, scale, tables, tiles):
    rows = chunk.shape[0]
    lane = iota((8, LANES), 1)
    parts = []
    for y in range(16):
        part = chunk[tiles * y : min(tiles * y + 8, rows)]
        if part.shape[0] < 8:
            pad = jnp.zeros((8 - part.shape[0], LANES), F32)
            part = jnp.concatenate([part, pad], axis=0)
        part = permute_in(part, tables)
        parts.append(jnp.where(lane < 16 * tiles, part, 0.0))
    layer = jnp.concatenate(parts, axis=0)
    return layer * scale if scale != 1.0 else layer


def to_octants(ref, out, scale, tables, tiles):
    rows = 16 * tiles

    def layer(x, carry):
        chunk = ref[pl.ds(pl.multiple_of(x * rows, 8), rows), :]
        out[layer_rows(x), :] = layer_to_octants(chunk, scale, tables, tiles)
        return carry

    lax.fori_loop(0, 16, layer, 0, unroll=2)


def layer_from_octants(layer, tables, tiles):
    return jnp.concatenate(
        [permute_in(layer[8 * y : 8 * y + 8], tables)[:tiles] for y in range(16)], axis=0
    )


def layer_rows(x):
    return pl.ds(pl.multiple_of(x * LANES, LANES), LANES)


def pressures(layer):
    return (layer + CUBIC_TERM * layer * layer * layer).astype(BF16)


def one_hot(tile, width):
    return jnp.concatenate(
        [jnp.where(tile == float(o + 1), 1.0, 0.0).astype(BF16)[:, :width] for o in range(4)],
        axis=1,
    )


def weight(c):
    return 0.5 + c * c


def flux(c, s, other, other_s):
    return (s + other_s) * (other - c)


def inside(c, s, masks):
    inner, last, outer = masks
    fy = flux(c[:-1], s[:-1], c[1:], s[1:])
    r = pltpu.roll(c, 7, 1)
    up = jnp.where(inner, r, jnp.where(last, c, pltpu.roll(r, LANES - 1, 2)))
    fz = flux(c, s, up, weight(up))
    r = pltpu.roll(fz, 1, 1)
    total = fz - jnp.where(outer, r, pltpu.roll(r, 1, 2))
    return jnp.concatenate([total[:1] + fy[:1], total[1:-1] + (fy[1:] - fy[:-1]), total[-1:] - fy[-1:]], axis=0)


def sweep_masks(q_count):
    k, lane = iota((16, 8, LANES), 1), iota((16, 8, LANES), 2)
    return k < 7, lane >= q_count - 1, k > 0


def load(ref, x):
    return ref[layer_rows(x), :].reshape(16, 8, LANES)


def sweep_range(ref, kap, start, stop, put, weights, fluxes, masks):
    c, s = load(ref, start), None
    before = load(ref, start - 1)
    s = weight(c)
    weights[...] = s
    fluxes[...] = flux(before, weight(before), c, s)

    def step(x, carry):
        c, up = load(ref, x), load(ref, x + 1)
        s, up_s = weights[...], weight(up)
        weights[...] = up_s
        fx = flux(c, s, up, up_s)
        total = (fx - fluxes[...]) + inside(c, s, masks)
        fluxes[...] = fx
        put(x, (c + load(kap, x) * total).reshape(LANES, LANES))
        return carry

    lax.fori_loop(start, stop, step, 0, unroll=2)


def inner_sweeps(phi, kap, middle, edges, put, weights, fluxes, q_count):
    masks = sweep_masks(q_count)

    def keep(x, layer):
        middle[layer_rows(x), :] = layer

    sweep_range(phi, kap, 1, 15, keep, weights, fluxes, masks)
    for n, x in enumerate((1, 2, 13, 14)):
        edges[layer_rows(n), :] = middle[layer_rows(x), :]
    sweep_range(middle, kap, 2, 14, put, weights, fluxes, masks)


def sweep_chain(layers, kaps, masks):
    weights = [weight(c) for c in layers]
    fx = [
        flux(layers[n], weights[n], layers[n + 1], weights[n + 1]) for n in range(len(layers) - 1)
    ]
    return [
        layers[n] + kaps[n - 1] * ((fx[n] - fx[n - 1]) + inside(layers[n], weights[n], masks))
        for n in range(1, len(layers) - 1)
    ]


def edge_sweeps(top, bottom, low, high, kap_edge, kap_low, kap_high, middle, q_count):
    masks = sweep_masks(q_count)
    k = [load(kap_edge, n) for n in range(4)]
    m = [load(middle, n) for n in range(4)]
    first = [load(low, 0), load(low, 1), load(bottom, 0), load(bottom, 1)]
    first = sweep_chain(first, [load(kap_low, 0), k[0]], masks)
    first = sweep_chain([*first, m[0], m[1]], k[:2], masks)
    last = [load(top, 0), load(top, 1), load(high, 0), load(high, 1)]
    last = sweep_chain(last, [k[3], load(kap_high, 0)], masks)
    last = sweep_chain([m[2], m[3], *last], k[2:], masks)
    return [layer.reshape(LANES, LANES) for layer in first + last]


def prepare(n_blk, cap, tiles, solvent):
    def body(grp, state, occ, col, octant, send, sel, filled, field, phi, up, down, *scratch):
        dil, ints, layers, int_sems, sem = scratch
        e = state.shape[-1]
        quarter = 16 * tiles

        @pl.when(grp[0] != solvent)
        def _():
            copies = [
                pltpu.make_async_copy(ref, ints.at[n], int_sems.at[n])
                for n, ref in enumerate((occ, col, octant))
            ]
            for copy in copies:
                copy.start()
            dilate(state, 1.0, dil)
            for copy in copies:
                copy.wait()
            full, column, o = ints[0].astype(F32), ints[1], ints[2]
            hits = jnp.where(column == iota((n_blk, e), 0), 1.0, 0.0)
            earlier = jnp.where(iota((e, e), 0) < iota((e, e), 1), 1.0, 0.0).astype(BF16)
            rank = dot(hits.astype(BF16), earlier, ((1,), (0,)))
            rank = jnp.sum(rank * hits, axis=0, keepdims=True).astype(jnp.int32)
            slot = column * cap + rank
            chosen = jnp.where(iota((n_blk * cap, e), 0) == slot, 1.0, 0.0)
            held = (chosen * full).astype(BF16)
            chosen = chosen.astype(BF16)
            sel[...] = chosen
            send[:, pl.ds(0, 512)] = dot(held, dil[...], ((1,), (1,))).astype(BF16)
            block = sum((jnp.where(o >= n * quarter, 1, 0) for n in range(1, 4)))
            spot = o - quarter * block
            tile = jnp.where(iota((LANES, e), 0) == spot, (block + 1).astype(F32), 0.0)
            tile = dot(chosen, tile.astype(BF16), ((1,), (1,)))
            send[:, pl.ds(512, LANES)] = tile.astype(BF16)
            put_faces(state, up, down)
            filled[...] = jnp.broadcast_to(full, (8, e))
            up[pl.ds(192, 8), :] = jnp.broadcast_to(full, (8, e))
            down[pl.ds(192, 8), :] = jnp.broadcast_to(full, (8, e))

        @pl.when(grp[0] == solvent)
        def _():
            tables = tables_in()
            to_octants(state, layers, 1.0, tables, tiles)
            copy = pltpu.make_async_copy(layers, phi, sem.at[0])
            copy.start()
            for i in range(8):
                parts = []
                for ox in range(2):
                    for oy in range(2):
                        p = pressures(layers[pl.ds(LANES * (8 * ox + i) + 64 * oy, 64), :])
                        parts.append(p[:, :quarter])
                field[pl.ds(64 * i, 64), :] = jnp.concatenate(parts, axis=1)
            copy.wait()

    return body


def rates(tiles):
    def body(mat, kap, edge, up, down):
        to_octants(mat, kap, 0.5 * SWEEP_STEP, tables_in(), tiles)
        up[...] = kap[layer_rows(15), :]
        down[...] = kap[layer_rows(0), :]
        for n, x in enumerate((0, 1, 14, 15)):
            edge[layer_rows(n), :] = kap[layer_rows(x), :]

    return body


def gather_field(quarter):
    def body(recv, field, out):
        hot = one_hot(recv[:, pl.ds(512, LANES)].astype(F32), quarter)
        out[...] = dot(hot, field[...], ((1,), (1,))).astype(BF16)

    return body


def elastic_forces(state, mat, occ, out, *scratch):
    elastic(state, mat, occ[pl.ds(0, 1), :].reshape(1, 1, occ.shape[-1]), out, *scratch[-2:])


def idle(*refs):
    pass


def first_step(state, base, mat, occ, sel, recv, low, high, out, send, up, down, *scratch):
    *work, dil, held, forces, mobility, result, sems = scratch
    stream = Stream(state, base, mat, out, held, forces, mobility, result, sems)
    filled = occ[pl.ds(0, 1), :].reshape(1, 1, occ.shape[-1])
    fills = (low[pl.ds(192, 1), :], high[pl.ds(192, 1), :])
    advance(stream, held, forces, mobility, result, filled, recv, sel, low, high, fills, *work)
    dilate(result, filled, dil)
    send[...] = dot(sel[...], dil[...], ((1,), (1,))).astype(BF16)
    put_faces(result, up, down)
    for copy in stream.out:
        copy.wait()


def last_step(state, base, mat, occ, sel, recv, low, high, fill_low, fill_high, out, *scratch):
    *work, held, forces, mobility, result, sems = scratch
    stream = Stream(state, base, mat, out, held, forces, mobility, result, sems)
    filled = occ[pl.ds(0, 1), :].reshape(1, 1, occ.shape[-1])
    fills = (fill_low[pl.ds(192, 1), :], fill_high[pl.ds(192, 1), :])
    advance(stream, held, forces, mobility, result, filled, recv, sel, low, high, fills, *work)
    for copy in stream.out:
        copy.wait()


def deposit(edged):
    def body(phi, *refs):
        if edged:
            edge, v0, v1, v2, tile, out, up, down = refs
        else:
            v0, v1, v2, out, up, down, tile, *_ = refs
        total = None
        for n, v in enumerate((v0, v1, v2)):
            spot = pl.ds(n * v.shape[0], v.shape[0])
            if not edged:
                tile[spot, :] = v[:, pl.ds(512, LANES)]
            hot = one_hot(tile[spot, :].astype(F32), LANES)
            part = dot(v[:, pl.ds(0, 512)], hot, ((0,), (0,)))
            total = part if total is None else total + part
        for x in range(16):
            i, ox = x % 8, x // 8
            if edged and x in (0, 1, 14, 15):
                layer = edge[layer_rows((0, 1, 14, 15).index(x)), :]
            else:
                layer = phi[layer_rows(x), :]
            added = jnp.concatenate(
                [
                    total[64 * i : 64 * i + 64, 256 * ox + LANES * o : 256 * ox + LANES * (o + 1)]
                    for o in range(2)
                ],
                axis=0,
            )
            layer = layer + (SWEEP_STEP * SOURCE_RATE) * added
            out[layer_rows(x), :] = layer
            if x < 2:
                down[layer_rows(x), :] = layer
            if x >= 14:
                up[layer_rows(x - 14), :] = layer

    return body


def inner_first(q_count):
    def body(phi, kap, out, edges, *scratch):
        def put(x, layer):
            out[layer_rows(x), :] = layer

        inner_sweeps(phi, kap, scratch[0], edges, put, *scratch[1:], q_count)

    return body


def outer_first(q_count):
    def body(up, down, low, high, kap_edge, kap_low, kap_high, mid, phi, tile, edge, s0, s1, s2, field):
        final = edge_sweeps(up, down, low, high, kap_edge, kap_low, kap_high, mid, q_count)
        for n in range(4):
            edge[layer_rows(n), :] = final[n]
        for x in range(16):
            i, ox = x % 8, x // 8
            layer = final[(0, 1, 14, 15).index(x)] if x in (0, 1, 14, 15) else phi[layer_rows(x), :]
            p = pressures(layer)
            for o in range(2):
                field[pl.ds(64 * i, 64), pl.ds(256 * ox + LANES * o, LANES)] = p[64 * o : 64 * o + 64]
        for n, s in enumerate((s0, s1, s2)):
            spot = pl.ds(n * s.shape[0], s.shape[0])
            hot = one_hot(tile[spot, :].astype(F32), LANES)
            s[...] = dot(hot, field[...], ((1,), (1,))).astype(BF16)

    return body


def inner_last(q_count, tiles):
    def body(phi, kap, out, edges, *scratch):
        tables = tables_out()
        rows = 16 * tiles

        def put(x, layer):
            spot = pl.ds(pl.multiple_of(x * rows, 8), rows)
            out[spot, :] = layer_from_octants(layer, tables, tiles)

        inner_sweeps(phi, kap, scratch[0], edges, put, *scratch[1:], q_count)

    return body


def outer_last(q_count, tiles):
    def body(up, down, low, high, kap_edge, kap_low, kap_high, mid, _, out, ends, sem):
        final = edge_sweeps(up, down, low, high, kap_edge, kap_low, kap_high, mid, q_count)
        tables = tables_out()
        rows = 16 * tiles
        for n in range(4):
            ends[pl.ds(rows * n, rows), :] = layer_from_octants(final[n], tables, tiles)
        copies = [
            pltpu.make_async_copy(
                ends.at[pl.ds(2 * rows * n, 2 * rows)], out.at[pl.ds(start, 2 * rows)], sem.at[n]
            )
            for n, start in enumerate((0, 14 * rows))
        ]
        for copy in copies:
            copy.start()
        for copy in copies:
            copy.wait()

    return body


def shards(state, material, occupied, brick_column, brick_octant):
    e = state.shape[-1]
    n_blk, n_grp = lax.axis_size("blk"), lax.axis_size("grp")
    solvent, groups = n_grp - 1, range(n_grp - 1)
    cap = max(2, 2 * e // n_blk)
    slots = n_blk * cap
    tiles = 6 * e // LANES
    q_count = 6 * e // 8
    axes = ("grp", "blk")
    grp = lax.axis_index("grp").astype(jnp.int32)
    grp_at = grp.reshape(1)
    current = state.reshape(1536, e)
    mat = material.reshape(1536, e)
    col = brick_column.reshape(1, e)
    octant = brick_octant.reshape(1, e)
    layers, ends, halo = shape_of((2048, LANES)), shape_of((512, LANES)), shape_of((256, LANES))
    rows, flat = shape_of((slots, 512), BF16), shape_of((1536, e))
    face, side, one = shape_of((192, e)), shape_of((200, e)), shape_of((LANES, LANES))
    tile = shape_of((slots * (n_grp - 1), LANES), BF16)

    def pairs(back, g):
        forth = [(g * n_blk + b, solvent * n_blk + b) for b in range(n_blk)]
        return [(j, i) for i, j in forth] if back else forth

    def planes(up, which):
        steps = [(b, b + 1) for b in range(n_blk - 1)]
        steps = steps if up else [(j, i) for i, j in steps]
        return [(g * n_blk + i, g * n_blk + j) for g in which for i, j in steps]

    def both_ways(up, down, which):
        return (
            lax.ppermute(up, axes, planes(True, which)),
            lax.ppermute(down, axes, planes(False, which)),
        )

    def swap(block):
        return lax.all_to_all(block, "blk", split_axis=0, concat_axis=0, tiled=True)

    send, sel, occ, field, phi, up, down = call(
        prepare(n_blk, cap, tiles, solvent),
        (grp_at, current, occupied.reshape(1, e), col, octant),
        (
            shape_of((slots, 512 + LANES), BF16),
            shape_of((slots, e), BF16),
            shape_of((8, e)),
            shape_of((512, 4 * q_count), BF16),
            layers,
            side,
            side,
        ),
        [
            pltpu.VMEM((512, e), BF16),
            pltpu.VMEM((3, 1, e), jnp.int32),
            pltpu.VMEM(layers.shape, F32),
            pltpu.SemaphoreType.DMA((3,)),
            pltpu.SemaphoreType.DMA((1,)),
        ],
        smem=1,
        away=(2, 3, 4),
        unused=(4,),
    )
    recv = swap(send)
    fields = []
    for g in groups:
        fields.append(lax.ppermute(field, axes, pairs(True, g)))
    side_low, side_high = both_ways(up, down, groups)
    work = [pltpu.VMEM((512, e), F32), pltpu.VMEM((1536, e), F32), pltpu.VMEM((1536, e), F32)]
    streaming = [
        pltpu.VMEM((3, 512, e), F32),
        pltpu.VMEM((3, 512, e), F32),
        pltpu.VMEM((1, 512, e), F32),
        pltpu.VMEM((3, 512, e), F32),
        pltpu.SemaphoreType.DMA((4, CHUNKS)),
    ]
    sweeping = [pltpu.VMEM(layers.shape, F32)] + [pltpu.VMEM((16, 8, LANES), F32)] * 2

    def gathered(g):
        def run():
            return call(gather_field(q_count), (recv, fields[g]), (rows,))[0]

        return run

    def nothing(*outs):
        return lambda: call(idle, (), outs, unused=range(len(outs)))

    mine = lax.switch(grp, [gathered(g) for g in groups] + [lambda: nothing(rows)()[0]])
    mine, recv = lax.optimization_barrier((mine, recv))
    mine = swap(mine)
    arrived = []
    for g in groups:
        arrived.append(lax.ppermute(recv, axes, pairs(False, g)))

    def solvent_rates():
        kap, edge, up, down = call(rates(tiles), (mat,), (layers, ends, one, one))
        return kap, edge, *both_ways(up, down, [solvent])

    def mech_elastic():
        outs = (layers, ends, one, one)
        args = (current, mat, occ)
        return tuple(call(elastic_forces, args, outs, work[1:], unused=(1, 2, 3)))

    def mech_first():
        return tuple(
            call(
                first_step,
                (
                    current.reshape(3, 512, e),
                    base.reshape(4, 512, e),
                    mat.reshape(3, 512, e),
                    occ,
                    sel,
                    mine,
                    side_low,
                    side_high,
                ),
                (shape_of((4, 512, e)), rows, face, face),
                work + [pltpu.VMEM((512, e), BF16)] + streaming,
                away=(0, 1, 2),
                unused=(0,),
            )
        )

    is_solvent = grp == solvent
    base, kap_edge, far_low, far_high = lax.cond(is_solvent, solvent_rates, mech_elastic)
    kap = base
    idle_first = lambda: tuple(nothing(shape_of((4, 512, e)), rows, face, face)())
    moved, send, fore, aft = lax.cond(is_solvent, idle_first, mech_first)

    def solvent_first():
        added, top, bottom, hot, *spare = call(
            deposit(False),
            (phi, *arrived),
            (layers, halo, halo, tile, flat, face, face),
            unused=(4, 5, 6),
        )
        low, high = both_ways(top, bottom, [solvent])
        inner, mid = call(inner_first(q_count), (added, kap), (layers, ends), sweeping)
        edge, s0, s1, s2 = call(
            outer_first(q_count),
            (top, bottom, low, high, kap_edge, far_low, far_high, mid, inner, hot),
            (ends, rows, rows, rows),
            [pltpu.VMEM((512, 4 * LANES), BF16)],
        )
        return inner, edge, hot, *spare, s0, s1, s2

    def mech_turn(g):
        def run():
            mine = swap(send)
            low, high = both_ways(fore, aft, [g])
            force, *spare = call(
                elastic_forces,
                (moved.reshape(2048, e), mat, occ),
                (flat, layers, ends, tile, rows, rows),
                work[1:],
                unused=range(1, 6),
            )
            blocks = list(spare[3:])
            blocks.insert(g, mine)
            return *spare[:3], force, low, high, *blocks

        return run

    turns = [mech_turn(g) for g in groups] + [solvent_first]
    inner, edge, hot, force, face_low, face_high, *blocks = lax.switch(grp, turns)
    back = [
        lax.ppermute(block, axes, pairs(False, g) + pairs(True, g))
        for g, block in zip(groups, blocks)
    ]

    def solvent_last():
        added, top, bottom = call(deposit(True), (inner, edge, *back, hot), (layers, halo, halo))
        low, high = both_ways(top, bottom, [solvent])
        out, mid = call(inner_last(q_count, tiles), (added, kap), (flat, ends), sweeping)
        (out,) = call(
            outer_last(q_count, tiles),
            (top, bottom, low, high, kap_edge, far_low, far_high, mid, out),
            (flat,),
            [pltpu.VMEM((4 * 16 * tiles, LANES), F32), pltpu.SemaphoreType.DMA((2,))],
            away=(8,),
            unused=(0,),
            alias={8: 0},
        )
        return out

    def swapped(g):
        return lambda: swap(back[g])

    def mech_last():
        mine = lax.switch(grp, [swapped(g) for g in groups])
        (out,) = call(
            last_step,
            (
                moved,
                force.reshape(3, 512, e),
                mat.reshape(3, 512, e),
                occ,
                sel,
                mine,
                face_low,
                face_high,
                side_low,
                side_high,
            ),
            (shape_of((3, 512, e)),),
            work + streaming,
            away=(0, 1, 2),
            unused=(0,),
        )
        return out.reshape(1536, e)

    return lax.cond(is_solvent, solvent_last, mech_last).reshape(state.shape)


def solution(mesh):
    in_specs = (
        P("grp", None, None, "blk"),
        P("grp", None, None, "blk"),
        P(("grp", "blk")),
        P(("grp", "blk"), None),
        P(("grp", "blk")),
    )
    out_specs = P("grp", None, None, "blk")
    return jax.shard_map(shards, mesh=mesh, in_specs=in_specs, out_specs=out_specs, check_vma=False)
```

```python
import jax
import jax.numpy as jnp
from jax import lax
from jax.experimental import pallas as pl
from jax.experimental.pallas import tpu as pltpu
from jax.sharding import PartitionSpec as P


UNIT_LENGTH = 0.02
TIME_STEP = 0.1
PENALTY = 1.0
PRESSURE_SCALE = 0.05
DILATION_SCALE = 50.0
SWEEP_STEP = 0.03
SOURCE_RATE = 2.0
CUBIC_TERM = 0.3

LANES = 128
VMEM_LIMIT = 24 << 20
F32, BF16 = jnp.float32, jnp.bfloat16
VMEM = pl.BlockSpec(memory_space=pltpu.VMEM)
SMEM = pl.BlockSpec(memory_space=pltpu.SMEM)
ANY = pl.BlockSpec(memory_space=pltpu.HBM)


def shape_of(shape, dtype=F32):
    return jax.ShapeDtypeStruct(shape, dtype)


def call(body, args, outs, scratch=(), smem=0, away=(), unused=(), alias=None):
    specs = [SMEM] * smem + [VMEM] * (len(args) - smem)
    return pl.pallas_call(
        body,
        out_shape=outs,
        in_specs=[ANY if n in away else spec for n, spec in enumerate(specs)],
        out_specs=tuple(ANY if n in unused else VMEM for n in range(len(outs))),
        scratch_shapes=list(scratch),
        input_output_aliases=alias or {},
        compiler_params=pltpu.CompilerParams(vmem_limit_bytes=VMEM_LIMIT),
    )(*args)


def iota(shape, dim):
    return lax.broadcasted_iota(jnp.int32, shape, dim)


def dot(a, b, dims):
    return lax.dot_general(a, b, (dims, ((), ())), preferred_element_type=F32)


def diff_i(below, here, above):
    if below is None:
        return above - here
    if above is None:
        return here - below
    return 0.5 * (above - below)


def diff_j(x):
    return jnp.concatenate([x[1:2] - x[0:1], 0.5 * (x[2:] - x[:-2]), x[7:8] - x[6:7]], axis=0)


def diff_k(x):
    k = iota(x.shape, 1)
    upper = jnp.where(k == 7, x, pltpu.roll(x, 7, 1))
    lower = jnp.where(k == 0, x, pltpu.roll(x, 1, 1))
    return jnp.where((k == 0) | (k == 7), 1.0, 0.5) * (upper - lower)


def slab(ref, c, i):
    rows = ref[pl.ds(c * 512 + 64 * i, 64), :]
    return rows.reshape(8, 8, rows.shape[-1])


def put_slab(ref, c, i, value):
    ref[pl.ds(c * 512 + 64 * i, 64), :] = value.reshape(64, value.shape[-1])


def gradients(ref, i):
    grads = []
    for c in range(3):
        here = UNIT_LENGTH * slab(ref, c, i)
        below = UNIT_LENGTH * slab(ref, c, i - 1) if i > 0 else None
        above = UNIT_LENGTH * slab(ref, c, i + 1) if i < 7 else None
        row = [diff_i(below, here, above), diff_j(here), diff_k(here)]
        row[c] = row[c] + 1.0
        grads.append(row)
    return grads


def determinant(grads):
    return (
        grads[0][0] * (grads[1][1] * grads[2][2] - grads[1][2] * grads[2][1])
        - grads[0][1] * (grads[1][0] * grads[2][2] - grads[1][2] * grads[2][0])
        + grads[0][2] * (grads[1][0] * grads[2][1] - grads[1][1] * grads[2][0])
    )


def cofactors(g):
    return [
        [
            g[1][1] * g[2][2] - g[1][2] * g[2][1],
            g[1][2] * g[2][0] - g[1][0] * g[2][2],
            g[1][0] * g[2][1] - g[1][1] * g[2][0],
        ],
        [
            g[0][2] * g[2][1] - g[0][1] * g[2][2],
            g[0][0] * g[2][2] - g[0][2] * g[2][0],
            g[0][1] * g[2][0] - g[0][0] * g[2][1],
        ],
        [
            g[0][1] * g[1][2] - g[0][2] * g[1][1],
            g[0][2] * g[1][0] - g[0][0] * g[1][2],
            g[0][0] * g[1][1] - g[0][1] * g[1][0],
        ],
    ]


def dilate(ref, filled, out):
    for i in range(8):
        change = (determinant(gradients(ref, i)) - 1.0) * filled * DILATION_SCALE
        out[pl.ds(64 * i, 64), :] = change.reshape(64, change.shape[-1]).astype(BF16)


def put_faces(ref, up, down):
    for c in range(3):
        up[pl.ds(64 * c, 64), :] = ref[pl.ds(c * 512 + 448, 64), :].astype(BF16)
        down[pl.ds(64 * c, 64), :] = ref[pl.ds(c * 512, 64), :].astype(BF16)


def elastic(ref, mat, filled, out, stress, partial):
    e = filled.shape[-1]
    for i in range(8):
        g = gradients(ref, i)
        shear, lame = slab(mat, 0, i), slab(mat, 1, i)
        c = {}
        for a in range(3):
            for b in range(a, 3):
                c[a, b] = g[0][a] * g[0][b] + g[1][a] * g[1][b] + g[2][a] * g[2][b]
        diag = [c[a, a] - 1.0 for a in range(3)]
        volume = lame * (0.5 * (diag[0] + diag[1] + diag[2]))
        s = {}
        for a in range(3):
            s[a, a] = shear * diag[a] + volume
            for b in range(a + 1, 3):
                s[a, b] = s[b, a] = shear * c[a, b]
        for a in range(3):
            first = [g[a][0] * s[0, b] + g[a][1] * s[1, b] + g[a][2] * s[2, b] for b in range(3)]
            put_slab(stress, a, i, first[0])
            put_slab(partial, a, i, diff_j(first[1]) + diff_k(first[2]))
    k = iota((8, 8, e), 1)
    lane = iota((1, 1, e), 2)
    penalty = PENALTY * UNIT_LENGTH
    fill_before = jnp.where(lane == 0, 0.0, pltpu.roll(filled, 1, 2)) * penalty
    fill_after = jnp.where(lane == e - 1, 0.0, pltpu.roll(filled, e - 1, 2)) * penalty
    before_scale = jnp.where(k == 0, fill_before, 0.0)
    after_scale = jnp.where(k == 7, fill_after, 0.0)
    for i in range(8):
        for a in range(3):
            here = slab(ref, a, i)
            force = slab(partial, a, i) + diff_i(
                slab(stress, a, i - 1) if i > 0 else None,
                slab(stress, a, i),
                slab(stress, a, i + 1) if i < 7 else None,
            )
            before = pltpu.roll(pltpu.roll(here, 1, 1), 1, 2)
            after = pltpu.roll(pltpu.roll(here, 7, 1), e - 1, 2)
            force = force + before_scale * (before - here) + after_scale * (after - here)
            put_slab(out, a, i, force)


def advance(ref, mat, filled, base, recv, sel, low, high, fills, out, pressure, stress, partial):
    e = filled.shape[-1]
    pressure[...] = dot(recv[...], sel[...], ((0,), (0,))) * PRESSURE_SCALE
    for i in range(8):
        cof = cofactors(gradients(ref, i))
        p = pressure[pl.ds(64 * i, 64), :].reshape(8, 8, e)
        for a in range(3):
            first = [p * cof[a][b] for b in range(3)]
            put_slab(stress, a, i, first[0])
            put_slab(partial, a, i, slab(base, a, i) - (diff_j(first[1]) + diff_k(first[2])))
    penalty = PENALTY * UNIT_LENGTH
    fill_low, fill_high = fills[0].reshape(1, 1, e), fills[1].reshape(1, 1, e)
    for i in range(8):
        rate = (TIME_STEP / UNIT_LENGTH) * slab(mat, 2, i) * filled
        for a in range(3):
            here = slab(ref, a, i)
            force = slab(partial, a, i) - diff_i(
                slab(stress, a, i - 1) if i > 0 else None,
                slab(stress, a, i),
                slab(stress, a, i + 1) if i < 7 else None,
            )
            if i == 0:
                other = low[pl.ds(64 * a, 64), :].astype(F32).reshape(8, 8, e)
                force = force + penalty * fill_low * (other - here)
            if i == 7:
                other = high[pl.ds(64 * a, 64), :].astype(F32).reshape(8, 8, e)
                force = force + penalty * fill_high * (other - here)
            put_slab(out, a, i, here + rate * force)


def permute_in(x, tables):
    x = jnp.take_along_axis(x, tables[0], axis=1, mode="promise_in_bounds")
    x = jnp.take_along_axis(x, tables[1], axis=0, mode="promise_in_bounds")
    return jnp.take_along_axis(x, tables[2], axis=1, mode="promise_in_bounds")


def tables_in():
    row, lane = iota((8, LANES), 0), iota((8, LANES), 1)
    high, low = lane // 16, lane % 16
    return (8 * low + (high - row + 8) % 8, (high - row + 8) % 8, 16 * ((high + row) % 8) + low)


def tables_out():
    row, lane = iota((8, LANES), 0), iota((8, LANES), 1)
    high, low = lane // 16, lane % 16
    return (
        16 * ((high - row + 8) % 8) + low,
        (high - row + 8) % 8,
        16 * ((lane % 8 + row) % 8) + lane // 8,
    )


def layer_to_octants(chunk, scale, tables, tiles):
    rows = chunk.shape[0]
    lane = iota((8, LANES), 1)
    parts = []
    for y in range(16):
        part = chunk[tiles * y : min(tiles * y + 8, rows)]
        if part.shape[0] < 8:
            pad = jnp.zeros((8 - part.shape[0], LANES), F32)
            part = jnp.concatenate([part, pad], axis=0)
        part = permute_in(part, tables)
        parts.append(jnp.where(lane < 16 * tiles, part, 0.0))
    layer = jnp.concatenate(parts, axis=0)
    return layer * scale if scale != 1.0 else layer


def to_octants(ref, out, scale, tables, tiles):
    rows = 16 * tiles

    def layer(x, carry):
        chunk = ref[pl.ds(pl.multiple_of(x * rows, 8), rows), :]
        out[layer_rows(x), :] = layer_to_octants(chunk, scale, tables, tiles)
        return carry

    lax.fori_loop(0, 16, layer, 0, unroll=2)


def layer_from_octants(layer, tables, tiles):
    return jnp.concatenate(
        [permute_in(layer[8 * y : 8 * y + 8], tables)[:tiles] for y in range(16)], axis=0
    )


def layer_rows(x):
    return pl.ds(pl.multiple_of(x * LANES, LANES), LANES)


def pressures(layer):
    return (layer + CUBIC_TERM * layer * layer * layer).astype(BF16)


def one_hot(tile, width):
    return jnp.concatenate(
        [jnp.where(tile == float(o + 1), 1.0, 0.0).astype(BF16)[:, :width] for o in range(4)],
        axis=1,
    )


def weight(c):
    return 0.5 + c * c


def flux(c, s, other, other_s):
    return (s + other_s) * (other - c)


def inside(c, s, masks):
    inner, last, outer = masks
    fy = flux(c[:-1], s[:-1], c[1:], s[1:])
    r = pltpu.roll(c, 7, 1)
    up = jnp.where(inner, r, jnp.where(last, c, pltpu.roll(r, LANES - 1, 2)))
    fz = flux(c, s, up, weight(up))
    r = pltpu.roll(fz, 1, 1)
    total = fz - jnp.where(outer, r, pltpu.roll(r, 1, 2))
    return jnp.concatenate([total[:1] + fy[:1], total[1:-1] + (fy[1:] - fy[:-1]), total[-1:] - fy[-1:]], axis=0)


def sweep_masks(q_count):
    k, lane = iota((16, 8, LANES), 1), iota((16, 8, LANES), 2)
    return k < 7, lane >= q_count - 1, k > 0


def load(ref, x):
    return ref[layer_rows(x), :].astype(F32).reshape(16, 8, LANES)


def sweep_range(ref, kap, start, stop, put, weights, fluxes, masks):
    c, s = load(ref, start), None
    before = load(ref, start - 1)
    s = weight(c)
    weights[...] = s
    fluxes[...] = flux(before, weight(before), c, s)

    def step(x, carry):
        c, up = load(ref, x), load(ref, x + 1)
        s, up_s = weights[...], weight(up)
        weights[...] = up_s
        fx = flux(c, s, up, up_s)
        total = (fx - fluxes[...]) + inside(c, s, masks)
        fluxes[...] = fx
        put(x, (c + load(kap, x) * total).reshape(LANES, LANES))
        return carry

    lax.fori_loop(start, stop, step, 0, unroll=2)


def inner_sweeps(phi, kap, middle, edges, put, weights, fluxes, q_count):
    masks = sweep_masks(q_count)

    def keep(x, layer):
        middle[layer_rows(x), :] = layer

    sweep_range(phi, kap, 1, 15, keep, weights, fluxes, masks)
    for n, x in enumerate((1, 2, 13, 14)):
        edges[layer_rows(n), :] = middle[layer_rows(x), :]
    for n, x in enumerate((0, 1, 14, 15)):
        edges[layer_rows(4 + n), :] = phi[layer_rows(x), :]
    sweep_range(middle, kap, 2, 14, put, weights, fluxes, masks)


def sweep_chain(layers, kaps, masks):
    weights = [weight(c) for c in layers]
    fx = [
        flux(layers[n], weights[n], layers[n + 1], weights[n + 1]) for n in range(len(layers) - 1)
    ]
    return [
        layers[n] + kaps[n - 1] * ((fx[n] - fx[n - 1]) + inside(layers[n], weights[n], masks))
        for n in range(1, len(layers) - 1)
    ]


def edge_sweeps(low, high, kap_edge, kap_low, kap_high, middle, q_count):
    masks = sweep_masks(q_count)
    k = [load(kap_edge, n) for n in range(4)]
    m = [load(middle, n) for n in range(8)]
    first = [load(low, 0), load(low, 1), m[4], m[5]]
    first = sweep_chain(first, [load(kap_low, 2), k[0]], masks)
    first = sweep_chain([*first, m[0], m[1]], k[:2], masks)
    last = [m[6], m[7], load(high, 0), load(high, 1)]
    last = sweep_chain(last, [k[3], load(kap_high, 2)], masks)
    last = sweep_chain([m[2], m[3], *last], k[2:], masks)
    return [layer.reshape(LANES, LANES) for layer in first + last]


def prepare(n_blk, cap, tiles, solvent):
    def body(grp, state, occ, col, octant, send, sel, filled, field, phi, up, down, *scratch):
        dil, ints, layers, int_sems, sem = scratch
        e = state.shape[-1]
        quarter = 16 * tiles

        @pl.when(grp[0] != solvent)
        def _():
            copies = [
                pltpu.make_async_copy(ref, ints.at[n], int_sems.at[n])
                for n, ref in enumerate((occ, col, octant))
            ]
            for copy in copies:
                copy.start()
            dilate(state, 1.0, dil)
            for copy in copies:
                copy.wait()
            full, column, o = ints[0].astype(F32), ints[1], ints[2]
            hits = jnp.where(column == iota((n_blk, e), 0), 1.0, 0.0)
            earlier = jnp.where(iota((e, e), 0) < iota((e, e), 1), 1.0, 0.0).astype(BF16)
            rank = dot(hits.astype(BF16), earlier, ((1,), (0,)))
            rank = jnp.sum(rank * hits, axis=0, keepdims=True).astype(jnp.int32)
            slot = column * cap + rank
            chosen = jnp.where(iota((n_blk * cap, e), 0) == slot, 1.0, 0.0)
            held = (chosen * full).astype(BF16)
            chosen = chosen.astype(BF16)
            sel[...] = chosen
            send[:, pl.ds(0, 512)] = dot(held, dil[...], ((1,), (1,))).astype(BF16)
            block = sum((jnp.where(o >= n * quarter, 1, 0) for n in range(1, 4)))
            spot = o - quarter * block
            tile = jnp.where(iota((LANES, e), 0) == spot, (block + 1).astype(F32), 0.0)
            tile = dot(chosen, tile.astype(BF16), ((1,), (1,)))
            send[:, pl.ds(512, LANES)] = tile.astype(BF16)
            put_faces(state, up, down)
            filled[...] = jnp.broadcast_to(full, (8, e))
            up[pl.ds(192, 8), :] = jnp.broadcast_to(full, (8, e)).astype(BF16)
            down[pl.ds(192, 8), :] = jnp.broadcast_to(full, (8, e)).astype(BF16)

        @pl.when(grp[0] == solvent)
        def _():
            tables = tables_in()
            to_octants(state, layers, 1.0, tables, tiles)
            copy = pltpu.make_async_copy(layers, phi, sem.at[0])
            copy.start()
            for i in range(8):
                parts = []
                for ox in range(2):
                    for oy in range(2):
                        p = pressures(layers[pl.ds(LANES * (8 * ox + i) + 64 * oy, 64), :])
                        parts.append(p[:, :quarter])
                field[pl.ds(64 * i, 64), :] = jnp.concatenate(parts, axis=1)
            copy.wait()

    return body


def rates(tiles):
    def body(mat, kap, edge):
        to_octants(mat, kap, 0.5 * SWEEP_STEP, tables_in(), tiles)
        for n, x in enumerate((0, 1, 14, 15)):
            edge[layer_rows(n), :] = kap[layer_rows(x), :]

    return body


def gather_field(quarter):
    def body(recv, field, out):
        hot = one_hot(recv[:, pl.ds(512, LANES)].astype(F32), quarter)
        out[...] = dot(hot, field[...], ((1,), (1,))).astype(BF16)

    return body


def elastic_forces(state, mat, occ, out, *scratch):
    elastic(state, mat, occ[pl.ds(0, 1), :].reshape(1, 1, occ.shape[-1]), out, *scratch[-2:])


def idle(*refs):
    pass


def first_step(state, mat, occ, base, sel, recv, low, high, out, send, up, down, *scratch):
    filled = occ[pl.ds(0, 1), :].reshape(1, 1, occ.shape[-1])
    fills = [ref[pl.ds(192, 8), :].astype(F32)[:1] for ref in (low, high)]
    advance(state, mat, filled, base, recv, sel, low, high, fills, out, *scratch[:3])
    dil = scratch[3]
    dilate(out, filled, dil)
    send[...] = dot(sel[...], dil[...], ((1,), (1,))).astype(BF16)
    put_faces(out, up, down)


def last_step(state, mat, occ, base, sel, recv, low, high, fill_low, fill_high, out, *scratch):
    filled = occ[pl.ds(0, 1), :].reshape(1, 1, occ.shape[-1])
    fills = [ref[pl.ds(192, 8), :].astype(F32)[:1] for ref in (fill_low, fill_high)]
    advance(state, mat, filled, base, recv, sel, low, high, fills, out, *scratch)


def deposit(edged):
    def body(phi, *refs):
        if edged:
            edge, v0, v1, v2, tile, out, up, down = refs
        else:
            border, v0, v1, v2, out, up, down, tile, _ = refs
            down[layer_rows(2), :] = border[layer_rows(0), :].astype(BF16)
            up[layer_rows(2), :] = border[layer_rows(3), :].astype(BF16)
        total = None
        for n, v in enumerate((v0, v1, v2)):
            spot = pl.ds(n * v.shape[0], v.shape[0])
            if not edged:
                tile[spot, :] = v[:, pl.ds(512, LANES)]
            hot = one_hot(tile[spot, :].astype(F32), LANES)
            part = dot(v[:, pl.ds(0, 512)], hot, ((0,), (0,)))
            total = part if total is None else total + part
        for x in range(16):
            i, ox = x % 8, x // 8
            if edged and x in (0, 1, 14, 15):
                layer = edge[layer_rows((0, 1, 14, 15).index(x)), :]
            else:
                layer = phi[layer_rows(x), :]
            added = jnp.concatenate(
                [
                    total[64 * i : 64 * i + 64, 256 * ox + LANES * o : 256 * ox + LANES * (o + 1)]
                    for o in range(2)
                ],
                axis=0,
            )
            layer = layer + (SWEEP_STEP * SOURCE_RATE) * added
            out[layer_rows(x), :] = layer
            if x < 2:
                down[layer_rows(x), :] = layer.astype(BF16)
            if x >= 14:
                up[layer_rows(x - 14), :] = layer.astype(BF16)

    return body


def inner_first(q_count):
    def body(phi, kap, out, edges, *scratch):
        def put(x, layer):
            out[layer_rows(x), :] = layer

        inner_sweeps(phi, kap, scratch[0], edges, put, *scratch[1:], q_count)

    return body


def outer_first(q_count):
    def body(low, high, kap_edge, kap_low, kap_high, mid, phi, tile, edge, s0, s1, s2, field):
        final = edge_sweeps(low, high, kap_edge, kap_low, kap_high, mid, q_count)
        for n in range(4):
            edge[layer_rows(n), :] = final[n]
        for x in range(16):
            i, ox = x % 8, x // 8
            layer = final[(0, 1, 14, 15).index(x)] if x in (0, 1, 14, 15) else phi[layer_rows(x), :]
            p = pressures(layer)
            for o in range(2):
                field[pl.ds(64 * i, 64), pl.ds(256 * ox + LANES * o, LANES)] = p[64 * o : 64 * o + 64]
        for n, s in enumerate((s0, s1, s2)):
            spot = pl.ds(n * s.shape[0], s.shape[0])
            hot = one_hot(tile[spot, :].astype(F32), LANES)
            s[...] = dot(hot, field[...], ((1,), (1,))).astype(BF16)

    return body


def inner_last(q_count, tiles):
    def body(phi, kap, out, edges, *scratch):
        tables = tables_out()
        rows = 16 * tiles

        def put(x, layer):
            spot = pl.ds(pl.multiple_of(x * rows, 8), rows)
            out[spot, :] = layer_from_octants(layer, tables, tiles)

        inner_sweeps(phi, kap, scratch[0], edges, put, *scratch[1:], q_count)

    return body


def outer_last(q_count, tiles):
    def body(low, high, kap_edge, kap_low, kap_high, mid, _, out, ends, sem):
        final = edge_sweeps(low, high, kap_edge, kap_low, kap_high, mid, q_count)
        tables = tables_out()
        rows = 16 * tiles
        for n in range(4):
            ends[pl.ds(rows * n, rows), :] = layer_from_octants(final[n], tables, tiles)
        copies = [
            pltpu.make_async_copy(
                ends.at[pl.ds(2 * rows * n, 2 * rows)], out.at[pl.ds(start, 2 * rows)], sem.at[n]
            )
            for n, start in enumerate((0, 14 * rows))
        ]
        for copy in copies:
            copy.start()
        for copy in copies:
            copy.wait()

    return body


def shards(state, material, occupied, brick_column, brick_octant):
    e = state.shape[-1]
    n_blk, n_grp = lax.axis_size("blk"), lax.axis_size("grp")
    solvent, groups = n_grp - 1, range(n_grp - 1)
    cap = max(2, 2 * e // n_blk)
    slots = n_blk * cap
    tiles = 6 * e // LANES
    q_count = 6 * e // 8
    axes = ("grp", "blk")
    grp = lax.axis_index("grp").astype(jnp.int32)
    grp_at = grp.reshape(1)
    current = state.reshape(1536, e)
    mat = material.reshape(1536, e)
    col = brick_column.reshape(1, e)
    octant = brick_octant.reshape(1, e)
    layers, ends, halves = shape_of((2048, LANES)), shape_of((512, LANES)), shape_of((1024, LANES))
    halo = shape_of((256, LANES), BF16)
    rows, flat = shape_of((slots, 512), BF16), shape_of((1536, e))
    face, side, wide = (shape_of((n, e), BF16) for n in (192, 200, 384))
    tile = shape_of((slots * (n_grp - 1), LANES), BF16)

    def pairs(back, g):
        forth = [(g * n_blk + b, solvent * n_blk + b) for b in range(n_blk)]
        return [(j, i) for i, j in forth] if back else forth

    def planes(up, which):
        steps = [(b, b + 1) for b in range(n_blk - 1)]
        steps = steps if up else [(j, i) for i, j in steps]
        return [(g * n_blk + i, g * n_blk + j) for g in which for i, j in steps]

    def both_ways(up, down, which):
        return (
            lax.ppermute(up, axes, planes(True, which)),
            lax.ppermute(down, axes, planes(False, which)),
        )

    def swap(block):
        return lax.all_to_all(block, "blk", split_axis=0, concat_axis=0, tiled=True)

    send, sel, occ, field, phi, up, down = call(
        prepare(n_blk, cap, tiles, solvent),
        (grp_at, current, occupied.reshape(1, e), col, octant),
        (
            shape_of((slots, 512 + LANES), BF16),
            shape_of((slots, e), BF16),
            shape_of((8, e)),
            shape_of((512, 4 * q_count), BF16),
            layers,
            side,
            side,
        ),
        [
            pltpu.VMEM((512, e), BF16),
            pltpu.VMEM((3, 1, e), jnp.int32),
            pltpu.VMEM(layers.shape, F32),
            pltpu.SemaphoreType.DMA((3,)),
            pltpu.SemaphoreType.DMA((1,)),
        ],
        smem=1,
        away=(2, 3, 4),
        unused=(4,),
    )
    recv = swap(send)
    fields = []
    for g in groups:
        fields.append(lax.ppermute(field, axes, pairs(True, g)))
    side_low, side_high = both_ways(up, down, groups)
    work = [pltpu.VMEM((512, e), F32), pltpu.VMEM((1536, e), F32), pltpu.VMEM((1536, e), F32)]
    sweeping = [pltpu.VMEM(layers.shape, F32)] + [pltpu.VMEM((16, 8, LANES), F32)] * 2

    def gathered(g):
        def run():
            return call(gather_field(q_count), (recv, fields[g]), (rows,))[0]

        return run

    def nothing(*outs):
        return lambda: call(idle, (), outs, unused=range(len(outs)))

    mine = lax.switch(grp, [gathered(g) for g in groups] + [lambda: nothing(rows)()[0]])
    mine, recv = lax.optimization_barrier((mine, recv))
    mine = swap(mine)
    arrived = []
    for g in groups:
        arrived.append(lax.ppermute(recv, axes, pairs(False, g)))

    def solvent_rates():
        return tuple(call(rates(tiles), (mat,), (layers, ends)))

    def mech_elastic():
        return tuple(
            call(elastic_forces, (current, mat, occ), (layers, ends), work[1:], unused=(1,))
        )

    def mech_first():
        return tuple(
            call(
                first_step,
                (current, mat, occ, base, sel, mine, side_low, side_high),
                (layers, rows, face, face),
                work + [pltpu.VMEM((512, e), BF16)],
            )
        )

    is_solvent = grp == solvent
    base, kap_edge = lax.cond(is_solvent, solvent_rates, mech_elastic)
    kap = base
    idle_first = lambda: tuple(nothing(layers, rows, face, face)())
    moved, send, fore, aft = lax.cond(is_solvent, idle_first, mech_first)

    def solvent_first():
        added, top, bottom, hot, spare = call(
            deposit(False), (phi, kap_edge, *arrived), (layers, wide, wide, tile, flat), unused=(4,)
        )
        low, high = both_ways(top, bottom, [solvent])
        inner, mid = call(inner_first(q_count), (added, kap), (layers, halves), sweeping)
        edge, s0, s1, s2 = call(
            outer_first(q_count),
            (low, high, kap_edge, low, high, mid, inner, hot),
            (ends, rows, rows, rows),
            [pltpu.VMEM((512, 4 * LANES), BF16)],
        )
        return inner, edge, hot, spare, low, high, s0, s1, s2

    def mech_turn(g):
        def run():
            mine = swap(send)
            force, *spare = call(
                elastic_forces,
                (moved, mat, occ),
                (flat, layers, ends, tile, wide, wide, rows, rows),
                work[1:],
                unused=range(1, 8),
            )
            blocks = list(spare[5:])
            blocks.insert(g, mine)
            return *spare[:3], force, *spare[3:5], *blocks

        return run

    turns = [mech_turn(g) for g in groups] + [solvent_first]
    inner, edge, hot, force, far_low, far_high, *blocks = lax.switch(grp, turns)
    back = [
        lax.ppermute(block, axes, pairs(False, g) + pairs(True, g))
        for g, block in zip(groups, blocks)
    ]

    def solvent_last():
        added, top, bottom = call(deposit(True), (inner, edge, *back, hot), (layers, halo, halo))
        low, high = both_ways(top, bottom, [solvent])
        out, mid = call(inner_last(q_count, tiles), (added, kap), (flat, halves), sweeping)
        (out,) = call(
            outer_last(q_count, tiles),
            (low, high, kap_edge, far_low, far_high, mid, out),
            (flat,),
            [pltpu.VMEM((4 * 16 * tiles, LANES), F32), pltpu.SemaphoreType.DMA((2,))],
            away=(6,),
            unused=(0,),
            alias={6: 0},
        )
        return out

    def swapped(g):
        return lambda: (swap(back[g]), *both_ways(fore, aft, [g]))

    def mech_last():
        mine, low, high = lax.switch(grp, [swapped(g) for g in groups])
        (out,) = call(
            last_step,
            (moved, mat, occ, force, sel, mine, low, high, side_low, side_high),
            (flat,),
            work,
        )
        return out

    return lax.cond(is_solvent, solvent_last, mech_last).reshape(state.shape)


def solution(mesh):
    in_specs = (
        P("grp", None, None, "blk"),
        P("grp", None, None, "blk"),
        P(("grp", "blk")),
        P(("grp", "blk"), None),
        P(("grp", "blk")),
    )
    out_specs = P("grp", None, None, "blk")
    return jax.shard_map(shards, mesh=mesh, in_specs=in_specs, out_specs=out_specs, check_vma=False)
```

```python
import jax
import jax.numpy as jnp
from jax import lax
from jax.experimental import pallas as pl
from jax.experimental.pallas import tpu as pltpu
from jax.sharding import PartitionSpec as P


UNIT_LENGTH = 0.02
TIME_STEP = 0.1
PENALTY = 1.0
PRESSURE_SCALE = 0.05
DILATION_SCALE = 50.0
SWEEP_STEP = 0.03
SOURCE_RATE = 2.0
CUBIC_TERM = 0.3

LANES = 128
VMEM_LIMIT = 24 << 20
F32, BF16 = jnp.float32, jnp.bfloat16
VMEM = pl.BlockSpec(memory_space=pltpu.VMEM)
SMEM = pl.BlockSpec(memory_space=pltpu.SMEM)
ANY = pl.BlockSpec(memory_space=pltpu.HBM)


def shape_of(shape, dtype=F32):
    return jax.ShapeDtypeStruct(shape, dtype)


def call(body, args, outs, scratch=(), smem=0, away=(), unused=(), alias=None):
    specs = [SMEM] * smem + [VMEM] * (len(args) - smem)
    return pl.pallas_call(
        body,
        out_shape=outs,
        in_specs=[ANY if n in away else spec for n, spec in enumerate(specs)],
        out_specs=tuple(ANY if n in unused else VMEM for n in range(len(outs))),
        scratch_shapes=list(scratch),
        input_output_aliases=alias or {},
        compiler_params=pltpu.CompilerParams(vmem_limit_bytes=VMEM_LIMIT),
    )(*args)


def iota(shape, dim):
    return lax.broadcasted_iota(jnp.int32, shape, dim)


def dot(a, b, dims):
    return lax.dot_general(a, b, (dims, ((), ())), preferred_element_type=F32)


def diff_i(below, here, above):
    if below is None:
        return above - here
    if above is None:
        return here - below
    return 0.5 * (above - below)


def diff_j(x):
    return jnp.concatenate([x[1:2] - x[0:1], 0.5 * (x[2:] - x[:-2]), x[7:8] - x[6:7]], axis=0)


def diff_k(x):
    k = iota(x.shape, 1)
    upper = jnp.where(k == 7, x, pltpu.roll(x, 7, 1))
    lower = jnp.where(k == 0, x, pltpu.roll(x, 1, 1))
    return jnp.where((k == 0) | (k == 7), 1.0, 0.5) * (upper - lower)


def slab(ref, c, i):
    rows = ref[pl.ds(c * 512 + 64 * i, 64), :]
    return rows.reshape(8, 8, rows.shape[-1])


def put_slab(ref, c, i, value):
    ref[pl.ds(c * 512 + 64 * i, 64), :] = value.reshape(64, value.shape[-1])


def gradients(ref, i):
    grads = []
    for c in range(3):
        here = UNIT_LENGTH * slab(ref, c, i)
        below = UNIT_LENGTH * slab(ref, c, i - 1) if i > 0 else None
        above = UNIT_LENGTH * slab(ref, c, i + 1) if i < 7 else None
        row = [diff_i(below, here, above), diff_j(here), diff_k(here)]
        row[c] = row[c] + 1.0
        grads.append(row)
    return grads


def determinant(grads):
    return (
        grads[0][0] * (grads[1][1] * grads[2][2] - grads[1][2] * grads[2][1])
        - grads[0][1] * (grads[1][0] * grads[2][2] - grads[1][2] * grads[2][0])
        + grads[0][2] * (grads[1][0] * grads[2][1] - grads[1][1] * grads[2][0])
    )


def cofactors(g):
    return [
        [
            g[1][1] * g[2][2] - g[1][2] * g[2][1],
            g[1][2] * g[2][0] - g[1][0] * g[2][2],
            g[1][0] * g[2][1] - g[1][1] * g[2][0],
        ],
        [
            g[0][2] * g[2][1] - g[0][1] * g[2][2],
            g[0][0] * g[2][2] - g[0][2] * g[2][0],
            g[0][1] * g[2][0] - g[0][0] * g[2][1],
        ],
        [
            g[0][1] * g[1][2] - g[0][2] * g[1][1],
            g[0][2] * g[1][0] - g[0][0] * g[1][2],
            g[0][0] * g[1][1] - g[0][1] * g[1][0],
        ],
    ]


def dilate(ref, filled, out):
    for i in range(8):
        change = (determinant(gradients(ref, i)) - 1.0) * filled * DILATION_SCALE
        out[pl.ds(64 * i, 64), :] = change.reshape(64, change.shape[-1]).astype(BF16)


def put_faces(ref, up, down):
    for c in range(3):
        up[pl.ds(64 * c, 64), :] = ref[pl.ds(c * 512 + 448, 64), :].astype(BF16)
        down[pl.ds(64 * c, 64), :] = ref[pl.ds(c * 512, 64), :].astype(BF16)


def elastic(ref, mat, filled, out, stress, partial):
    e = filled.shape[-1]
    for i in range(8):
        g = gradients(ref, i)
        shear, lame = slab(mat, 0, i), slab(mat, 1, i)
        c = {}
        for a in range(3):
            for b in range(a, 3):
                c[a, b] = g[0][a] * g[0][b] + g[1][a] * g[1][b] + g[2][a] * g[2][b]
        diag = [c[a, a] - 1.0 for a in range(3)]
        volume = lame * (0.5 * (diag[0] + diag[1] + diag[2]))
        s = {}
        for a in range(3):
            s[a, a] = shear * diag[a] + volume
            for b in range(a + 1, 3):
                s[a, b] = s[b, a] = shear * c[a, b]
        for a in range(3):
            first = [g[a][0] * s[0, b] + g[a][1] * s[1, b] + g[a][2] * s[2, b] for b in range(3)]
            put_slab(stress, a, i, first[0])
            put_slab(partial, a, i, diff_j(first[1]) + diff_k(first[2]))
    k = iota((8, 8, e), 1)
    lane = iota((1, 1, e), 2)
    penalty = PENALTY * UNIT_LENGTH
    fill_before = jnp.where(lane == 0, 0.0, pltpu.roll(filled, 1, 2)) * penalty
    fill_after = jnp.where(lane == e - 1, 0.0, pltpu.roll(filled, e - 1, 2)) * penalty
    before_scale = jnp.where(k == 0, fill_before, 0.0)
    after_scale = jnp.where(k == 7, fill_after, 0.0)
    for i in range(8):
        for a in range(3):
            here = slab(ref, a, i)
            force = slab(partial, a, i) + diff_i(
                slab(stress, a, i - 1) if i > 0 else None,
                slab(stress, a, i),
                slab(stress, a, i + 1) if i < 7 else None,
            )
            before = pltpu.roll(pltpu.roll(here, 1, 1), 1, 2)
            after = pltpu.roll(pltpu.roll(here, 7, 1), e - 1, 2)
            force = force + before_scale * (before - here) + after_scale * (after - here)
            put_slab(out, a, i, force)


def advance(ref, rates, filled, base, recv, sel, low, high, fills, out, pressure, stress, partial):
    e = filled.shape[-1]
    pressure[...] = dot(recv[...], sel[...], ((0,), (0,))) * PRESSURE_SCALE
    for i in range(8):
        cof = cofactors(gradients(ref, i))
        p = pressure[pl.ds(64 * i, 64), :].reshape(8, 8, e)
        for a in range(3):
            first = [p * cof[a][b] for b in range(3)]
            put_slab(stress, a, i, first[0])
            put_slab(partial, a, i, slab(base, a, i) - (diff_j(first[1]) + diff_k(first[2])))
    penalty = PENALTY * UNIT_LENGTH
    fill_low, fill_high = fills[0].reshape(1, 1, e), fills[1].reshape(1, 1, e)
    for i in range(8):
        rate = slab(rates, 0, i)
        for a in range(3):
            here = slab(ref, a, i)
            force = slab(partial, a, i) - diff_i(
                slab(stress, a, i - 1) if i > 0 else None,
                slab(stress, a, i),
                slab(stress, a, i + 1) if i < 7 else None,
            )
            if i == 0:
                other = low[pl.ds(64 * a, 64), :].astype(F32).reshape(8, 8, e)
                force = force + penalty * fill_low * (other - here)
            if i == 7:
                other = high[pl.ds(64 * a, 64), :].astype(F32).reshape(8, 8, e)
                force = force + penalty * fill_high * (other - here)
            put_slab(out, a, i, here + rate * force)


def permute_in(x, tables):
    x = jnp.take_along_axis(x, tables[0], axis=1, mode="promise_in_bounds")
    x = jnp.take_along_axis(x, tables[1], axis=0, mode="promise_in_bounds")
    return jnp.take_along_axis(x, tables[2], axis=1, mode="promise_in_bounds")


def tables_in():
    row, lane = iota((8, LANES), 0), iota((8, LANES), 1)
    high, low = lane // 16, lane % 16
    return (8 * low + (high - row + 8) % 8, (high - row + 8) % 8, 16 * ((high + row) % 8) + low)


def tables_out():
    row, lane = iota((8, LANES), 0), iota((8, LANES), 1)
    high, low = lane // 16, lane % 16
    return (
        16 * ((high - row + 8) % 8) + low,
        (high - row + 8) % 8,
        16 * ((lane % 8 + row) % 8) + lane // 8,
    )


def layer_to_octants(chunk, scale, tables, tiles):
    rows = chunk.shape[0]
    lane = iota((8, LANES), 1)
    parts = []
    for y in range(16):
        part = chunk[tiles * y : min(tiles * y + 8, rows)]
        if part.shape[0] < 8:
            pad = jnp.zeros((8 - part.shape[0], LANES), F32)
            part = jnp.concatenate([part, pad], axis=0)
        part = permute_in(part, tables)
        parts.append(jnp.where(lane < 16 * tiles, part, 0.0))
    layer = jnp.concatenate(parts, axis=0)
    return layer * scale if scale != 1.0 else layer


def to_octants(ref, out, scale, tables, tiles):
    rows = 16 * tiles

    def layer(x, carry):
        chunk = ref[pl.ds(pl.multiple_of(x * rows, 8), rows), :]
        out[layer_rows(x), :] = layer_to_octants(chunk, scale, tables, tiles)
        return carry

    lax.fori_loop(0, 16, layer, 0, unroll=2)


def layer_from_octants(layer, tables, tiles):
    return jnp.concatenate(
        [permute_in(layer[8 * y : 8 * y + 8], tables)[:tiles] for y in range(16)], axis=0
    )


def layer_rows(x):
    return pl.ds(pl.multiple_of(x * LANES, LANES), LANES)


def pressures(layer):
    return (layer + CUBIC_TERM * layer * layer * layer).astype(BF16)


def one_hot(tile, width):
    return jnp.concatenate(
        [jnp.where(tile == float(o + 1), 1.0, 0.0).astype(BF16)[:, :width] for o in range(4)],
        axis=1,
    )


def weight(c):
    return 0.5 + c * c


def flux(c, s, other, other_s):
    return (s + other_s) * (other - c)


def inside(c, s, masks):
    inner, last, outer = masks
    fy = flux(c[:-1], s[:-1], c[1:], s[1:])
    r = pltpu.roll(c, 7, 1)
    up = jnp.where(inner, r, jnp.where(last, c, pltpu.roll(r, LANES - 1, 2)))
    fz = flux(c, s, up, weight(up))
    r = pltpu.roll(fz, 1, 1)
    total = fz - jnp.where(outer, r, pltpu.roll(r, 1, 2))
    return jnp.concatenate([total[:1] + fy[:1], total[1:-1] + (fy[1:] - fy[:-1]), total[-1:] - fy[-1:]], axis=0)


def sweep_masks(q_count):
    k, lane = iota((16, 8, LANES), 1), iota((16, 8, LANES), 2)
    return k < 7, lane >= q_count - 1, k > 0


def load(ref, x):
    return ref[layer_rows(x), :].astype(F32).reshape(16, 8, LANES)


def sweep_range(ref, kap, start, stop, put, weights, fluxes, masks):
    c, s = load(ref, start), None
    before = load(ref, start - 1)
    s = weight(c)
    weights[...] = s
    fluxes[...] = flux(before, weight(before), c, s)

    def step(x, carry):
        c, up = load(ref, x), load(ref, x + 1)
        s, up_s = weights[...], weight(up)
        weights[...] = up_s
        fx = flux(c, s, up, up_s)
        total = (fx - fluxes[...]) + inside(c, s, masks)
        fluxes[...] = fx
        put(x, (c + load(kap, x) * total).reshape(LANES, LANES))
        return carry

    lax.fori_loop(start, stop, step, 0, unroll=2)


def inner_sweeps(phi, kap, middle, edges, put, weights, fluxes, q_count):
    masks = sweep_masks(q_count)

    def keep(x, layer):
        middle[layer_rows(x), :] = layer

    sweep_range(phi, kap, 1, 15, keep, weights, fluxes, masks)
    for n, x in enumerate((1, 2, 13, 14)):
        edges[layer_rows(n), :] = middle[layer_rows(x), :]
    for n, x in enumerate((0, 1, 14, 15)):
        edges[layer_rows(4 + n), :] = phi[layer_rows(x), :]
    sweep_range(middle, kap, 2, 14, put, weights, fluxes, masks)


def sweep_chain(layers, kaps, masks):
    weights = [weight(c) for c in layers]
    fx = [
        flux(layers[n], weights[n], layers[n + 1], weights[n + 1]) for n in range(len(layers) - 1)
    ]
    return [
        layers[n] + kaps[n - 1] * ((fx[n] - fx[n - 1]) + inside(layers[n], weights[n], masks))
        for n in range(1, len(layers) - 1)
    ]


def edge_sweeps(low, high, kap_edge, kap_low, kap_high, middle, q_count):
    masks = sweep_masks(q_count)
    k = [load(kap_edge, n) for n in range(4)]
    m = [load(middle, n) for n in range(8)]
    first = [load(low, 0), load(low, 1), m[4], m[5]]
    first = sweep_chain(first, [load(kap_low, 2), k[0]], masks)
    first = sweep_chain([*first, m[0], m[1]], k[:2], masks)
    last = [m[6], m[7], load(high, 0), load(high, 1)]
    last = sweep_chain(last, [k[3], load(kap_high, 2)], masks)
    last = sweep_chain([m[2], m[3], *last], k[2:], masks)
    return [layer.reshape(LANES, LANES) for layer in first + last]


def prepare(n_blk, cap, tiles, solvent):
    def body(grp, state, occ, col, octant, send, sel, filled, near, far, phi, up, down, *scratch):
        dil, ints, layers, int_sems, sem = scratch
        e = state.shape[-1]
        quarter = 16 * tiles

        @pl.when(grp[0] != solvent)
        def _():
            copies = [
                pltpu.make_async_copy(ref, ints.at[n], int_sems.at[n])
                for n, ref in enumerate((occ, col, octant))
            ]
            for copy in copies:
                copy.start()
            dilate(state, 1.0, dil)
            for copy in copies:
                copy.wait()
            full, column, o = ints[0].astype(F32), ints[1], ints[2]
            hits = jnp.where(column == iota((n_blk, e), 0), 1.0, 0.0)
            earlier = jnp.where(iota((e, e), 0) < iota((e, e), 1), 1.0, 0.0).astype(BF16)
            rank = dot(hits.astype(BF16), earlier, ((1,), (0,)))
            rank = jnp.sum(rank * hits, axis=0, keepdims=True).astype(jnp.int32)
            slot = column * cap + rank
            chosen = jnp.where(iota((n_blk * cap, e), 0) == slot, 1.0, 0.0)
            held = (chosen * full).astype(BF16)
            chosen = chosen.astype(BF16)
            sel[...] = chosen
            send[:, pl.ds(0, 512)] = dot(held, dil[...], ((1,), (1,))).astype(BF16)
            block = sum((jnp.where(o >= n * quarter, 1, 0) for n in range(1, 4)))
            spot = o - quarter * block
            tile = jnp.where(iota((LANES, e), 0) == spot, (block + 1).astype(F32), 0.0)
            tile = dot(chosen, tile.astype(BF16), ((1,), (1,)))
            send[:, pl.ds(512, LANES)] = tile.astype(BF16)
            put_faces(state, up, down)
            filled[...] = jnp.broadcast_to(full, (8, e))
            up[pl.ds(192, 8), :] = jnp.broadcast_to(full, (8, e)).astype(BF16)
            down[pl.ds(192, 8), :] = jnp.broadcast_to(full, (8, e)).astype(BF16)

        @pl.when(grp[0] == solvent)
        def _():
            tables = tables_in()
            to_octants(state, layers, 1.0, tables, tiles)
            copy = pltpu.make_async_copy(layers, phi, sem.at[0])
            copy.start()
            for i in range(8):
                parts = []
                for ox in range(2):
                    for oy in range(2):
                        p = pressures(layers[pl.ds(LANES * (8 * ox + i) + 64 * oy, 64), :])
                        parts.append(p[:, :quarter])
                half = near if i < 4 else far
                half[pl.ds(64 * (i % 4), 64), :] = jnp.concatenate(parts, axis=1)
            copy.wait()

    return body


def rates(tiles):
    def body(mat, kap, edge):
        to_octants(mat, kap, 0.5 * SWEEP_STEP, tables_in(), tiles)
        for n, x in enumerate((0, 1, 14, 15)):
            edge[layer_rows(n), :] = kap[layer_rows(x), :]

    return body


def gather_field(quarter):
    def body(recv, near, far, out):
        hot = one_hot(recv[:, pl.ds(512, LANES)].astype(F32), quarter)
        for n, half in enumerate((near, far)):
            out[:, pl.ds(256 * n, 256)] = dot(hot, half[...], ((1,), (1,))).astype(BF16)

    return body


def elastic_and_rate(state, mat, occ, out, rate, *scratch):
    filled = occ[pl.ds(0, 1), :].reshape(1, 1, occ.shape[-1])
    for i in range(8):
        put_slab(rate, 0, i, (TIME_STEP / UNIT_LENGTH) * slab(mat, 2, i) * filled)
    elastic(state, mat, filled, out, *scratch)


def elastic_forces(state, mat, occ, out, *scratch):
    elastic(state, mat, occ[pl.ds(0, 1), :].reshape(1, 1, occ.shape[-1]), out, *scratch[-2:])


def idle(*refs):
    pass


def first_step(state, rates, occ, base, sel, recv, low, high, out, send, up, down, *scratch):
    filled = occ[pl.ds(0, 1), :].reshape(1, 1, occ.shape[-1])
    fills = [ref[pl.ds(192, 8), :].astype(F32)[:1] for ref in (low, high)]
    advance(state, rates, filled, base, recv, sel, low, high, fills, out, *scratch[:3])
    dil = scratch[3]
    dilate(out, filled, dil)
    send[...] = dot(sel[...], dil[...], ((1,), (1,))).astype(BF16)
    put_faces(out, up, down)


def last_step(state, rates, occ, base, sel, recv, low, high, fill_low, fill_high, out, *scratch):
    filled = occ[pl.ds(0, 1), :].reshape(1, 1, occ.shape[-1])
    fills = [ref[pl.ds(192, 8), :].astype(F32)[:1] for ref in (fill_low, fill_high)]
    advance(state, rates, filled, base, recv, sel, low, high, fills, out, *scratch)


def deposit(edged):
    def body(phi, *refs):
        if edged:
            edge, v0, v1, v2, tile, out, up, down = refs
        else:
            border, v0, v1, v2, out, up, down, tile, _ = refs
            down[layer_rows(2), :] = border[layer_rows(0), :].astype(BF16)
            up[layer_rows(2), :] = border[layer_rows(3), :].astype(BF16)
        total = None
        for n, v in enumerate((v0, v1, v2)):
            spot = pl.ds(n * v.shape[0], v.shape[0])
            if not edged:
                tile[spot, :] = v[:, pl.ds(512, LANES)]
            hot = one_hot(tile[spot, :].astype(F32), LANES)
            part = dot(v[:, pl.ds(0, 512)], hot, ((0,), (0,)))
            total = part if total is None else total + part
        for x in range(16):
            i, ox = x % 8, x // 8
            if edged and x in (0, 1, 14, 15):
                layer = edge[layer_rows((0, 1, 14, 15).index(x)), :]
            else:
                layer = phi[layer_rows(x), :]
            added = jnp.concatenate(
                [
                    total[64 * i : 64 * i + 64, 256 * ox + LANES * o : 256 * ox + LANES * (o + 1)]
                    for o in range(2)
                ],
                axis=0,
            )
            layer = layer + (SWEEP_STEP * SOURCE_RATE) * added
            out[layer_rows(x), :] = layer
            if x < 2:
                down[layer_rows(x), :] = layer.astype(BF16)
            if x >= 14:
                up[layer_rows(x - 14), :] = layer.astype(BF16)

    return body


def inner_first(q_count):
    def body(phi, kap, out, edges, *scratch):
        def put(x, layer):
            out[layer_rows(x), :] = layer

        inner_sweeps(phi, kap, scratch[0], edges, put, *scratch[1:], q_count)

    return body


def outer_first(q_count):
    def body(low, high, kap_edge, kap_low, kap_high, mid, phi, tile, edge, s0, s1, s2, field):
        final = edge_sweeps(low, high, kap_edge, kap_low, kap_high, mid, q_count)
        for n in range(4):
            edge[layer_rows(n), :] = final[n]
        for x in range(16):
            i, ox = x % 8, x // 8
            layer = final[(0, 1, 14, 15).index(x)] if x in (0, 1, 14, 15) else phi[layer_rows(x), :]
            p = pressures(layer)
            for o in range(2):
                field[pl.ds(64 * i, 64), pl.ds(256 * ox + LANES * o, LANES)] = p[64 * o : 64 * o + 64]
        for n, s in enumerate((s0, s1, s2)):
            spot = pl.ds(n * s.shape[0], s.shape[0])
            hot = one_hot(tile[spot, :].astype(F32), LANES)
            s[...] = dot(hot, field[...], ((1,), (1,))).astype(BF16)

    return body


def inner_last(q_count, tiles):
    def body(phi, kap, out, edges, *scratch):
        tables = tables_out()
        rows = 16 * tiles

        def put(x, layer):
            spot = pl.ds(pl.multiple_of(x * rows, 8), rows)
            out[spot, :] = layer_from_octants(layer, tables, tiles)

        inner_sweeps(phi, kap, scratch[0], edges, put, *scratch[1:], q_count)

    return body


def outer_last(q_count, tiles):
    def body(low, high, kap_edge, kap_low, kap_high, mid, _, out, ends, sem):
        final = edge_sweeps(low, high, kap_edge, kap_low, kap_high, mid, q_count)
        tables = tables_out()
        rows = 16 * tiles
        for n in range(4):
            ends[pl.ds(rows * n, rows), :] = layer_from_octants(final[n], tables, tiles)
        copies = [
            pltpu.make_async_copy(
                ends.at[pl.ds(2 * rows * n, 2 * rows)], out.at[pl.ds(start, 2 * rows)], sem.at[n]
            )
            for n, start in enumerate((0, 14 * rows))
        ]
        for copy in copies:
            copy.start()
        for copy in copies:
            copy.wait()

    return body


def shards(state, material, occupied, brick_column, brick_octant):
    e = state.shape[-1]
    n_blk, n_grp = lax.axis_size("blk"), lax.axis_size("grp")
    solvent, groups = n_grp - 1, range(n_grp - 1)
    cap = max(2, 2 * e // n_blk)
    slots = n_blk * cap
    tiles = 6 * e // LANES
    q_count = 6 * e // 8
    axes = ("grp", "blk")
    grp = lax.axis_index("grp").astype(jnp.int32)
    grp_at = grp.reshape(1)
    current = state.reshape(1536, e)
    mat = material.reshape(1536, e)
    col = brick_column.reshape(1, e)
    octant = brick_octant.reshape(1, e)
    layers, ends, halves = shape_of((2048, LANES)), shape_of((512, LANES)), shape_of((1024, LANES))
    halo = shape_of((256, LANES), BF16)
    rows, flat = shape_of((slots, 512), BF16), shape_of((1536, e))
    face, side, wide = (shape_of((n, e), BF16) for n in (192, 200, 384))
    tile = shape_of((slots * (n_grp - 1), LANES), BF16)

    def pairs(back, g):
        forth = [(g * n_blk + b, solvent * n_blk + b) for b in range(n_blk)]
        return [(j, i) for i, j in forth] if back else forth

    def planes(up, which):
        steps = [(b, b + 1) for b in range(n_blk - 1)]
        steps = steps if up else [(j, i) for i, j in steps]
        return [(g * n_blk + i, g * n_blk + j) for g in which for i, j in steps]

    def both_ways(up, down, which):
        return (
            lax.ppermute(up, axes, planes(True, which)),
            lax.ppermute(down, axes, planes(False, which)),
        )

    def swap(block):
        return lax.all_to_all(block, "blk", split_axis=0, concat_axis=0, tiled=True)

    send, sel, occ, near, far, phi, up, down = call(
        prepare(n_blk, cap, tiles, solvent),
        (grp_at, current, occupied.reshape(1, e), col, octant),
        (
            shape_of((slots, 512 + LANES), BF16),
            shape_of((slots, e), BF16),
            shape_of((8, e)),
            shape_of((256, 4 * q_count), BF16),
            shape_of((256, 4 * q_count), BF16),
            layers,
            side,
            side,
        ),
        [
            pltpu.VMEM((512, e), BF16),
            pltpu.VMEM((3, 1, e), jnp.int32),
            pltpu.VMEM(layers.shape, F32),
            pltpu.SemaphoreType.DMA((3,)),
            pltpu.SemaphoreType.DMA((1,)),
        ],
        smem=1,
        away=(2, 3, 4),
        unused=(5,),
    )
    recv = swap(send)

    def field_to(half, route):
        return lax.ppermute(half, axes, route)

    def across(i, j):
        return [(i * n_blk + b, j * n_blk + b) for b in range(n_blk)]

    near0 = field_to(near, pairs(True, 0))
    far1 = field_to(far, pairs(True, 1))
    fields = [(near0, field_to(far1, across(1, 0)))]
    fields.append((field_to(near0, across(0, 1)), far1))
    for g in groups[2:]:
        fields.append(tuple(field_to(half, pairs(True, g)) for half in (near, far)))
    side_low, side_high = both_ways(up, down, groups)
    work = [pltpu.VMEM((512, e), F32), pltpu.VMEM((1536, e), F32), pltpu.VMEM((1536, e), F32)]
    sweeping = [pltpu.VMEM(layers.shape, F32)] + [pltpu.VMEM((16, 8, LANES), F32)] * 2

    def gathered(g):
        def run():
            return call(gather_field(q_count), (recv, *fields[g]), (rows,))[0]

        return run

    def nothing(*outs):
        return lambda: call(idle, (), outs, unused=range(len(outs)))

    mine = lax.switch(grp, [gathered(g) for g in groups] + [lambda: nothing(rows)()[0]])
    mine, recv = lax.optimization_barrier((mine, recv))
    mine = swap(mine)
    arrived = []
    for g in groups:
        arrived.append(lax.ppermute(recv, axes, pairs(False, g)))

    def solvent_rates():
        return tuple(call(rates(tiles), (mat,), (layers, ends)))

    def mech_elastic():
        return tuple(call(elastic_and_rate, (current, mat, occ), (layers, ends), work[1:]))

    def mech_first():
        return tuple(
            call(
                first_step,
                (current, kap_edge, occ, base, sel, mine, side_low, side_high),
                (layers, rows, face, face),
                work + [pltpu.VMEM((512, e), BF16)],
            )
        )

    is_solvent = grp == solvent
    base, kap_edge = lax.cond(is_solvent, solvent_rates, mech_elastic)
    kap = base
    idle_first = lambda: tuple(nothing(layers, rows, face, face)())
    moved, send, fore, aft = lax.cond(is_solvent, idle_first, mech_first)

    def solvent_first():
        added, top, bottom, hot, spare = call(
            deposit(False), (phi, kap_edge, *arrived), (layers, wide, wide, tile, flat), unused=(4,)
        )
        low, high = both_ways(top, bottom, [solvent])
        inner, mid = call(inner_first(q_count), (added, kap), (layers, halves), sweeping)
        edge, s0, s1, s2 = call(
            outer_first(q_count),
            (low, high, kap_edge, low, high, mid, inner, hot),
            (ends, rows, rows, rows),
            [pltpu.VMEM((512, 4 * LANES), BF16)],
        )
        return inner, edge, hot, spare, low, high, s0, s1, s2

    def mech_turn(g):
        def run():
            mine = swap(send)
            force, *spare = call(
                elastic_forces,
                (moved, mat, occ),
                (flat, layers, ends, tile, wide, wide, rows, rows),
                work[1:],
                unused=range(1, 8),
            )
            blocks = list(spare[5:])
            blocks.insert(g, mine)
            return *spare[:3], force, *spare[3:5], *blocks

        return run

    turns = [mech_turn(g) for g in groups] + [solvent_first]
    inner, edge, hot, force, far_low, far_high, *blocks = lax.switch(grp, turns)
    back = [
        lax.ppermute(block, axes, pairs(False, g) + pairs(True, g))
        for g, block in zip(groups, blocks)
    ]

    def solvent_last():
        added, top, bottom = call(deposit(True), (inner, edge, *back, hot), (layers, halo, halo))
        low, high = both_ways(top, bottom, [solvent])
        out, mid = call(inner_last(q_count, tiles), (added, kap), (flat, halves), sweeping)
        (out,) = call(
            outer_last(q_count, tiles),
            (low, high, kap_edge, far_low, far_high, mid, out),
            (flat,),
            [pltpu.VMEM((4 * 16 * tiles, LANES), F32), pltpu.SemaphoreType.DMA((2,))],
            away=(6,),
            unused=(0,),
            alias={6: 0},
        )
        return out

    def swapped(g):
        return lambda: (swap(back[g]), *both_ways(fore, aft, [g]))

    def mech_last():
        mine, low, high = lax.switch(grp, [swapped(g) for g in groups])
        (out,) = call(
            last_step,
            (moved, kap_edge, occ, force, sel, mine, low, high, side_low, side_high),
            (flat,),
            work,
        )
        return out

    return lax.cond(is_solvent, solvent_last, mech_last).reshape(state.shape)


def solution(mesh):
    in_specs = (
        P("grp", None, None, "blk"),
        P("grp", None, None, "blk"),
        P(("grp", "blk")),
        P(("grp", "blk"), None),
        P(("grp", "blk")),
    )
    out_specs = P("grp", None, None, "blk")
    return jax.shard_map(shards, mesh=mesh, in_specs=in_specs, out_specs=out_specs, check_vma=False)
```

```python
import jax
import jax.numpy as jnp
from jax import lax
from jax.experimental import pallas as pl
from jax.experimental.pallas import tpu as pltpu
from jax.sharding import PartitionSpec as P


UNIT_LENGTH = 0.02
TIME_STEP = 0.1
PENALTY = 1.0
PRESSURE_SCALE = 0.05
DILATION_SCALE = 50.0
SWEEP_STEP = 0.03
SOURCE_RATE = 2.0
CUBIC_TERM = 0.3

LANES = 128
VMEM_LIMIT = 24 << 20
F32, BF16 = jnp.float32, jnp.bfloat16
VMEM = pl.BlockSpec(memory_space=pltpu.VMEM)
SMEM = pl.BlockSpec(memory_space=pltpu.SMEM)
ANY = pl.BlockSpec(memory_space=pltpu.HBM)


def shape_of(shape, dtype=F32):
    return jax.ShapeDtypeStruct(shape, dtype)


def call(body, args, outs, scratch=(), smem=0, away=(), unused=(), alias=None):
    specs = [SMEM] * smem + [VMEM] * (len(args) - smem)
    return pl.pallas_call(
        body,
        out_shape=outs,
        in_specs=[ANY if n in away else spec for n, spec in enumerate(specs)],
        out_specs=tuple(ANY if n in unused else VMEM for n in range(len(outs))),
        scratch_shapes=list(scratch),
        input_output_aliases=alias or {},
        compiler_params=pltpu.CompilerParams(vmem_limit_bytes=VMEM_LIMIT),
    )(*args)


def iota(shape, dim):
    return lax.broadcasted_iota(jnp.int32, shape, dim)


def dot(a, b, dims):
    return lax.dot_general(a, b, (dims, ((), ())), preferred_element_type=F32)


def diff_i(below, here, above):
    if below is None:
        return above - here
    if above is None:
        return here - below
    return 0.5 * (above - below)


def diff_j(x):
    return jnp.concatenate([x[1:2] - x[0:1], 0.5 * (x[2:] - x[:-2]), x[7:8] - x[6:7]], axis=0)


def diff_k(x):
    k = iota(x.shape, 1)
    upper = jnp.where(k == 7, x, pltpu.roll(x, 7, 1))
    lower = jnp.where(k == 0, x, pltpu.roll(x, 1, 1))
    return jnp.where((k == 0) | (k == 7), 1.0, 0.5) * (upper - lower)


def slab(ref, c, i):
    rows = ref[pl.ds(c * 512 + 64 * i, 64), :]
    return rows.reshape(8, 8, rows.shape[-1])


def put_slab(ref, c, i, value):
    ref[pl.ds(c * 512 + 64 * i, 64), :] = value.reshape(64, value.shape[-1])


def gradients(ref, i):
    grads = []
    for c in range(3):
        here = UNIT_LENGTH * slab(ref, c, i)
        below = UNIT_LENGTH * slab(ref, c, i - 1) if i > 0 else None
        above = UNIT_LENGTH * slab(ref, c, i + 1) if i < 7 else None
        row = [diff_i(below, here, above), diff_j(here), diff_k(here)]
        row[c] = row[c] + 1.0
        grads.append(row)
    return grads


def determinant(grads):
    return (
        grads[0][0] * (grads[1][1] * grads[2][2] - grads[1][2] * grads[2][1])
        - grads[0][1] * (grads[1][0] * grads[2][2] - grads[1][2] * grads[2][0])
        + grads[0][2] * (grads[1][0] * grads[2][1] - grads[1][1] * grads[2][0])
    )


def cofactors(g):
    return [
        [
            g[1][1] * g[2][2] - g[1][2] * g[2][1],
            g[1][2] * g[2][0] - g[1][0] * g[2][2],
            g[1][0] * g[2][1] - g[1][1] * g[2][0],
        ],
        [
            g[0][2] * g[2][1] - g[0][1] * g[2][2],
            g[0][0] * g[2][2] - g[0][2] * g[2][0],
            g[0][1] * g[2][0] - g[0][0] * g[2][1],
        ],
        [
            g[0][1] * g[1][2] - g[0][2] * g[1][1],
            g[0][2] * g[1][0] - g[0][0] * g[1][2],
            g[0][0] * g[1][1] - g[0][1] * g[1][0],
        ],
    ]


def dilate(ref, filled, out):
    for i in range(8):
        change = (determinant(gradients(ref, i)) - 1.0) * filled * DILATION_SCALE
        out[pl.ds(64 * i, 64), :] = change.reshape(64, change.shape[-1]).astype(BF16)


def put_faces(ref, up, down):
    for c in range(3):
        up[pl.ds(64 * c, 64), :] = ref[pl.ds(c * 512 + 448, 64), :].astype(BF16)
        down[pl.ds(64 * c, 64), :] = ref[pl.ds(c * 512, 64), :].astype(BF16)


def elastic(ref, mat, filled, out, stress, partial):
    e = filled.shape[-1]
    for i in range(8):
        g = gradients(ref, i)
        shear, lame = slab(mat, 0, i), slab(mat, 1, i)
        c = {}
        for a in range(3):
            for b in range(a, 3):
                c[a, b] = g[0][a] * g[0][b] + g[1][a] * g[1][b] + g[2][a] * g[2][b]
        diag = [c[a, a] - 1.0 for a in range(3)]
        volume = lame * (0.5 * (diag[0] + diag[1] + diag[2]))
        s = {}
        for a in range(3):
            s[a, a] = shear * diag[a] + volume
            for b in range(a + 1, 3):
                s[a, b] = s[b, a] = shear * c[a, b]
        for a in range(3):
            first = [g[a][0] * s[0, b] + g[a][1] * s[1, b] + g[a][2] * s[2, b] for b in range(3)]
            put_slab(stress, a, i, first[0])
            put_slab(partial, a, i, diff_j(first[1]) + diff_k(first[2]))
    k = iota((8, 8, e), 1)
    lane = iota((1, 1, e), 2)
    penalty = PENALTY * UNIT_LENGTH
    fill_before = jnp.where(lane == 0, 0.0, pltpu.roll(filled, 1, 2)) * penalty
    fill_after = jnp.where(lane == e - 1, 0.0, pltpu.roll(filled, e - 1, 2)) * penalty
    before_scale = jnp.where(k == 0, fill_before, 0.0)
    after_scale = jnp.where(k == 7, fill_after, 0.0)
    for i in range(8):
        for a in range(3):
            here = slab(ref, a, i)
            force = slab(partial, a, i) + diff_i(
                slab(stress, a, i - 1) if i > 0 else None,
                slab(stress, a, i),
                slab(stress, a, i + 1) if i < 7 else None,
            )
            before = pltpu.roll(pltpu.roll(here, 1, 1), 1, 2)
            after = pltpu.roll(pltpu.roll(here, 7, 1), e - 1, 2)
            force = force + before_scale * (before - here) + after_scale * (after - here)
            put_slab(out, a, i, force)


def advance(ref, mat, filled, base, recv, sel, low, high, fills, out, pressure, stress, partial):
    e = filled.shape[-1]
    pressure[...] = dot(recv[...], sel[...], ((0,), (0,))) * PRESSURE_SCALE
    for i in range(8):
        cof = cofactors(gradients(ref, i))
        p = pressure[pl.ds(64 * i, 64), :].reshape(8, 8, e)
        for a in range(3):
            first = [p * cof[a][b] for b in range(3)]
            put_slab(stress, a, i, first[0])
            put_slab(partial, a, i, slab(base, a, i) - (diff_j(first[1]) + diff_k(first[2])))
    penalty = PENALTY * UNIT_LENGTH
    fill_low, fill_high = fills[0].reshape(1, 1, e), fills[1].reshape(1, 1, e)
    for i in range(8):
        rate = (TIME_STEP / UNIT_LENGTH) * slab(mat, 2, i) * filled
        for a in range(3):
            here = slab(ref, a, i)
            force = slab(partial, a, i) - diff_i(
                slab(stress, a, i - 1) if i > 0 else None,
                slab(stress, a, i),
                slab(stress, a, i + 1) if i < 7 else None,
            )
            if i == 0:
                other = low[pl.ds(64 * a, 64), :].astype(F32).reshape(8, 8, e)
                force = force + penalty * fill_low * (other - here)
            if i == 7:
                other = high[pl.ds(64 * a, 64), :].astype(F32).reshape(8, 8, e)
                force = force + penalty * fill_high * (other - here)
            put_slab(out, a, i, here + rate * force)


def permute_in(x, tables):
    x = jnp.take_along_axis(x, tables[0], axis=1, mode="promise_in_bounds")
    x = jnp.take_along_axis(x, tables[1], axis=0, mode="promise_in_bounds")
    return jnp.take_along_axis(x, tables[2], axis=1, mode="promise_in_bounds")


def tables_in():
    row, lane = iota((8, LANES), 0), iota((8, LANES), 1)
    high, low = lane // 16, lane % 16
    return (8 * low + (high - row + 8) % 8, (high - row + 8) % 8, 16 * ((high + row) % 8) + low)


def tables_out():
    row, lane = iota((8, LANES), 0), iota((8, LANES), 1)
    high, low = lane // 16, lane % 16
    return (
        16 * ((high - row + 8) % 8) + low,
        (high - row + 8) % 8,
        16 * ((lane % 8 + row) % 8) + lane // 8,
    )


def layer_to_octants(chunk, scale, tables, tiles):
    rows = chunk.shape[0]
    lane = iota((8, LANES), 1)
    parts = []
    for y in range(16):
        part = chunk[tiles * y : min(tiles * y + 8, rows)]
        if part.shape[0] < 8:
            pad = jnp.zeros((8 - part.shape[0], LANES), F32)
            part = jnp.concatenate([part, pad], axis=0)
        part = permute_in(part, tables)
        parts.append(jnp.where(lane < 16 * tiles, part, 0.0))
    layer = jnp.concatenate(parts, axis=0)
    return layer * scale if scale != 1.0 else layer


def to_octants(ref, out, scale, tables, tiles):
    rows = 16 * tiles

    def layer(x, carry):
        chunk = ref[pl.ds(pl.multiple_of(x * rows, 8), rows), :]
        out[layer_rows(x), :] = layer_to_octants(chunk, scale, tables, tiles)
        return carry

    lax.fori_loop(0, 16, layer, 0, unroll=2)


def layer_from_octants(layer, tables, tiles):
    return jnp.concatenate(
        [permute_in(layer[8 * y : 8 * y + 8], tables)[:tiles] for y in range(16)], axis=0
    )


def layer_rows(x):
    return pl.ds(pl.multiple_of(x * LANES, LANES), LANES)


def pressures(layer):
    return (layer + CUBIC_TERM * layer * layer * layer).astype(BF16)


def one_hot(tile, width):
    return jnp.concatenate(
        [jnp.where(tile == float(o + 1), 1.0, 0.0).astype(BF16)[:, :width] for o in range(4)],
        axis=1,
    )


def weight(c):
    return 0.5 + c * c


def flux(c, s, other, other_s):
    return (s + other_s) * (other - c)


def inside(c, s, masks):
    inner, last, outer = masks
    fy = flux(c[:-1], s[:-1], c[1:], s[1:])
    r = pltpu.roll(c, 7, 1)
    up = jnp.where(inner, r, jnp.where(last, c, pltpu.roll(r, LANES - 1, 2)))
    fz = flux(c, s, up, weight(up))
    r = pltpu.roll(fz, 1, 1)
    total = fz - jnp.where(outer, r, pltpu.roll(r, 1, 2))
    return jnp.concatenate([total[:1] + fy[:1], total[1:-1] + (fy[1:] - fy[:-1]), total[-1:] - fy[-1:]], axis=0)


def sweep_masks(q_count):
    k, lane = iota((16, 8, LANES), 1), iota((16, 8, LANES), 2)
    return k < 7, lane >= q_count - 1, k > 0


def load(ref, x):
    return ref[layer_rows(x), :].astype(F32).reshape(16, 8, LANES)


def sweep_range(ref, kap, start, stop, put, weights, fluxes, masks):
    c, s = load(ref, start), None
    before = load(ref, start - 1)
    s = weight(c)
    weights[...] = s
    fluxes[...] = flux(before, weight(before), c, s)

    def step(x, carry):
        c, up = load(ref, x), load(ref, x + 1)
        s, up_s = weights[...], weight(up)
        weights[...] = up_s
        fx = flux(c, s, up, up_s)
        total = (fx - fluxes[...]) + inside(c, s, masks)
        fluxes[...] = fx
        put(x, (c + load(kap, x) * total).reshape(LANES, LANES))
        return carry

    lax.fori_loop(start, stop, step, 0, unroll=2)


def inner_sweeps(phi, kap, middle, edges, put, weights, fluxes, q_count):
    masks = sweep_masks(q_count)

    def keep(x, layer):
        middle[layer_rows(x), :] = layer

    sweep_range(phi, kap, 1, 15, keep, weights, fluxes, masks)
    for n, x in enumerate((1, 2, 13, 14)):
        edges[layer_rows(n), :] = middle[layer_rows(x), :]
    for n, x in enumerate((0, 1, 14, 15)):
        edges[layer_rows(4 + n), :] = phi[layer_rows(x), :]
    sweep_range(middle, kap, 2, 14, put, weights, fluxes, masks)


def sweep_chain(layers, kaps, masks):
    weights = [weight(c) for c in layers]
    fx = [
        flux(layers[n], weights[n], layers[n + 1], weights[n + 1]) for n in range(len(layers) - 1)
    ]
    return [
        layers[n] + kaps[n - 1] * ((fx[n] - fx[n - 1]) + inside(layers[n], weights[n], masks))
        for n in range(1, len(layers) - 1)
    ]


def edge_sweeps(low, high, kap_edge, kap_low, kap_high, middle, q_count):
    masks = sweep_masks(q_count)
    k = [load(kap_edge, n) for n in range(4)]
    m = [load(middle, n) for n in range(8)]
    first = [load(low, 0), load(low, 1), m[4], m[5]]
    first = sweep_chain(first, [load(kap_low, 2), k[0]], masks)
    first = sweep_chain([*first, m[0], m[1]], k[:2], masks)
    last = [m[6], m[7], load(high, 0), load(high, 1)]
    last = sweep_chain(last, [k[3], load(kap_high, 2)], masks)
    last = sweep_chain([m[2], m[3], *last], k[2:], masks)
    return [layer.reshape(LANES, LANES) for layer in first + last]


def prepare(n_blk, cap, tiles, solvent):
    def body(grp, state, occ, col, octant, send, sel, filled, near, far, phi, up, down, *scratch):
        dil, ints, layers, int_sems, sem = scratch
        e = state.shape[-1]
        quarter = 16 * tiles

        @pl.when(grp[0] != solvent)
        def _():
            copies = [
                pltpu.make_async_copy(ref, ints.at[n], int_sems.at[n])
                for n, ref in enumerate((occ, col, octant))
            ]
            for copy in copies:
                copy.start()
            dilate(state, 1.0, dil)
            for copy in copies:
                copy.wait()
            full, column, o = ints[0].astype(F32), ints[1], ints[2]
            hits = jnp.where(column == iota((n_blk, e), 0), 1.0, 0.0)
            earlier = jnp.where(iota((e, e), 0) < iota((e, e), 1), 1.0, 0.0).astype(BF16)
            rank = dot(hits.astype(BF16), earlier, ((1,), (0,)))
            rank = jnp.sum(rank * hits, axis=0, keepdims=True).astype(jnp.int32)
            slot = column * cap + rank
            chosen = jnp.where(iota((n_blk * cap, e), 0) == slot, 1.0, 0.0)
            held = (chosen * full).astype(BF16)
            chosen = chosen.astype(BF16)
            sel[...] = chosen
            send[:, pl.ds(0, 512)] = dot(held, dil[...], ((1,), (1,))).astype(BF16)
            block = sum((jnp.where(o >= n * quarter, 1, 0) for n in range(1, 4)))
            spot = o - quarter * block
            tile = jnp.where(iota((LANES, e), 0) == spot, (block + 1).astype(F32), 0.0)
            tile = dot(chosen, tile.astype(BF16), ((1,), (1,)))
            send[:, pl.ds(512, LANES)] = tile.astype(BF16)
            put_faces(state, up, down)
            filled[...] = jnp.broadcast_to(full, (8, e))
            up[pl.ds(192, 8), :] = jnp.broadcast_to(full, (8, e)).astype(BF16)
            down[pl.ds(192, 8), :] = jnp.broadcast_to(full, (8, e)).astype(BF16)

        @pl.when(grp[0] == solvent)
        def _():
            tables = tables_in()
            to_octants(state, layers, 1.0, tables, tiles)
            copy = pltpu.make_async_copy(layers, phi, sem.at[0])
            copy.start()
            for i in range(8):
                parts = []
                for ox in range(2):
                    for oy in range(2):
                        p = pressures(layers[pl.ds(LANES * (8 * ox + i) + 64 * oy, 64), :])
                        parts.append(p[:, :quarter])
                half = near if i < 4 else far
                half[pl.ds(64 * (i % 4), 64), :] = jnp.concatenate(parts, axis=1)
            copy.wait()

    return body


def rates(tiles):
    def body(mat, kap, edge):
        to_octants(mat, kap, 0.5 * SWEEP_STEP, tables_in(), tiles)
        for n, x in enumerate((0, 1, 14, 15)):
            edge[layer_rows(n), :] = kap[layer_rows(x), :]

    return body


def gather_field(quarter):
    def body(recv, near, far, out):
        hot = one_hot(recv[:, pl.ds(512, LANES)].astype(F32), quarter)
        for n, half in enumerate((near, far)):
            out[:, pl.ds(256 * n, 256)] = dot(hot, half[...], ((1,), (1,))).astype(BF16)

    return body


def elastic_forces(state, mat, occ, out, *scratch):
    elastic(state, mat, occ[pl.ds(0, 1), :].reshape(1, 1, occ.shape[-1]), out, *scratch[-2:])


def idle(*refs):
    pass


def first_step(state, mat, occ, base, sel, recv, low, high, out, send, up, down, *scratch):
    filled = occ[pl.ds(0, 1), :].reshape(1, 1, occ.shape[-1])
    fills = [ref[pl.ds(192, 8), :].astype(F32)[:1] for ref in (low, high)]
    advance(state, mat, filled, base, recv, sel, low, high, fills, out, *scratch[:3])
    dil = scratch[3]
    dilate(out, filled, dil)
    send[...] = dot(sel[...], dil[...], ((1,), (1,))).astype(BF16)
    put_faces(out, up, down)


def last_step(state, mat, occ, base, sel, recv, low, high, fill_low, fill_high, out, *scratch):
    filled = occ[pl.ds(0, 1), :].reshape(1, 1, occ.shape[-1])
    fills = [ref[pl.ds(192, 8), :].astype(F32)[:1] for ref in (fill_low, fill_high)]
    advance(state, mat, filled, base, recv, sel, low, high, fills, out, *scratch)


def deposit(edged):
    def body(phi, *refs):
        if edged:
            edge, v0, v1, v2, tile, out, up, down = refs
        else:
            border, v0, v1, v2, out, up, down, tile, _ = refs
            down[layer_rows(2), :] = border[layer_rows(0), :].astype(BF16)
            up[layer_rows(2), :] = border[layer_rows(3), :].astype(BF16)
        total = None
        for n, v in enumerate((v0, v1, v2)):
            spot = pl.ds(n * v.shape[0], v.shape[0])
            if not edged:
                tile[spot, :] = v[:, pl.ds(512, LANES)]
            hot = one_hot(tile[spot, :].astype(F32), LANES)
            part = dot(v[:, pl.ds(0, 512)], hot, ((0,), (0,)))
            total = part if total is None else total + part
        for x in range(16):
            i, ox = x % 8, x // 8
            if edged and x in (0, 1, 14, 15):
                layer = edge[layer_rows((0, 1, 14, 15).index(x)), :]
            else:
                layer = phi[layer_rows(x), :]
            added = jnp.concatenate(
                [
                    total[64 * i : 64 * i + 64, 256 * ox + LANES * o : 256 * ox + LANES * (o + 1)]
                    for o in range(2)
                ],
                axis=0,
            )
            layer = layer + (SWEEP_STEP * SOURCE_RATE) * added
            out[layer_rows(x), :] = layer
            if x < 2:
                down[layer_rows(x), :] = layer.astype(BF16)
            if x >= 14:
                up[layer_rows(x - 14), :] = layer.astype(BF16)

    return body


def inner_first(q_count):
    def body(phi, kap, out, edges, *scratch):
        def put(x, layer):
            out[layer_rows(x), :] = layer

        inner_sweeps(phi, kap, scratch[0], edges, put, *scratch[1:], q_count)

    return body


def outer_first(q_count):
    def body(low, high, kap_edge, kap_low, kap_high, mid, phi, tile, edge, s0, s1, s2, field):
        final = edge_sweeps(low, high, kap_edge, kap_low, kap_high, mid, q_count)
        for n in range(4):
            edge[layer_rows(n), :] = final[n]
        for x in range(16):
            i, ox = x % 8, x // 8
            layer = final[(0, 1, 14, 15).index(x)] if x in (0, 1, 14, 15) else phi[layer_rows(x), :]
            p = pressures(layer)
            for o in range(2):
                field[pl.ds(64 * i, 64), pl.ds(256 * ox + LANES * o, LANES)] = p[64 * o : 64 * o + 64]
        for n, s in enumerate((s0, s1, s2)):
            spot = pl.ds(n * s.shape[0], s.shape[0])
            hot = one_hot(tile[spot, :].astype(F32), LANES)
            s[...] = dot(hot, field[...], ((1,), (1,))).astype(BF16)

    return body


def inner_last(q_count, tiles):
    def body(phi, kap, out, edges, *scratch):
        tables = tables_out()
        rows = 16 * tiles

        def put(x, layer):
            spot = pl.ds(pl.multiple_of(x * rows, 8), rows)
            out[spot, :] = layer_from_octants(layer, tables, tiles)

        inner_sweeps(phi, kap, scratch[0], edges, put, *scratch[1:], q_count)

    return body


def outer_last(q_count, tiles):
    def body(low, high, kap_edge, kap_low, kap_high, mid, _, out, ends, sem):
        final = edge_sweeps(low, high, kap_edge, kap_low, kap_high, mid, q_count)
        tables = tables_out()
        rows = 16 * tiles
        for n in range(4):
            ends[pl.ds(rows * n, rows), :] = layer_from_octants(final[n], tables, tiles)
        copies = [
            pltpu.make_async_copy(
                ends.at[pl.ds(2 * rows * n, 2 * rows)], out.at[pl.ds(start, 2 * rows)], sem.at[n]
            )
            for n, start in enumerate((0, 14 * rows))
        ]
        for copy in copies:
            copy.start()
        for copy in copies:
            copy.wait()

    return body


def shards(state, material, occupied, brick_column, brick_octant):
    e = state.shape[-1]
    n_blk, n_grp = lax.axis_size("blk"), lax.axis_size("grp")
    solvent, groups = n_grp - 1, range(n_grp - 1)
    cap = max(2, 2 * e // n_blk)
    slots = n_blk * cap
    tiles = 6 * e // LANES
    q_count = 6 * e // 8
    axes = ("grp", "blk")
    grp = lax.axis_index("grp").astype(jnp.int32)
    grp_at = grp.reshape(1)
    current = state.reshape(1536, e)
    mat = material.reshape(1536, e)
    col = brick_column.reshape(1, e)
    octant = brick_octant.reshape(1, e)
    layers, ends, halves = shape_of((2048, LANES)), shape_of((512, LANES)), shape_of((1024, LANES))
    halo = shape_of((256, LANES), BF16)
    rows, flat = shape_of((slots, 512), BF16), shape_of((1536, e))
    face, side, wide = (shape_of((n, e), BF16) for n in (192, 200, 384))
    tile = shape_of((slots * (n_grp - 1), LANES), BF16)

    def pairs(back, g):
        forth = [(g * n_blk + b, solvent * n_blk + b) for b in range(n_blk)]
        return [(j, i) for i, j in forth] if back else forth

    def planes(up, which):
        steps = [(b, b + 1) for b in range(n_blk - 1)]
        steps = steps if up else [(j, i) for i, j in steps]
        return [(g * n_blk + i, g * n_blk + j) for g in which for i, j in steps]

    def both_ways(up, down, which):
        return (
            lax.ppermute(up, axes, planes(True, which)),
            lax.ppermute(down, axes, planes(False, which)),
        )

    def swap(block):
        return lax.all_to_all(block, "blk", split_axis=0, concat_axis=0, tiled=True)

    send, sel, occ, near, far, phi, up, down = call(
        prepare(n_blk, cap, tiles, solvent),
        (grp_at, current, occupied.reshape(1, e), col, octant),
        (
            shape_of((slots, 512 + LANES), BF16),
            shape_of((slots, e), BF16),
            shape_of((8, e)),
            shape_of((256, 4 * q_count), BF16),
            shape_of((256, 4 * q_count), BF16),
            layers,
            side,
            side,
        ),
        [
            pltpu.VMEM((512, e), BF16),
            pltpu.VMEM((3, 1, e), jnp.int32),
            pltpu.VMEM(layers.shape, F32),
            pltpu.SemaphoreType.DMA((3,)),
            pltpu.SemaphoreType.DMA((1,)),
        ],
        smem=1,
        away=(2, 3, 4),
        unused=(5,),
    )
    recv = swap(send)

    def field_to(half, route):
        return lax.ppermute(half, axes, route)

    def across(i, j):
        return [(i * n_blk + b, j * n_blk + b) for b in range(n_blk)]

    near0 = field_to(near, pairs(True, 0))
    far1 = field_to(far, pairs(True, 1))
    fields = [(near0, field_to(far1, across(1, 0)))]
    fields.append((field_to(near0, across(0, 1)), far1))
    for g in groups[2:]:
        fields.append(tuple(field_to(half, pairs(True, g)) for half in (near, far)))
    side_low, side_high = both_ways(up, down, groups)
    work = [pltpu.VMEM((512, e), F32), pltpu.VMEM((1536, e), F32), pltpu.VMEM((1536, e), F32)]
    sweeping = [pltpu.VMEM(layers.shape, F32)] + [pltpu.VMEM((16, 8, LANES), F32)] * 2

    def gathered(g):
        def run():
            return call(gather_field(q_count), (recv, *fields[g]), (rows,))[0]

        return run

    def nothing(*outs):
        return lambda: call(idle, (), outs, unused=range(len(outs)))

    mine = lax.switch(grp, [gathered(g) for g in groups] + [lambda: nothing(rows)()[0]])
    mine, recv = lax.optimization_barrier((mine, recv))
    mine = swap(mine)
    arrived = []
    for g in groups:
        arrived.append(lax.ppermute(recv, axes, pairs(False, g)))

    def solvent_rates():
        return tuple(call(rates(tiles), (mat,), (layers, ends)))

    def mech_elastic():
        return tuple(
            call(elastic_forces, (current, mat, occ), (layers, ends), work[1:], unused=(1,))
        )

    def mech_first():
        return tuple(
            call(
                first_step,
                (current, mat, occ, base, sel, mine, side_low, side_high),
                (layers, rows, face, face),
                work + [pltpu.VMEM((512, e), BF16)],
            )
        )

    is_solvent = grp == solvent
    base, kap_edge = lax.cond(is_solvent, solvent_rates, mech_elastic)
    kap = base
    idle_first = lambda: tuple(nothing(layers, rows, face, face)())
    moved, send, fore, aft = lax.cond(is_solvent, idle_first, mech_first)

    def solvent_first():
        added, top, bottom, hot, spare = call(
            deposit(False), (phi, kap_edge, *arrived), (layers, wide, wide, tile, flat), unused=(4,)
        )
        low, high = both_ways(top, bottom, [solvent])
        inner, mid = call(inner_first(q_count), (added, kap), (layers, halves), sweeping)
        edge, s0, s1, s2 = call(
            outer_first(q_count),
            (low, high, kap_edge, low, high, mid, inner, hot),
            (ends, rows, rows, rows),
            [pltpu.VMEM((512, 4 * LANES), BF16)],
        )
        return inner, edge, hot, spare, low, high, s0, s1, s2

    def mech_turn(g):
        def run():
            mine = swap(send)
            force, *spare = call(
                elastic_forces,
                (moved, mat, occ),
                (flat, layers, ends, tile, wide, wide, rows, rows),
                work[1:],
                unused=range(1, 8),
            )
            blocks = list(spare[5:])
            blocks.insert(g, mine)
            return *spare[:3], force, *spare[3:5], *blocks

        return run

    turns = [mech_turn(g) for g in groups] + [solvent_first]
    inner, edge, hot, force, far_low, far_high, *blocks = lax.switch(grp, turns)
    back = [
        lax.ppermute(block, axes, pairs(False, g) + pairs(True, g))
        for g, block in zip(groups, blocks)
    ]

    def solvent_last():
        added, top, bottom = call(deposit(True), (inner, edge, *back, hot), (layers, halo, halo))
        low, high = both_ways(top, bottom, [solvent])
        out, mid = call(inner_last(q_count, tiles), (added, kap), (flat, halves), sweeping)
        (out,) = call(
            outer_last(q_count, tiles),
            (low, high, kap_edge, far_low, far_high, mid, out),
            (flat,),
            [pltpu.VMEM((4 * 16 * tiles, LANES), F32), pltpu.SemaphoreType.DMA((2,))],
            away=(6,),
            unused=(0,),
            alias={6: 0},
        )
        return out

    def swapped(g):
        return lambda: (swap(back[g]), *both_ways(fore, aft, [g]))

    def mech_last():
        mine, low, high = lax.switch(grp, [swapped(g) for g in groups])
        (out,) = call(
            last_step,
            (moved, mat, occ, force, sel, mine, low, high, side_low, side_high),
            (flat,),
            work,
        )
        return out

    return lax.cond(is_solvent, solvent_last, mech_last).reshape(state.shape)


def solution(mesh):
    in_specs = (
        P("grp", None, None, "blk"),
        P("grp", None, None, "blk"),
        P(("grp", "blk")),
        P(("grp", "blk"), None),
        P(("grp", "blk")),
    )
    out_specs = P("grp", None, None, "blk")
    return jax.shard_map(shards, mesh=mesh, in_specs=in_specs, out_specs=out_specs, check_vma=False)
```
